32 devices in a mesh: field: 2 (over y), sky: 4 (over z), epoch: 2 (over x), vel: 2 (over core).
Axes of the slice: x: 2, y: 2, z: 4, core: 2. Of those that a mesh axis runs over, the one named last changes fastest.
Arguments:
- images: bfloat16 [64, 8, 128, 128], P(('epoch', 'vel'), ('field', 'sky')), parts along dimension 1, may hold values from -6 to 6
- variances: bfloat16 [64, 8, 128, 128], P(('epoch', 'vel'), ('field', 'sky')), parts along dimension 1, may hold values from 0.5 to 2
- valid: int32 [64, 8], P(('epoch', 'vel'), ('field', 'sky')), parts along dimension 1, may hold values from 0 to 1, as said below
- psf_sigma: float32 [128], P(('field', 'epoch', 'vel')), parts along dimension 0, may hold values from 0.8 to 2.5
- offsets: int32 [2, 16, 64], P(None, None, 'epoch'), may hold values from -12 to 12, as said below
Outputs:
- likelihood: float32 [16, 8, 128, 128], P(('epoch', 'vel'), ('field', 'sky')), parts along dimension 1
- flux: float32 [16, 8, 128, 128], P(('epoch', 'vel'), ('field', 'sky')), parts along dimension 1
The draws below stay inside these ranges and needn't reach their ends.
There are 2 independent parts, one for each index of `field`. The reference program is written for one: setup_inputs(seed, part) draws one part's arguments, and reference() takes and returns one part's arrays. A program takes and returns all parts, laid end to end along the dimension named above; an argument that names none is the same for every part. Nothing has to cross between parts.
Inputs may be any that keep to these rules, and one draw needn't show every extreme that they name: Each hypothesis moves linearly: offsets[c, k, e] = floor(s[c, k] * e / 63) for integer speeds s within the range; both ends of the range are reached. `valid`: in one tile of the field, drawn from the seed, exactly one epoch is usable; in every other tile each frame is usable with probability 3/4, independently.
All inputs are finite; a program needn't handle non-finite values.
Results may differ from the reference program's by a relative error of at most 0.0058.
Values may be sent and summed in bfloat16 or wider, within the bound.
A program may use at most 64 MiB of HBM per device.

```python
import math
import jax
import jax.numpy as jnp
from jax import lax

TILE = 128
VELS = 16
REACH = 12
PSFR = 7
GRID_X = 4
EPOCHS = 64
N_SKY = 4


def draw_offsets(key, part):
    speeds = jax.random.randint(key, (2, VELS), -REACH, REACH + 1).astype(jnp.int32)
    speeds = speeds.at[1, 0].set(REACH).at[0, 1].set(-REACH)
    epoch_ids = jnp.arange(EPOCHS, dtype=jnp.int32)
    return (speeds[:, :, None] * epoch_ids[None, None, :] // (EPOCHS - 1)).astype(jnp.int32)


def draw_valid(key, part):
    levels = jax.random.randint(jax.random.fold_in(key, 11), (EPOCHS, N_SKY), 0, 4)
    usable = (levels < 3).astype(jnp.int32)
    sparse_tile = jax.random.randint(jax.random.fold_in(key, 12), (), 0, N_SKY)
    kept_epoch = jax.random.randint(jax.random.fold_in(key, 13), (), 0, EPOCHS)
    tile_ids = jnp.arange(N_SKY, dtype=jnp.int32)
    epoch_ids = jnp.arange(EPOCHS, dtype=jnp.int32)
    single = (epoch_ids[:, None] == kept_epoch).astype(jnp.int32) * jnp.ones((1, N_SKY), jnp.int32)
    return jnp.where(tile_ids[None, :] == sparse_tile, single, usable).astype(jnp.int32)


def shard_levels(own_key, shape, split, least, top_value):
    def one(axis_at, blocks):
        draws = jax.random.uniform(jax.random.fold_in(jax.random.fold_in(own_key, 6), axis_at), (blocks,), jnp.float32, least / len(split), top_value / len(split))
        return jnp.repeat(jnp.exp(draws), shape[axis_at] // blocks).reshape((-1,) + (1,) * (len(shape) - axis_at - 1))

    loudness = one(*split[0])
    for cut in split[1:]:
        loudness = loudness * one(*cut)
    return loudness


def scatter_about(stream_key, dims, scale, reach, shards=(), held_as=jnp.bfloat16):
    array = scale * jax.random.normal(stream_key, dims, jnp.float32)
    if shards:
        array = array * shard_levels(stream_key, dims, shards, -0.22, 0.18)
    return jnp.clip(array, -reach, reach).astype(held_as)


def setup_inputs(seed: int = 0, part: int = 0) -> dict:
    streams_of = jax.random.split(jax.random.key(seed), 6)
    own_keys = jax.random.split(jax.random.fold_in(streams_of[5], part), 6)
    images = scatter_about(own_keys[0], (EPOCHS, N_SKY, TILE, TILE), 1.0, 6.0, ((0, 4), (1, 4)))
    variances = jnp.clip(jnp.exp(math.log(2.0) - 1.3862944 * jax.random.uniform(own_keys[1], (EPOCHS, N_SKY, TILE, TILE), jnp.float32) ** shard_levels(own_keys[1], (EPOCHS, N_SKY, TILE, TILE), ((0, 4), (1, 4)), -0.2, 0.2)), 0.5, 2.0).astype(jnp.bfloat16)
    valid = draw_valid(jax.random.fold_in(jax.random.fold_in(streams_of[5], part), 71), part)
    psf_sigma = jnp.clip(jnp.exp(math.log(2.5) - 1.13943427 * jax.random.uniform(own_keys[3], (EPOCHS,), jnp.float32) ** shard_levels(own_keys[3], (EPOCHS,), ((0, 4),), -0.2, 0.2)), 0.8, 2.5)
    offsets = draw_offsets(jax.random.fold_in(streams_of[5], 71), part)
    return dict(images=images, variances=variances, valid=valid, psf_sigma=psf_sigma, offsets=offsets)


phi_floor = 0.25

def round_keep(values):
    rounded = values.astype(jnp.bfloat16)
    rounded = lax.optimization_barrier(rounded)
    return rounded.astype(jnp.float32)

def kernel_taps(psf_sigma):
    spread = jnp.arange(-PSFR, PSFR + 1).astype(jnp.float32)
    profile = jnp.exp(-0.5 * (spread[None, :] / psf_sigma[:, None]) ** 2)
    profile = profile / lax.optimization_barrier(jnp.sum(profile, axis=1, keepdims=True))
    return (round_keep(profile), round_keep(profile * profile))

def whole_field(tiles):
    epoch_count = tiles.shape[0]
    grid_rows = N_SKY // GRID_X
    placed = jnp.roll(tiles, GRID_X // 2, axis=1)
    shaped = placed.reshape(epoch_count, grid_rows, GRID_X, TILE, TILE)
    return shaped.transpose(0, 1, 3, 2, 4).reshape(epoch_count, grid_rows * TILE, GRID_X * TILE)

def back_to_tiles(field):
    leading = field.shape[0]
    grid_rows = N_SKY // GRID_X
    shaped = field.reshape(leading, grid_rows, TILE, GRID_X, TILE)
    placed = shaped.transpose(0, 1, 3, 2, 4).reshape(leading, N_SKY, TILE, TILE)
    return jnp.roll(placed, -(GRID_X // 2), axis=1)

def correlate(field, kernel, axis):
    widths = [(0, 0), (0, 0), (0, 0)]
    widths[axis] = (PSFR, PSFR)
    padded = jnp.pad(field, widths)
    length = field.shape[axis]
    summed = jnp.zeros(field.shape, jnp.float32)
    for tap_index in range(2 * PSFR + 1):
        window = lax.slice_in_dim(padded, tap_index, tap_index + length, axis=axis)
        summed = summed + kernel[:, tap_index][:, None, None] * window
    return summed

def reference(images, variances, valid, psf_sigma, offsets):
    usable = valid.astype(jnp.float32)[:, :, None, None]
    scaled = images.astype(jnp.float32) / variances.astype(jnp.float32) * usable
    inverse = usable / variances.astype(jnp.float32)
    scaled = whole_field(round_keep(scaled))
    inverse = whole_field(round_keep(inverse))
    edges = ((0, 0), (REACH, REACH), (REACH, REACH))
    scaled = jnp.pad(scaled, edges)
    inverse = jnp.pad(inverse, edges)
    first_taps, second_taps = kernel_taps(psf_sigma)
    psi = correlate(round_keep(correlate(scaled, first_taps, 1)), first_taps, 2)
    phi = correlate(round_keep(correlate(inverse, second_taps, 1)), second_taps, 2)
    paired = jnp.stack([psi, phi], axis=1)
    height = paired.shape[2] - 2 * REACH
    breadth = paired.shape[3] - 2 * REACH

    def stack_one(motion):

        def accumulate(epoch_id, summed):
            epoch_map = lax.dynamic_index_in_dim(paired, epoch_id, 0, keepdims=False)
            start_y = (REACH + motion[0, epoch_id]).astype(jnp.int32)
            start_x = (REACH + motion[1, epoch_id]).astype(jnp.int32)
            window = lax.dynamic_slice(epoch_map, (jnp.zeros((), jnp.int32), start_y, start_x), (2, height, breadth))
            return summed + window
        return lax.fori_loop(0, EPOCHS, accumulate, jnp.zeros((2, height, breadth), jnp.float32))
    sums = lax.map(stack_one, jnp.transpose(offsets, (1, 0, 2)))
    psi_sum = sums[:, 0]
    phi_sum = jnp.maximum(sums[:, 1], phi_floor)
    likelihood = psi_sum / jnp.sqrt(phi_sum)
    flux = psi_sum / phi_sum
    return (back_to_tiles(likelihood), back_to_tiles(flux))
```

```python
import functools

import jax
import jax.numpy as jnp
from jax import lax
from jax.experimental import pallas as pl
from jax.experimental.pallas import tpu as pltpu
from jax.sharding import PartitionSpec as P

VELS = 16
REACH = 12
PSFR = 7
GRID_X = 4
MARGIN = REACH + PSFR
LANES = 128
HEAD = 16
PACK = 16
BACK = 32
EDGE = 32

phi_floor = 0.25


def shifted(block, axis, distance):
    devices = range(lax.axis_size(axis))
    route = [((i - distance) % len(devices), i) for i in devices]
    return lax.ppermute(block, axis, route)


def positions(index, tile):
    return jnp.where(
        index < tile,
        index,
        jnp.where(
            index < tile + MARGIN,
            index - tile - MARGIN,
            jnp.where(index < tile + 2 * MARGIN, index - MARGIN, 4 * tile),
        ),
    )


FAR = -1.0e9


def exponents(distance):
    away = distance.astype(jnp.float32)
    return jnp.where(jnp.abs(distance) <= PSFR, -0.5 * away * away, FAR)


def fused_kernel(plan, *refs):
    tile, sky, blocks, block, epochs, runs = plan
    (offsets, motion, sigmas, own, halo, psi_out, phi_out, plane_a, plane_b, ends, ends_made, ends_sem, row_q,
     own_q, side_q, bands, send_v, recv_v, send_x, recv_x, keep, sv, rv, sx, rx) = refs
    maps = 2
    rows_in = row_q.shape[1]
    rows_out = plane_a.shape[1]
    width = 2 * LANES
    mesh_id = pl.DeviceIdType.MESH
    group = lax.axis_index("epoch")
    member = lax.axis_index("vel")
    partner = 1 - member

    barrier = pltpu.get_barrier_semaphore()
    greeted = 1
    pl.semaphore_signal(barrier, inc=1, device_id={"vel": partner}, device_id_type=mesh_id)
    for a in range(1, blocks):
        peer = lax.rem(group + a, blocks)
        pl.semaphore_signal(barrier, inc=1, device_id={"epoch": peer}, device_id_type=mesh_id)
        greeted += 1
    pl.semaphore_wait(barrier, greeted)

    shape = (rows_out, rows_in)
    row_q[...] = exponents(
        positions(lax.broadcasted_iota(jnp.int32, shape, 1), tile)
        - lax.broadcasted_iota(jnp.int32, shape, 0) + REACH
    )
    shape = (LANES, width)
    held = lax.broadcasted_iota(jnp.int32, shape, 0)
    shifted_out = lax.broadcasted_iota(jnp.int32, shape, 1) - REACH
    own_q[...] = exponents(held - shifted_out)
    side_q[0] = exponents(positions(held + tile, tile) - shifted_out)

    first = member * epochs

    at_epoch = lax.broadcasted_iota(jnp.int32, motion.shape[1:], 1)
    moved = jnp.zeros(motion.shape[1:], jnp.int32)
    for way in range(2):
        start = jnp.where(at_epoch == first, motion[way], 0)
        moved += jnp.abs(motion[way] - jnp.sum(start, axis=1, keepdims=True))
    held_here = (at_epoch >= first) & (at_epoch < first + epochs)
    counted = jnp.zeros(ends_made.shape, jnp.int32)
    at_run = lax.broadcasted_iota(jnp.int32, ends_made.shape, 1)
    for run in range(runs - 1):
        count = jnp.sum((held_here & (moved <= run)).astype(jnp.int32), axis=1, keepdims=True)
        counted = jnp.where(at_run == run, count, counted)
    ends_made[...] = counted
    ends_copy = pltpu.make_async_copy(ends_made, ends, ends_sem)
    ends_copy.start()
    plane_a[:maps] = jnp.zeros_like(plane_a[:maps])
    plane_b[:maps] = jnp.zeros_like(plane_b[:maps])

    def correlate(e, turn):
        sigma = jnp.full((8, LANES), sigmas[e], jnp.float32)
        power = 1.0 / (sigma * sigma)
        tap = lax.broadcasted_iota(jnp.int32, (8, LANES), 1) - PSFR
        norm = jnp.sum(jnp.exp(exponents(tap) * power), axis=1, keepdims=True)
        scale = (1.0 / norm)[:1]
        power = power[:1, :1]

        def both(q):
            profile = jnp.exp(q * power) * scale
            return profile.astype(jnp.bfloat16), (profile * profile).astype(jnp.bfloat16)

        row_bands = both(row_q[...])
        for part, q in enumerate((own_q[...], side_q[0])):
            for m, made in enumerate(both(q)):
                bands[turn, m, part * LANES : (part + 1) * LANES] = made
        for m in range(maps):
            side = halo[e, m]
            held = jnp.concatenate([own[e, m], side], axis=1)
            rows = jnp.dot(row_bands[m], held, preferred_element_type=jnp.float32)
            done = jnp.dot(
                rows.astype(jnp.bfloat16), bands[turn, m], preferred_element_type=jnp.float32
            )
            at = maps * e + m
            plane_a[at + maps] = plane_a[at] + done[:, :LANES]
            plane_b[at + maps] = plane_b[at] + done[:, LANES:]

    step = 2 if epochs % 2 == 0 else 1

    def several(i, carry):
        for turn in range(step):
            correlate(step * i + turn, turn)
        return carry

    lax.fori_loop(0, epochs // step, several, 0)

    def vel_copy(at):
        return pltpu.make_async_remote_copy(
            src_ref=send_v.at[at], dst_ref=recv_v.at[at], send_sem=sv.at[at], recv_sem=rv.at[at],
            device_id={"vel": partner}, device_id_type=mesh_id,
        )

    def epoch_copy(at):
        peer = lax.rem(group + 1 + at // block, blocks)
        return pltpu.make_async_remote_copy(
            src_ref=send_x.at[at], dst_ref=recv_x.at[at], send_sem=sx.at[at], recv_sem=rx.at[at],
            device_id={"epoch": peer}, device_id_type=mesh_id,
        )

    def stack(slot, carry):
        a = blocks - 1 - slot // (2 * block)
        turn = lax.rem(slot, 2 * block)
        mine = ((turn > 0) & (lax.rem(turn, 2) == 0)) | (turn == 2 * block - 1)
        b = jnp.where(mine, 0, 1)
        j = jnp.where(turn == 2 * block - 1, block - 1, jnp.where(mine, turn // 2 - 1, (turn + 1) // 2))
        place = a * block + j
        k = (lax.rem(group + a, blocks) * 2 + lax.rem(member + b, 2)) * block + j
        lane = lax.broadcasted_iota(jnp.int32, (tile, LANES), 1)
        summed = [jnp.zeros((tile, LANES), jnp.float32) for _ in range(maps)]
        low = jnp.zeros((), jnp.int32)
        for run in range(runs):
            high = ends[k, run] if run < runs - 1 else epochs
            at = first + jnp.minimum(low, epochs - 1)
            down = offsets[0, k, at] + REACH
            right = offsets[1, k, at] + REACH
            rows = pl.ds(down, tile)
            for m in range(maps):
                left_part = plane_a[maps * high + m, rows, :] - plane_a[maps * low + m, rows, :]
                right_part = plane_b[maps * high + m, rows, :] - plane_b[maps * low + m, rows, :]
                merged = jnp.where(lane >= right, left_part, right_part)
                summed[m] += pltpu.roll(merged, LANES - right, axis=1)
            low = high
        for m in range(maps):
            keep[b, j, m] = summed[m]

        @pl.when(b == 1)
        def _():
            send_v[place] = keep[1, j].astype(jnp.bfloat16)
            vel_copy(place).start()

        @pl.when(b == 0)
        def _():
            vel_copy(place).wait_recv()
            keep[0, j] = keep[0, j] + recv_v[place].astype(jnp.float32)

            @pl.when(a > 0)
            def _():
                send_x[place - block] = keep[0, j].astype(jnp.bfloat16)
                epoch_copy(place - block).start()

        return carry

    ends_copy.wait()
    lax.fori_loop(0, 2 * blocks * block, stack, 0)

    def finish(j, carry):
        total = keep[0, j]
        for a in range(1, blocks):
            at = (a - 1) * block + j
            epoch_copy(at).wait_recv()
            total = total + recv_x[at].astype(jnp.float32)
        psi_out[j] = total[0]
        phi_out[j] = total[1]
        return carry

    lax.fori_loop(0, block, finish, 0)

    def drain_v(at, carry):
        vel_copy(at).wait_send()
        return carry

    lax.fori_loop(0, blocks * block, drain_v, 0)

    def drain_x(at, carry):
        epoch_copy(at).wait_send()
        return carry

    lax.fori_loop(0, (blocks - 1) * block, drain_x, 0)


def strips(own, tile_count, tile):
    position = (lax.axis_index("sky") + GRID_X // 2) % tile_count
    column = position % GRID_X
    left = shifted(own[..., tile - MARGIN :], "sky", 1)
    right = shifted(own[..., :MARGIN], "sky", -1)
    left = jnp.where(column > 0, left, jnp.zeros_like(left))
    right = jnp.where(column < GRID_X - 1, right, jnp.zeros_like(right))
    blank = jnp.zeros(own.shape[:3] + (LANES - 2 * MARGIN,), jnp.bfloat16)
    both = jnp.concatenate([own, left, right, blank], axis=3)
    upper = shifted(both[:, :, tile - MARGIN :], "sky", GRID_X)
    lower = shifted(both[:, :, :MARGIN], "sky", -GRID_X)
    upper = jnp.where(position >= GRID_X, upper, jnp.zeros_like(upper))
    lower = jnp.where(position < tile_count - GRID_X, lower, jnp.zeros_like(lower))
    blank = jnp.zeros(both.shape[:2] + (LANES - 2 * MARGIN, both.shape[3]), jnp.bfloat16)
    both = jnp.concatenate([both, upper, lower, blank], axis=2)
    return both[..., :tile], both[..., tile:]


def near_kernel(plan, *refs):
    tile, sky, blocks, block, epochs, runs, slots = plan
    (offsets, motion, sigmas, valid, images, variances, psi_out, phi_out, plane, edge, ends, ends_made, ends_sem,
     image, variance, load_sem, place, shift, row_q, own_q, near_q, far_q, own, sent, came, sz, rz,
     send_v, recv_v, send_x, recv_x, keep, sv, rv, sx, rx) = refs
    maps = 2
    groups = -(-epochs // slots)
    rows_out = row_q.shape[0]
    mesh_id = pl.DeviceIdType.MESH
    me = lax.axis_index("sky")
    group = lax.axis_index("epoch")
    member = lax.axis_index("vel")
    column = lax.rem(lax.rem(me + GRID_X // 2, sky), GRID_X)
    before = lax.rem(me + sky - 1, sky)
    after = lax.rem(me + 1, sky)
    partner = 1 - member

    barrier = pltpu.get_barrier_semaphore()
    greeted = 3
    pl.semaphore_signal(barrier, inc=1, device_id={"vel": partner}, device_id_type=mesh_id)
    for a in range(1, blocks):
        peer = lax.rem(group + a, blocks)
        pl.semaphore_signal(barrier, inc=1, device_id={"epoch": peer}, device_id_type=mesh_id)
        greeted += 1
    for other in (before, after):
        pl.semaphore_signal(barrier, inc=1, device_id={"sky": other}, device_id_type=mesh_id)

    def members(g):
        return range(g * slots, min((g + 1) * slots, epochs))

    def load(which, g):
        source, held = ((images, image), (variances, variance))[which]
        span = pl.ds(g * slots, len(members(g)))
        return pltpu.make_async_copy(source.at[span, 0], held.at[span], load_sem.at[which, g])

    for g in range(groups):
        for which in range(2):
            load(which, g).start()

    def iota(shape, axis):
        return lax.broadcasted_iota(jnp.int32, shape, axis)

    def one_hot(hit):
        return jnp.where(hit, 1.0, 0.0).astype(jnp.bfloat16)

    lane = iota((tile, LANES), 1)
    row = iota((tile, LANES), 0)

    def make_place(s, carry):
        low = lane - (slot_start(s) + MARGIN + BACK)
        place[s, :, :LANES] = one_hot((row < MARGIN) & (((low - row) & (LANES - 1)) == 0))
        high = lane - slot_start(s)
        place[s, :, LANES:] = one_hot((row >= tile - MARGIN) & (high == row - (tile - MARGIN)))
        return carry

    def slot_start(s):
        return MARGIN * s

    lax.fori_loop(0, slots, make_place, 0)

    def side_copy(to_after, g):
        return pltpu.make_async_remote_copy(
            src_ref=sent.at[to_after, g],
            dst_ref=came.at[to_after, g],
            send_sem=sz.at[to_after, g],
            recv_sem=rz.at[to_after, g],
            device_id={"sky": after if to_after else before},
            device_id_type=mesh_id,
        )

    for g in range(groups):
        for which in range(2):
            load(which, g).wait()
        for e in members(g):
            usable = valid[e].astype(jnp.float32)
            inverse = usable / variance[e].astype(jnp.float32)
            scaled = image[e].astype(jnp.float32) * inverse
            own[e, 0] = scaled.astype(jnp.bfloat16)
            own[e, 1] = inverse.astype(jnp.bfloat16)
        spread = jnp.concatenate([place[s] for s in range(len(members(g)))], axis=0)
        for m in range(maps):
            strip = jnp.concatenate([own[e, m] for e in members(g)], axis=1)
            placed = jnp.dot(strip, spread, preferred_element_type=jnp.float32)
            sent[0, g, m] = placed[:, :LANES].astype(jnp.bfloat16)
            sent[1, g, m] = placed[:, LANES:].astype(jnp.bfloat16)
        if g == 0:
            pl.semaphore_wait(barrier, greeted)

        @pl.when(column > 0)
        def _():
            side_copy(0, g).start()

        @pl.when(column < GRID_X - 1)
        def _():
            side_copy(1, g).start()

    @pl.when(column == 0)
    def _():
        came[1] = jnp.zeros_like(came[1])

    @pl.when(column == GRID_X - 1)
    def _():
        came[0] = jnp.zeros_like(came[0])

    def make_shift(at, carry):
        shift[at] = one_hot(row == lane + (at - REACH))
        return carry

    lax.fori_loop(0, 2 * REACH + 1, make_shift, 0)

    row_q[...] = exponents(iota(row_q.shape, 1) - iota(row_q.shape, 0) + HEAD)

    def edge_index(shape):
        return ((iota(shape, 1) + EDGE // 2) & (EDGE - 1)) - EDGE // 2

    def edge_column(shape):
        index = edge_index(shape)
        beyond = jnp.where(index < 0, index, index + tile)
        return jnp.where((index >= -REACH) & (index < REACH), beyond, 4 * tile)

    def side_pixel(kept):
        left = (kept >= BACK - MARGIN) & (kept < BACK)
        right = (kept >= 2 * BACK) & (kept < 2 * BACK + MARGIN)
        return jnp.where(left, kept - BACK, jnp.where(right, kept - 2 * BACK + tile, -4 * tile))

    at = iota(own_q.shape, 0)
    own_q[...] = exponents(jnp.where(at < PACK, at, at + tile - 2 * PACK) - edge_column(own_q.shape))
    at = iota(near_q.shape, 0)
    kept = jnp.where(at < PACK, at + BACK - PACK, at - PACK + 2 * BACK)
    near_q[...] = exponents(side_pixel(kept) - iota(near_q.shape, 1))
    at = iota(far_q.shape, 0)
    kept = jnp.where(at < BACK, at, at + BACK)
    far_q[...] = exponents(side_pixel(kept) - edge_column(far_q.shape))

    first = member * epochs
    at_epoch = iota(motion.shape[1:], 1)
    moved = jnp.zeros(motion.shape[1:], jnp.int32)
    for way in range(2):
        start = jnp.where(at_epoch == first, motion[way], 0)
        moved += jnp.abs(motion[way] - jnp.sum(start, axis=1, keepdims=True))
    held_here = (at_epoch >= first) & (at_epoch < first + epochs)
    counted = jnp.zeros(ends_made.shape, jnp.int32)
    at_run = iota(ends_made.shape, 1)
    for run in range(runs - 1):
        count = jnp.sum((held_here & (moved <= run)).astype(jnp.int32), axis=1, keepdims=True)
        counted = jnp.where(at_run == run, count, counted)
    ends_made[...] = counted
    ends_copy = pltpu.make_async_copy(ends_made, ends, ends_sem)
    ends_copy.start()
    plane[:maps] = jnp.zeros_like(plane[:maps])
    edge[:maps] = jnp.zeros_like(edge[:maps])

    parts = tile // EDGE
    edge_rows = edge.shape[1]
    edge_group = iota((edge_rows, LANES), 1) + EDGE // 2
    edge_group = (edge_group & (LANES - 1)) // EDGE

    def correlate(e, g, s):
        sigma = jnp.full((8, LANES), sigmas[e], jnp.float32)
        power = 1.0 / (sigma * sigma)
        tap = iota((8, LANES), 1) - PSFR
        norm = jnp.sum(jnp.exp(exponents(tap) * power), axis=1, keepdims=True)
        scale = (1.0 / norm)[:1]
        power = power[:1, :1]

        def both(q):
            profile = jnp.exp(q * power) * scale
            return profile.astype(jnp.bfloat16), (profile * profile).astype(jnp.bfloat16)

        row_bands, own_bands, near_bands, far_bands = (both(q[...]) for q in (row_q, own_q, near_q, far_q))

        def blank(rows):
            return jnp.zeros((rows, LANES), jnp.bfloat16)

        window = slot_start(s)
        in_slot = (lane >= window) & (lane < window + MARGIN)
        turn = (2 * LANES + BACK - MARGIN - window) & (LANES - 1)
        for m in range(maps):
            from_own = jnp.concatenate(
                [
                    row_bands[m][HEAD : HEAD + tile],
                    jnp.concatenate(
                        [own_bands[m][:PACK], blank(tile - 2 * PACK), own_bands[m][PACK:]], axis=0
                    ),
                ],
                axis=1,
            )
            near = [
                blank(BACK - PACK), near_bands[m][:PACK], blank(BACK),
                near_bands[m][PACK:], blank(2 * BACK - PACK),
            ]
            far = [far_bands[m][:BACK], blank(BACK), far_bands[m][BACK:], blank(BACK)]
            from_side = jnp.concatenate([jnp.concatenate(near, axis=0), jnp.concatenate(far, axis=0)], axis=1)
            side = jnp.where(in_slot, came[1, g, m].astype(jnp.float32), came[0, g, m].astype(jnp.float32))
            side = pltpu.roll(side, turn, axis=1).astype(jnp.bfloat16)
            held = jnp.concatenate([own[e, m], side], axis=1)
            columns = jnp.dot(
                held, jnp.concatenate([from_own, from_side], axis=0), preferred_element_type=jnp.float32
            )
            done = jnp.dot(row_bands[m], columns.astype(jnp.bfloat16), preferred_element_type=jnp.float32)
            slot = maps * e + m
            plane[slot + maps] = plane[slot] + done[:, :LANES]
            beyond = done[:, LANES:]
            packed = beyond[:edge_rows]
            for part in range(1, parts):
                packed = jnp.where(edge_group == part, beyond[EDGE * part : EDGE * part + edge_rows], packed)
            edge[slot + maps] = edge[slot] + packed

    step = 2 if epochs % 2 == 0 and slots % 2 == 0 else 1

    def several(i, carry):
        g = (step * i) // slots

        @pl.when(lax.rem(step * i, slots) == 0)
        def _():
            @pl.when(column < GRID_X - 1)
            def _():
                side_copy(0, g).wait_recv()

            @pl.when(column > 0)
            def _():
                side_copy(1, g).wait_recv()

        for turn in range(step):
            correlate(step * i + turn, g, lax.rem(step * i, slots) + turn)
        return carry

    lax.fori_loop(0, epochs // step, several, 0)

    def vel_copy(at):
        return pltpu.make_async_remote_copy(
            src_ref=send_v.at[at], dst_ref=recv_v.at[at], send_sem=sv.at[at], recv_sem=rv.at[at],
            device_id={"vel": partner}, device_id_type=mesh_id,
        )

    def epoch_copy(at):
        peer = lax.rem(group + 1 + at // block, blocks)
        return pltpu.make_async_remote_copy(
            src_ref=send_x.at[at], dst_ref=recv_x.at[at], send_sem=sx.at[at], recv_sem=rx.at[at],
            device_id={"epoch": peer}, device_id_type=mesh_id,
        )

    index = edge_index((EDGE, LANES))
    near_edge = (lane[:EDGE] < EDGE // 2) | (lane[:EDGE] >= LANES - EDGE // 2)

    def stack(slot, carry):
        a = blocks - 1 - slot // (2 * block)
        turn = lax.rem(slot, 2 * block)
        mine = ((turn > 0) & (lax.rem(turn, 2) == 0)) | (turn == 2 * block - 1)
        b = jnp.where(mine, 0, 1)
        j = jnp.where(turn == 2 * block - 1, block - 1, jnp.where(mine, turn // 2 - 1, (turn + 1) // 2))
        spot = a * block + j
        k = (lax.rem(group + a, blocks) * 2 + lax.rem(member + b, 2)) * block + j
        low = jnp.zeros((), jnp.int32)
        summed = jnp.zeros((maps * tile, LANES), jnp.float32)
        margins = [jnp.zeros((EDGE, LANES), jnp.float32) for _ in range(maps)]
        lefts, rights = [], []
        for run in range(runs):
            high = ends[k, run] if run < runs - 1 else epochs
            at = first + jnp.minimum(low, epochs - 1)
            down = offsets[0, k, at]
            right = offsets[1, k, at]
            rows = pl.ds(down + HEAD, tile)
            few = pl.ds(down + HEAD, EDGE)
            taken = (index >= jnp.minimum(right, 0)) & (index < jnp.maximum(right, 0))
            pieces = []
            for m in range(maps):
                piece = plane[maps * high + m, rows, :]
                rim = edge[maps * high + m, few, :]
                if run > 0:
                    piece = piece - plane[maps * low + m, rows, :]
                    rim = rim - edge[maps * low + m, few, :]
                pieces.append(piece.astype(jnp.bfloat16))
                rim = jnp.where(taken, rim, 0.0)
                margins[m] += pltpu.roll(rim, (LANES - right) & (LANES - 1), axis=1)
            lefts.append(jnp.concatenate(pieces, axis=0))
            rights.append(shift[right + REACH])
            low = high
            if len(lefts) == 2 or run == runs - 1:
                summed += jnp.dot(
                    jnp.concatenate(lefts, axis=1), jnp.concatenate(rights, axis=0),
                    preferred_element_type=jnp.float32,
                )
                lefts, rights = [], []
        for m in range(maps):
            for part in range(parts):
                rim = margins[m] if part == 0 else pltpu.roll(margins[m], LANES - EDGE * part, axis=1)
                begin = EDGE * part
                keep[b, j, m, begin : begin + EDGE] = (
                    summed[m * tile + begin : m * tile + begin + EDGE] + jnp.where(near_edge, rim, 0.0)
                )

        @pl.when(b == 1)
        def _():
            send_v[spot] = keep[1, j].astype(jnp.bfloat16)
            vel_copy(spot).start()

        @pl.when(b == 0)
        def _():
            vel_copy(spot).wait_recv()
            keep[0, j] = keep[0, j] + recv_v[spot].astype(jnp.float32)

            @pl.when(a > 0)
            def _():
                send_x[spot - block] = keep[0, j].astype(jnp.bfloat16)
                epoch_copy(spot - block).start()

        return carry

    ends_copy.wait()
    lax.fori_loop(0, 2 * blocks * block, stack, 0)

    def finish(j, carry):
        total = keep[0, j]
        for a in range(1, blocks):
            at = (a - 1) * block + j
            epoch_copy(at).wait_recv()
            total = total + recv_x[at].astype(jnp.float32)
        psi_out[j] = total[0]
        phi_out[j] = total[1]
        return carry

    lax.fori_loop(0, block, finish, 0)

    def drain_v(at, carry):
        vel_copy(at).wait_send()
        return carry

    lax.fori_loop(0, blocks * block, drain_v, 0)

    def drain_x(at, carry):
        epoch_copy(at).wait_send()
        return carry

    lax.fori_loop(0, (blocks - 1) * block, drain_x, 0)

    for g in range(groups):
        @pl.when(column > 0)
        def _():
            side_copy(0, g).wait_send()

        @pl.when(column < GRID_X - 1)
        def _():
            side_copy(1, g).wait_send()


def near_stacks(images, variances, valid, psf_sigma, offsets, plan):
    tile, sky, blocks, block, epochs, runs, slots = plan
    groups = -(-epochs // slots)
    rows_out = tile + 2 * HEAD
    smem = pl.BlockSpec(memory_space=pltpu.SMEM)
    vmem = pl.BlockSpec(memory_space=pltpu.VMEM)
    anywhere = pl.BlockSpec(memory_space=pl.ANY)
    dma = pltpu.SemaphoreType.DMA
    half = blocks * block
    far = max(1, (blocks - 1) * block)
    narrow, wide = jnp.bfloat16, jnp.float32
    scratch = [
        pltpu.VMEM((2 * (epochs + 1), rows_out, LANES), wide),
        pltpu.VMEM((2 * (epochs + 1), EDGE + 2 * HEAD, LANES), wide),
        pltpu.SMEM((VELS, LANES), jnp.int32),
        pltpu.VMEM((VELS, LANES), jnp.int32),
        dma(()),
        pltpu.VMEM((epochs, tile, tile), narrow),
        pltpu.VMEM((epochs, tile, tile), narrow),
        dma((2, groups)),
        pltpu.VMEM((slots, tile, 2 * LANES), narrow),
        pltpu.VMEM((2 * REACH + 1, tile, LANES), narrow),
        pltpu.VMEM((rows_out, tile), wide),
        pltpu.VMEM((2 * PACK, LANES), wide),
        pltpu.VMEM((2 * PACK, LANES), wide),
        pltpu.VMEM((2 * BACK, LANES), wide),
        pltpu.VMEM((epochs, 2, tile, tile), narrow),
        pltpu.VMEM((2, groups, 2, tile, LANES), narrow),
        pltpu.VMEM((2, groups, 2, tile, LANES), narrow),
        dma((2, groups)), dma((2, groups)),
        pltpu.VMEM((half, 2, tile, tile), narrow),
        pltpu.VMEM((half, 2, tile, tile), narrow),
        pltpu.VMEM((far, 2, tile, tile), narrow),
        pltpu.VMEM((far, 2, tile, tile), narrow),
        pltpu.VMEM((2, block, 2, tile, tile), wide),
        dma((half,)), dma((half,)), dma((far,)), dma((far,)),
    ]
    out = jax.ShapeDtypeStruct((block, tile, tile), jnp.float32)
    return pl.pallas_call(
        functools.partial(near_kernel, plan),
        out_shape=(out, out),
        in_specs=[smem, vmem, smem, smem, anywhere, anywhere],
        out_specs=(vmem, vmem),
        scratch_shapes=scratch,
        compiler_params=pltpu.CompilerParams(
            collective_id=0, has_side_effects=True, vmem_limit_bytes=56 * 2**20
        ),
    )(offsets, offsets, psf_sigma, valid.reshape(epochs), images, variances)


def far_stacks(images, variances, valid, psf_sigma, offsets, plan):
    tile, sky, blocks, block, epochs, runs = plan
    rows_out = -(-(tile + 2 * REACH) // 16) * 16
    smem = pl.BlockSpec(memory_space=pltpu.SMEM)
    vmem = pl.BlockSpec(memory_space=pltpu.VMEM)
    dma = pltpu.SemaphoreType.DMA
    half = blocks * block
    far = max(1, (blocks - 1) * block)
    scratch = [
        pltpu.VMEM((2 * (epochs + 1), rows_out, LANES), jnp.float32),
        pltpu.VMEM((2 * (epochs + 1), rows_out, LANES), jnp.float32),
        pltpu.SMEM((VELS, LANES), jnp.int32),
        pltpu.VMEM((VELS, LANES), jnp.int32),
        dma(()),
        pltpu.VMEM((rows_out, tile + LANES), jnp.float32),
        pltpu.VMEM((LANES, 2 * LANES), jnp.float32),
        pltpu.VMEM((1, LANES, 2 * LANES), jnp.float32),
        pltpu.VMEM((2, 2, 2 * LANES, 2 * LANES), jnp.bfloat16),
        pltpu.VMEM((half, 2, tile, tile), jnp.bfloat16),
        pltpu.VMEM((half, 2, tile, tile), jnp.bfloat16),
        pltpu.VMEM((far, 2, tile, tile), jnp.bfloat16),
        pltpu.VMEM((far, 2, tile, tile), jnp.bfloat16),
        pltpu.VMEM((2, block, 2, tile, tile), jnp.float32),
        dma((half,)), dma((half,)), dma((far,)), dma((far,)),
    ]
    usable = valid[:, 0].astype(jnp.float32)[:, None, None]
    inverse = usable / variances[:, 0].astype(jnp.float32)
    scaled = images[:, 0].astype(jnp.float32) * inverse
    own = jnp.stack([scaled.astype(jnp.bfloat16), inverse.astype(jnp.bfloat16)], axis=1)
    out = jax.ShapeDtypeStruct((block, tile, tile), jnp.float32)
    return pl.pallas_call(
        functools.partial(fused_kernel, plan),
        out_shape=(out, out),
        in_specs=[smem, vmem, smem, vmem, vmem],
        out_specs=(vmem, vmem),
        scratch_shapes=scratch,
        compiler_params=pltpu.CompilerParams(
            collective_id=0, has_side_effects=True, vmem_limit_bytes=56 * 2**20
        ),
    )(offsets, offsets, psf_sigma, *strips(own, sky, tile))


def on_device(images, variances, valid, psf_sigma, offsets):
    epochs = images.shape[0]
    tile = images.shape[-1]
    sky = lax.axis_size("sky")
    blocks = lax.axis_size("epoch")
    block = VELS // (blocks * lax.axis_size("vel"))
    last_epoch = epochs * blocks * lax.axis_size("vel") - 1
    runs = 1 + 2 * -(-REACH * (epochs - 1) // last_epoch)
    plan = (tile, sky, blocks, block, epochs, runs)
    if sky == GRID_X:
        plan += (LANES // MARGIN // 2 * 2,)
        psi_sum, phi_sum = near_stacks(images, variances, valid, psf_sigma, offsets, plan)
    else:
        psi_sum, phi_sum = far_stacks(images, variances, valid, psf_sigma, offsets, plan)
    phi_sum = jnp.maximum(phi_sum, phi_floor)
    likelihood = psi_sum / jnp.sqrt(phi_sum)
    flux = psi_sum / phi_sum
    return (likelihood[:, None], flux[:, None])


def solution(mesh):
    placed = (
        P(("epoch", "vel"), ("field", "sky"), None, None),
        P(("epoch", "vel"), ("field", "sky"), None, None),
        P(("epoch", "vel"), ("field", "sky")),
        P(("field", "epoch", "vel")),
        P(None, None, "epoch"),
    )
    return jax.shard_map(
        on_device,
        mesh=mesh,
        in_specs=placed,
        out_specs=(
            P(("epoch", "vel"), ("field", "sky"), None, None),
            P(("epoch", "vel"), ("field", "sky"), None, None),
        ),
        check_vma=False,
    )
```

```python
import functools

import jax
import jax.numpy as jnp
from jax import lax
from jax.experimental import pallas as pl
from jax.experimental.pallas import tpu as pltpu
from jax.sharding import PartitionSpec as P

VELS = 16
REACH = 12
PSFR = 7
GRID_X = 4
MARGIN = REACH + PSFR
LANES = 128
HEAD = 16
PACK = 16
EDGE = 16
WINDOW = 32
CHUNK = 4

phi_floor = 0.25


def shifted(block, axis, distance):
    devices = range(lax.axis_size(axis))
    route = [((i - distance) % len(devices), i) for i in devices]
    return lax.ppermute(block, axis, route)


def positions(index, tile):
    return jnp.where(
        index < tile,
        index,
        jnp.where(
            index < tile + MARGIN,
            index - tile - MARGIN,
            jnp.where(index < tile + 2 * MARGIN, index - MARGIN, 4 * tile),
        ),
    )


FAR = -1.0e9


def exponents(distance):
    away = distance.astype(jnp.float32)
    return jnp.where(jnp.abs(distance) <= PSFR, -0.5 * away * away, FAR)


def fused_kernel(plan, *refs):
    tile, sky, blocks, block, epochs, runs = plan
    (offsets, motion, sigmas, own, halo, psi_out, phi_out, plane_a, plane_b, ends, ends_made, ends_sem, row_q,
     own_q, side_q, bands, send_v, recv_v, send_x, recv_x, keep, sv, rv, sx, rx) = refs
    maps = 2
    rows_in = row_q.shape[1]
    rows_out = plane_a.shape[1]
    width = 2 * LANES
    mesh_id = pl.DeviceIdType.MESH
    group = lax.axis_index("epoch")
    member = lax.axis_index("vel")
    partner = 1 - member

    barrier = pltpu.get_barrier_semaphore()
    greeted = 1
    pl.semaphore_signal(barrier, inc=1, device_id={"vel": partner}, device_id_type=mesh_id)
    for a in range(1, blocks):
        peer = lax.rem(group + a, blocks)
        pl.semaphore_signal(barrier, inc=1, device_id={"epoch": peer}, device_id_type=mesh_id)
        greeted += 1
    pl.semaphore_wait(barrier, greeted)

    shape = (rows_out, rows_in)
    row_q[...] = exponents(
        positions(lax.broadcasted_iota(jnp.int32, shape, 1), tile)
        - lax.broadcasted_iota(jnp.int32, shape, 0) + REACH
    )
    shape = (LANES, width)
    held = lax.broadcasted_iota(jnp.int32, shape, 0)
    shifted_out = lax.broadcasted_iota(jnp.int32, shape, 1) - REACH
    own_q[...] = exponents(held - shifted_out)
    side_q[0] = exponents(positions(held + tile, tile) - shifted_out)

    first = member * epochs

    at_epoch = lax.broadcasted_iota(jnp.int32, motion.shape[1:], 1)
    moved = jnp.zeros(motion.shape[1:], jnp.int32)
    for way in range(2):
        start = jnp.where(at_epoch == first, motion[way], 0)
        moved += jnp.abs(motion[way] - jnp.sum(start, axis=1, keepdims=True))
    held_here = (at_epoch >= first) & (at_epoch < first + epochs)
    counted = jnp.zeros(ends_made.shape, jnp.int32)
    at_run = lax.broadcasted_iota(jnp.int32, ends_made.shape, 1)
    for run in range(runs - 1):
        count = jnp.sum((held_here & (moved <= run)).astype(jnp.int32), axis=1, keepdims=True)
        counted = jnp.where(at_run == run, count, counted)
    ends_made[...] = counted
    ends_copy = pltpu.make_async_copy(ends_made, ends, ends_sem)
    ends_copy.start()
    plane_a[:maps] = jnp.zeros_like(plane_a[:maps])
    plane_b[:maps] = jnp.zeros_like(plane_b[:maps])

    def correlate(e, turn):
        sigma = jnp.full((8, LANES), sigmas[e], jnp.float32)
        power = 1.0 / (sigma * sigma)
        tap = lax.broadcasted_iota(jnp.int32, (8, LANES), 1) - PSFR
        norm = jnp.sum(jnp.exp(exponents(tap) * power), axis=1, keepdims=True)
        scale = (1.0 / norm)[:1]
        power = power[:1, :1]

        def both(q):
            profile = jnp.exp(q * power) * scale
            return profile.astype(jnp.bfloat16), (profile * profile).astype(jnp.bfloat16)

        row_bands = both(row_q[...])
        for part, q in enumerate((own_q[...], side_q[0])):
            for m, made in enumerate(both(q)):
                bands[turn, m, part * LANES : (part + 1) * LANES] = made
        for m in range(maps):
            side = halo[e, m]
            held = jnp.concatenate([own[e, m], side], axis=1)
            rows = jnp.dot(row_bands[m], held, preferred_element_type=jnp.float32)
            done = jnp.dot(
                rows.astype(jnp.bfloat16), bands[turn, m], preferred_element_type=jnp.float32
            )
            at = maps * e + m
            plane_a[at + maps] = plane_a[at] + done[:, :LANES]
            plane_b[at + maps] = plane_b[at] + done[:, LANES:]

    step = 2 if epochs % 2 == 0 else 1

    def several(i, carry):
        for turn in range(step):
            correlate(step * i + turn, turn)
        return carry

    lax.fori_loop(0, epochs // step, several, 0)

    def vel_copy(at):
        return pltpu.make_async_remote_copy(
            src_ref=send_v.at[at], dst_ref=recv_v.at[at], send_sem=sv.at[at], recv_sem=rv.at[at],
            device_id={"vel": partner}, device_id_type=mesh_id,
        )

    def epoch_copy(at):
        peer = lax.rem(group + 1 + at // block, blocks)
        return pltpu.make_async_remote_copy(
            src_ref=send_x.at[at], dst_ref=recv_x.at[at], send_sem=sx.at[at], recv_sem=rx.at[at],
            device_id={"epoch": peer}, device_id_type=mesh_id,
        )

    def stack(slot, carry):
        a = blocks - 1 - slot // (2 * block)
        turn = lax.rem(slot, 2 * block)
        mine = ((turn > 0) & (lax.rem(turn, 2) == 0)) | (turn == 2 * block - 1)
        b = jnp.where(mine, 0, 1)
        j = jnp.where(turn == 2 * block - 1, block - 1, jnp.where(mine, turn // 2 - 1, (turn + 1) // 2))
        place = a * block + j
        k = (lax.rem(group + a, blocks) * 2 + lax.rem(member + b, 2)) * block + j
        lane = lax.broadcasted_iota(jnp.int32, (tile, LANES), 1)
        summed = [jnp.zeros((tile, LANES), jnp.float32) for _ in range(maps)]
        low = jnp.zeros((), jnp.int32)
        for run in range(runs):
            high = ends[k, run] if run < runs - 1 else epochs
            at = first + jnp.minimum(low, epochs - 1)
            down = offsets[0, k, at] + REACH
            right = offsets[1, k, at] + REACH
            rows = pl.ds(down, tile)
            for m in range(maps):
                left_part = plane_a[maps * high + m, rows, :] - plane_a[maps * low + m, rows, :]
                right_part = plane_b[maps * high + m, rows, :] - plane_b[maps * low + m, rows, :]
                merged = jnp.where(lane >= right, left_part, right_part)
                summed[m] += pltpu.roll(merged, LANES - right, axis=1)
            low = high
        for m in range(maps):
            keep[b, j, m] = summed[m]

        @pl.when(b == 1)
        def _():
            send_v[place] = keep[1, j].astype(jnp.bfloat16)
            vel_copy(place).start()

        @pl.when(b == 0)
        def _():
            vel_copy(place).wait_recv()
            keep[0, j] = keep[0, j] + recv_v[place].astype(jnp.float32)

            @pl.when(a > 0)
            def _():
                send_x[place - block] = keep[0, j].astype(jnp.bfloat16)
                epoch_copy(place - block).start()

        return carry

    ends_copy.wait()
    lax.fori_loop(0, 2 * blocks * block, stack, 0)

    def finish(j, carry):
        total = keep[0, j]
        for a in range(1, blocks):
            at = (a - 1) * block + j
            epoch_copy(at).wait_recv()
            total = total + recv_x[at].astype(jnp.float32)
        psi_out[j] = total[0]
        phi_out[j] = total[1]
        return carry

    lax.fori_loop(0, block, finish, 0)

    def drain_v(at, carry):
        vel_copy(at).wait_send()
        return carry

    lax.fori_loop(0, blocks * block, drain_v, 0)

    def drain_x(at, carry):
        epoch_copy(at).wait_send()
        return carry

    lax.fori_loop(0, (blocks - 1) * block, drain_x, 0)


def strips(own, tile_count, tile):
    position = (lax.axis_index("sky") + GRID_X // 2) % tile_count
    column = position % GRID_X
    left = shifted(own[..., tile - MARGIN :], "sky", 1)
    right = shifted(own[..., :MARGIN], "sky", -1)
    left = jnp.where(column > 0, left, jnp.zeros_like(left))
    right = jnp.where(column < GRID_X - 1, right, jnp.zeros_like(right))
    blank = jnp.zeros(own.shape[:3] + (LANES - 2 * MARGIN,), jnp.bfloat16)
    both = jnp.concatenate([own, left, right, blank], axis=3)
    upper = shifted(both[:, :, tile - MARGIN :], "sky", GRID_X)
    lower = shifted(both[:, :, :MARGIN], "sky", -GRID_X)
    upper = jnp.where(position >= GRID_X, upper, jnp.zeros_like(upper))
    lower = jnp.where(position < tile_count - GRID_X, lower, jnp.zeros_like(lower))
    blank = jnp.zeros(both.shape[:2] + (LANES - 2 * MARGIN, both.shape[3]), jnp.bfloat16)
    both = jnp.concatenate([both, upper, lower, blank], axis=2)
    return both[..., :tile], both[..., tile:]


def near_kernel(plan, *refs):
    tile, sky, blocks, block, epochs, runs, chunk = plan
    (offsets, motion, sigmas, valid, images, variances, psi_out, phi_out, plane, edge, ends, ends_made, ends_sem,
     image, variance, load_sem, shift, edge_shift, unplace, row_q, edge_q,
     send_v, recv_v, send_x, recv_x, keep, strip, send_z, recv_z, passed,
     sv, rv, sx, rx, sz, rz, sp, rp) = refs
    maps = 2
    mesh_id = pl.DeviceIdType.MESH
    me = lax.axis_index("sky")
    group = lax.axis_index("epoch")
    member = lax.axis_index("vel")
    column = lax.rem(lax.rem(me + GRID_X // 2, sky), GRID_X)
    before = lax.rem(me + sky - 1, sky)
    after = lax.rem(me + 1, sky)
    partner = 1 - member
    peer = 1 - group
    has_before = column > 0
    has_after = column < GRID_X - 1

    barrier = pltpu.get_barrier_semaphore()
    pl.semaphore_signal(barrier, inc=1, device_id={"vel": partner}, device_id_type=mesh_id)
    pl.semaphore_signal(barrier, inc=1, device_id={"epoch": peer}, device_id_type=mesh_id)

    @pl.when(has_before)
    def _():
        pl.semaphore_signal(barrier, inc=1, device_id={"sky": before}, device_id_type=mesh_id)

    @pl.when(has_after)
    def _():
        pl.semaphore_signal(barrier, inc=1, device_id={"sky": after}, device_id_type=mesh_id)

    greeted = 2 + jnp.where(has_before, 1, 0) + jnp.where(has_after, 1, 0)

    def load(which, c):
        source, held = ((images, image), (variances, variance))[which]
        span = pl.ds(c * chunk, chunk)
        return pltpu.make_async_copy(source.at[span, 0], held.at[span], load_sem.at[which, c])

    for c in range(epochs // chunk):
        for which in range(2):
            load(which, c).start()

    def iota(shape, axis):
        return lax.broadcasted_iota(jnp.int32, shape, axis)

    def one_hot(hit):
        return jnp.where(hit, 1.0, 0.0).astype(jnp.bfloat16)

    lane = iota((tile, LANES), 1)
    row = iota((tile, LANES), 0)

    def beyond(lanes):
        at_left = (lanes >= 0) & (lanes < MARGIN)
        at_right = (lanes >= WINDOW) & (lanes < WINDOW + MARGIN)
        return jnp.where(at_left, lanes - MARGIN, jnp.where(at_right, lanes - WINDOW + tile, 8 * tile))

    def edge_column(lanes):
        index = (lanes & (EDGE - 1)) - EDGE // 2
        held = (index >= -PSFR) & (index < PSFR)
        return jnp.where(held, jnp.where(index < 0, index, index + tile), 4 * tile)

    short = iota((EDGE, LANES), 1)
    from_edge = edge_column(iota((EDGE, LANES), 0))

    def make_shift(at, carry):
        right = at - REACH
        shift[at, :, :LANES] = one_hot(row == lane + right)
        shift[at, :, LANES:] = one_hot(row == beyond(lane) + right)
        edge_shift[at, :, :LANES] = one_hot(from_edge == short + right)
        edge_shift[at, :, LANES:] = one_hot(from_edge == beyond(short) + right)
        return carry

    lax.fori_loop(0, 2 * REACH + 1, make_shift, 0)
    for odd in range(2):
        for m in range(maps):
            begin = WINDOW * odd + 2 * WINDOW * m
            inside = (row >= begin) & (row < begin + MARGIN)
            unplace[odd, m, :tile] = one_hot(inside & (lane == row - begin))
            unplace[odd, m, tile:] = one_hot(inside & (lane == row - begin + tile - MARGIN))

    row_q[...] = exponents(iota(row_q.shape, 1) - iota(row_q.shape, 0) + HEAD)
    at = iota(edge_q.shape, 0)
    at = jnp.where(at < PACK, at, at + tile - 2 * PACK)
    edge_q[...] = exponents(at - edge_column(iota(edge_q.shape, 1)))

    first = member * epochs
    at_epoch = iota(motion.shape[1:], 1)
    moved = jnp.zeros(motion.shape[1:], jnp.int32)
    for way in range(2):
        start = jnp.where(at_epoch == first, motion[way], 0)
        moved += jnp.abs(motion[way] - jnp.sum(start, axis=1, keepdims=True))
    held_here = (at_epoch >= first) & (at_epoch < first + epochs)
    counted = jnp.zeros(ends_made.shape, jnp.int32)
    at_run = iota(ends_made.shape, 1)
    for run in range(runs - 1):
        count = jnp.sum((held_here & (moved <= run)).astype(jnp.int32), axis=1, keepdims=True)
        counted = jnp.where(at_run == run, count, counted)
    ends_made[...] = counted
    ends_copy = pltpu.make_async_copy(ends_made, ends, ends_sem)
    ends_copy.start()
    plane[:maps] = jnp.zeros_like(plane[:maps])
    edge[:maps] = jnp.zeros_like(edge[:maps])

    @pl.when(column == 0)
    def _():
        recv_z[1] = jnp.zeros_like(recv_z[1])
        passed[1] = jnp.zeros_like(passed[1])

    @pl.when(column == GRID_X - 1)
    def _():
        recv_z[0] = jnp.zeros_like(recv_z[0])
        passed[0] = jnp.zeros_like(passed[0])

    def correlate(e):
        usable = valid[e].astype(jnp.float32)
        inverse = usable / variance[e].astype(jnp.float32)
        scaled = image[e].astype(jnp.float32) * inverse
        sigma = jnp.full((8, LANES), sigmas[e], jnp.float32)
        power = 1.0 / (sigma * sigma)
        tap = iota((8, LANES), 1) - PSFR
        norm = jnp.sum(jnp.exp(exponents(tap) * power), axis=1, keepdims=True)
        scale = (1.0 / norm)[:1]
        power = power[:1, :1]

        def both(q):
            profile = jnp.exp(q * power) * scale
            return profile.astype(jnp.bfloat16), (profile * profile).astype(jnp.bfloat16)

        row_bands, edge_bands = both(row_q[...]), both(edge_q[...])
        for m, field in enumerate((scaled, inverse)):
            blank = jnp.zeros((tile - 2 * PACK, LANES), jnp.bfloat16)
            bands = jnp.concatenate(
                [
                    row_bands[m][HEAD : HEAD + tile],
                    jnp.concatenate([edge_bands[m][:PACK], blank, edge_bands[m][PACK:]], axis=0),
                ],
                axis=1,
            )
            columns = jnp.dot(field.astype(jnp.bfloat16), bands, preferred_element_type=jnp.float32)
            done = jnp.dot(row_bands[m], columns.astype(jnp.bfloat16), preferred_element_type=jnp.float32)
            slot = maps * e + m
            plane[slot + maps] = plane[slot] + done[:, :LANES]
            edge[slot + maps] = edge[slot] + done[:, LANES:]

    step = 2

    def several(i, carry):
        @pl.when(lax.rem(step * i, chunk) == 0)
        def _():
            for which in range(2):
                load(which, step * i // chunk).wait()

        for turn in range(step):
            correlate(step * i + turn)
        return carry

    lax.fori_loop(0, epochs // step, several, 0)

    def vel_copy(at):
        return pltpu.make_async_remote_copy(
            src_ref=send_v.at[at], dst_ref=recv_v.at[at], send_sem=sv.at[at], recv_sem=rv.at[at],
            device_id={"vel": partner}, device_id_type=mesh_id,
        )

    def epoch_copy(at):
        return pltpu.make_async_remote_copy(
            src_ref=send_x.at[at], dst_ref=recv_x.at[at], send_sem=sx.at[at], recv_sem=rx.at[at],
            device_id={"epoch": peer}, device_id_type=mesh_id,
        )

    def side_copy(to_after, at):
        return pltpu.make_async_remote_copy(
            src_ref=send_z.at[to_after, at], dst_ref=recv_z.at[to_after, at],
            send_sem=sz.at[to_after, at], recv_sem=rz.at[to_after, at],
            device_id={"sky": after if to_after else before}, device_id_type=mesh_id,
        )

    pairs = block // 2

    def pass_copy(to_after, at):
        return pltpu.make_async_remote_copy(
            src_ref=recv_z.at[to_after, pairs + at], dst_ref=passed.at[to_after, at],
            send_sem=sp.at[to_after, at], recv_sem=rp.at[to_after, at],
            device_id={"epoch": peer}, device_id_type=mesh_id,
        )

    part = iota((tile, LANES), 1) // EDGE
    first_window = (lane & WINDOW) == 0

    def stack(slot, carry):
        a = blocks - 1 - slot // (2 * block)
        turn = lax.rem(slot, 2 * block)
        mine = ((turn > 0) & (lax.rem(turn, 2) == 0)) | (turn == 2 * block - 1)
        b = jnp.where(mine, 0, 1)
        j = jnp.where(turn == 2 * block - 1, block - 1, jnp.where(mine, turn // 2 - 1, (turn + 1) // 2))
        spot = a * block + j
        k = (lax.rem(group + a, blocks) * 2 + lax.rem(member + b, 2)) * block + j
        low = jnp.zeros((), jnp.int32)
        summed = jnp.zeros((maps * tile, 2 * LANES), jnp.float32)
        rims = [jnp.zeros((tile, LANES), jnp.float32) for _ in range(maps)]
        lefts, rights, rim_rights = [], [], []
        for run in range(runs):
            high = ends[k, run] if run < runs - 1 else epochs
            at = first + jnp.minimum(low, epochs - 1)
            down = offsets[0, k, at]
            right = offsets[1, k, at]
            rows = pl.ds(down + HEAD, tile)
            pieces = []
            for m in range(maps):
                piece = plane[maps * high + m, rows, :]
                rim = edge[maps * high + m, rows, :]
                if run > 0:
                    piece = piece - plane[maps * low + m, rows, :]
                    rim = rim - edge[maps * low + m, rows, :]
                pieces.append(piece.astype(jnp.bfloat16))
                rims[m] = jnp.where(part == run, rim, rims[m])
            lefts.append(jnp.concatenate(pieces, axis=0))
            rights.append(shift[right + REACH])
            rim_rights.append(edge_shift[right + REACH])
            low = high
            if run == runs - 1:
                lefts.append(jnp.concatenate([rim.astype(jnp.bfloat16) for rim in rims], axis=0))
                spare = jnp.zeros((LANES - EDGE * runs, 2 * LANES), jnp.bfloat16)
                rights.append(jnp.concatenate(rim_rights + [spare], axis=0))
            while len(lefts) > 1:
                summed += jnp.dot(
                    jnp.concatenate(lefts[:2], axis=1), jnp.concatenate(rights[:2], axis=0),
                    preferred_element_type=jnp.float32,
                )
                lefts, rights = lefts[2:], rights[2:]
        outer = summed[:tile, LANES:] + pltpu.roll(summed[tile:, LANES:], 2 * WINDOW, axis=1)

        @pl.when(b == 1)
        def _():
            for m in range(maps):
                send_v[spot, m] = summed[m * tile : (m + 1) * tile, :LANES].astype(jnp.bfloat16)
            send_v[spot, maps] = outer.astype(jnp.bfloat16)
            vel_copy(spot).start()

        @pl.when(b == 0)
        def _():
            vel_copy(spot).wait_recv()
            for m in range(maps):
                total = summed[m * tile : (m + 1) * tile, :LANES] + recv_v[spot, m].astype(jnp.float32)
                keep[spot, m] = total
            strip[spot] = outer + recv_v[spot, maps].astype(jnp.float32)

            @pl.when(a > 0)
            def _():
                send_x[j] = keep[spot].astype(jnp.bfloat16)
                epoch_copy(j).start()

            @pl.when(lax.rem(j, 2) == 1)
            def _():
                even, odd = strip[spot - 1], strip[spot]
                at = spot // 2
                send_z[0, at] = jnp.where(first_window, even, pltpu.roll(odd, WINDOW, axis=1)).astype(jnp.bfloat16)
                send_z[1, at] = jnp.where(first_window, pltpu.roll(even, LANES - WINDOW, axis=1), odd).astype(jnp.bfloat16)

                @pl.when(has_before)
                def _():
                    side_copy(0, at).start()

                @pl.when(has_after)
                def _():
                    side_copy(1, at).start()

        return carry

    ends_copy.wait()
    pl.semaphore_wait(barrier, greeted)
    lax.fori_loop(0, 2 * blocks * block, stack, 0)

    for at in range(pairs):
        @pl.when(has_before)
        def _():
            side_copy(1, pairs + at).wait_recv()
            pass_copy(1, at).start()

        @pl.when(has_after)
        def _():
            side_copy(0, pairs + at).wait_recv()
            pass_copy(0, at).start()

    for at in range(pairs):
        @pl.when(has_before)
        def _():
            side_copy(1, at).wait_recv()
            pass_copy(1, at).wait_recv()

        @pl.when(has_after)
        def _():
            side_copy(0, at).wait_recv()
            pass_copy(0, at).wait_recv()

        for odd in range(2):
            j = 2 * at + odd
            epoch_copy(j).wait_recv()
            strips_in = jnp.concatenate([recv_z[1, at], recv_z[0, at], passed[1, at], passed[0, at]], axis=1)
            for m, out in enumerate((psi_out, phi_out)):
                added = jnp.dot(
                    strips_in, jnp.concatenate([unplace[odd, m]] * 2, axis=0), preferred_element_type=jnp.float32
                )
                out[j] = keep[j, m] + recv_x[j, m].astype(jnp.float32) + added

    def drain_v(at, carry):
        vel_copy(at).wait_send()
        return carry

    lax.fori_loop(0, blocks * block, drain_v, 0)

    def drain_x(at, carry):
        epoch_copy(at).wait_send()
        return carry

    lax.fori_loop(0, block, drain_x, 0)

    for to_after, there, back in ((0, has_before, has_after), (1, has_after, has_before)):
        @pl.when(there)
        def _():
            for at in range(blocks * pairs):
                side_copy(to_after, at).wait_send()

        @pl.when(back)
        def _():
            for at in range(pairs):
                pass_copy(to_after, at).wait_send()


def near_stacks(images, variances, valid, psf_sigma, offsets, plan):
    tile, sky, blocks, block, epochs, runs, chunk = plan
    rows_out = tile + 2 * HEAD
    smem = pl.BlockSpec(memory_space=pltpu.SMEM)
    vmem = pl.BlockSpec(memory_space=pltpu.VMEM)
    anywhere = pl.BlockSpec(memory_space=pl.ANY)
    dma = pltpu.SemaphoreType.DMA
    half = blocks * block
    pairs = block // 2
    narrow, wide = jnp.bfloat16, jnp.float32
    scratch = [
        pltpu.VMEM((2 * (epochs + 1), rows_out, LANES), wide),
        pltpu.VMEM((2 * (epochs + 1), rows_out, LANES), wide),
        pltpu.SMEM((VELS, LANES), jnp.int32),
        pltpu.VMEM((VELS, LANES), jnp.int32),
        dma(()),
        pltpu.VMEM((epochs, tile, tile), narrow),
        pltpu.VMEM((epochs, tile, tile), narrow),
        dma((2, epochs // chunk)),
        pltpu.VMEM((2 * REACH + 1, tile, 2 * LANES), narrow),
        pltpu.VMEM((2 * REACH + 1, EDGE, 2 * LANES), narrow),
        pltpu.VMEM((2, 2, 2 * tile, LANES), narrow),
        pltpu.VMEM((rows_out, tile), wide),
        pltpu.VMEM((2 * PACK, LANES), wide),
        pltpu.VMEM((half, 3, tile, tile), narrow),
        pltpu.VMEM((half, 3, tile, tile), narrow),
        pltpu.VMEM((block, 2, tile, tile), narrow),
        pltpu.VMEM((block, 2, tile, tile), narrow),
        pltpu.VMEM((half, 2, tile, tile), wide),
        pltpu.VMEM((half, tile, LANES), wide),
        pltpu.VMEM((2, half // 2, tile, LANES), narrow),
        pltpu.VMEM((2, half // 2, tile, LANES), narrow),
        pltpu.VMEM((2, pairs, tile, LANES), narrow),
        dma((half,)), dma((half,)), dma((block,)), dma((block,)),
        dma((2, half // 2)), dma((2, half // 2)), dma((2, pairs)), dma((2, pairs)),
    ]
    out = jax.ShapeDtypeStruct((block, tile, tile), jnp.float32)
    return pl.pallas_call(
        functools.partial(near_kernel, plan),
        out_shape=(out, out),
        in_specs=[smem, vmem, smem, smem, anywhere, anywhere],
        out_specs=(vmem, vmem),
        scratch_shapes=scratch,
        compiler_params=pltpu.CompilerParams(
            collective_id=0, has_side_effects=True, vmem_limit_bytes=56 * 2**20
        ),
    )(offsets, offsets, psf_sigma, valid.reshape(epochs), images, variances)


def far_stacks(images, variances, valid, psf_sigma, offsets, plan):
    tile, sky, blocks, block, epochs, runs = plan
    rows_out = -(-(tile + 2 * REACH) // 16) * 16
    smem = pl.BlockSpec(memory_space=pltpu.SMEM)
    vmem = pl.BlockSpec(memory_space=pltpu.VMEM)
    dma = pltpu.SemaphoreType.DMA
    half = blocks * block
    far = max(1, (blocks - 1) * block)
    scratch = [
        pltpu.VMEM((2 * (epochs + 1), rows_out, LANES), jnp.float32),
        pltpu.VMEM((2 * (epochs + 1), rows_out, LANES), jnp.float32),
        pltpu.SMEM((VELS, LANES), jnp.int32),
        pltpu.VMEM((VELS, LANES), jnp.int32),
        dma(()),
        pltpu.VMEM((rows_out, tile + LANES), jnp.float32),
        pltpu.VMEM((LANES, 2 * LANES), jnp.float32),
        pltpu.VMEM((1, LANES, 2 * LANES), jnp.float32),
        pltpu.VMEM((2, 2, 2 * LANES, 2 * LANES), jnp.bfloat16),
        pltpu.VMEM((half, 2, tile, tile), jnp.bfloat16),
        pltpu.VMEM((half, 2, tile, tile), jnp.bfloat16),
        pltpu.VMEM((far, 2, tile, tile), jnp.bfloat16),
        pltpu.VMEM((far, 2, tile, tile), jnp.bfloat16),
        pltpu.VMEM((2, block, 2, tile, tile), jnp.float32),
        dma((half,)), dma((half,)), dma((far,)), dma((far,)),
    ]
    usable = valid[:, 0].astype(jnp.float32)[:, None, None]
    inverse = usable / variances[:, 0].astype(jnp.float32)
    scaled = images[:, 0].astype(jnp.float32) * inverse
    own = jnp.stack([scaled.astype(jnp.bfloat16), inverse.astype(jnp.bfloat16)], axis=1)
    out = jax.ShapeDtypeStruct((block, tile, tile), jnp.float32)
    return pl.pallas_call(
        functools.partial(fused_kernel, plan),
        out_shape=(out, out),
        in_specs=[smem, vmem, smem, vmem, vmem],
        out_specs=(vmem, vmem),
        scratch_shapes=scratch,
        compiler_params=pltpu.CompilerParams(
            collective_id=0, has_side_effects=True, vmem_limit_bytes=56 * 2**20
        ),
    )(offsets, offsets, psf_sigma, *strips(own, sky, tile))


def on_device(images, variances, valid, psf_sigma, offsets):
    epochs = images.shape[0]
    tile = images.shape[-1]
    sky = lax.axis_size("sky")
    blocks = lax.axis_size("epoch")
    block = VELS // (blocks * lax.axis_size("vel"))
    last_epoch = epochs * blocks * lax.axis_size("vel") - 1
    runs = 1 + 2 * -(-REACH * (epochs - 1) // last_epoch)
    plan = (tile, sky, blocks, block, epochs, runs)
    few = EDGE * runs <= LANES and epochs % CHUNK == 0
    if sky == GRID_X and blocks == 2 and lax.axis_size("vel") == 2 and block % 2 == 0 and few:
        plan += (CHUNK,)
        psi_sum, phi_sum = near_stacks(images, variances, valid, psf_sigma, offsets, plan)
    else:
        psi_sum, phi_sum = far_stacks(images, variances, valid, psf_sigma, offsets, plan)
    phi_sum = jnp.maximum(phi_sum, phi_floor)
    likelihood = psi_sum / jnp.sqrt(phi_sum)
    flux = psi_sum / phi_sum
    return (likelihood[:, None], flux[:, None])


def solution(mesh):
    placed = (
        P(("epoch", "vel"), ("field", "sky"), None, None),
        P(("epoch", "vel"), ("field", "sky"), None, None),
        P(("epoch", "vel"), ("field", "sky")),
        P(("field", "epoch", "vel")),
        P(None, None, "epoch"),
    )
    return jax.shard_map(
        on_device,
        mesh=mesh,
        in_specs=placed,
        out_specs=(
            P(("epoch", "vel"), ("field", "sky"), None, None),
            P(("epoch", "vel"), ("field", "sky"), None, None),
        ),
        check_vma=False,
    )
```

```python
import functools

import jax
import jax.numpy as jnp
from jax import lax
from jax.experimental import pallas as pl
from jax.experimental.pallas import tpu as pltpu
from jax.sharding import PartitionSpec as P

VELS = 16
REACH = 12
PSFR = 7
GRID_X = 4
MARGIN = REACH + PSFR
LANES = 128
HEAD = 16
PACK = 16
EDGE = 16
WINDOW = 32
CHUNK = 4
KEPT = 55705600

phi_floor = 0.25


def shifted(block, axis, distance):
    devices = range(lax.axis_size(axis))
    route = [((i - distance) % len(devices), i) for i in devices]
    return lax.ppermute(block, axis, route)


def positions(index, tile):
    return jnp.where(
        index < tile,
        index,
        jnp.where(
            index < tile + MARGIN,
            index - tile - MARGIN,
            jnp.where(index < tile + 2 * MARGIN, index - MARGIN, 4 * tile),
        ),
    )


FAR = -1.0e9


def exponents(distance):
    away = distance.astype(jnp.float32)
    return jnp.where(jnp.abs(distance) <= PSFR, -0.5 * away * away, FAR)


def fused_kernel(plan, *refs):
    tile, sky, blocks, block, epochs, runs = plan
    (offsets, motion, sigmas, own, halo, psi_out, phi_out, plane_a, plane_b, ends, ends_made, ends_sem, row_q,
     own_q, side_q, bands, send_v, recv_v, send_x, recv_x, keep, sv, rv, sx, rx) = refs
    maps = 2
    rows_in = row_q.shape[1]
    rows_out = plane_a.shape[1]
    width = 2 * LANES
    mesh_id = pl.DeviceIdType.MESH
    group = lax.axis_index("epoch")
    member = lax.axis_index("vel")
    partner = 1 - member

    barrier = pltpu.get_barrier_semaphore()
    greeted = 1
    pl.semaphore_signal(barrier, inc=1, device_id={"vel": partner}, device_id_type=mesh_id)
    for a in range(1, blocks):
        peer = lax.rem(group + a, blocks)
        pl.semaphore_signal(barrier, inc=1, device_id={"epoch": peer}, device_id_type=mesh_id)
        greeted += 1
    pl.semaphore_wait(barrier, greeted)

    shape = (rows_out, rows_in)
    row_q[...] = exponents(
        positions(lax.broadcasted_iota(jnp.int32, shape, 1), tile)
        - lax.broadcasted_iota(jnp.int32, shape, 0) + REACH
    )
    shape = (LANES, width)
    held = lax.broadcasted_iota(jnp.int32, shape, 0)
    shifted_out = lax.broadcasted_iota(jnp.int32, shape, 1) - REACH
    own_q[...] = exponents(held - shifted_out)
    side_q[0] = exponents(positions(held + tile, tile) - shifted_out)

    first = member * epochs

    at_epoch = lax.broadcasted_iota(jnp.int32, motion.shape[1:], 1)
    moved = jnp.zeros(motion.shape[1:], jnp.int32)
    for way in range(2):
        start = jnp.where(at_epoch == first, motion[way], 0)
        moved += jnp.abs(motion[way] - jnp.sum(start, axis=1, keepdims=True))
    held_here = (at_epoch >= first) & (at_epoch < first + epochs)
    counted = jnp.zeros(ends_made.shape, jnp.int32)
    at_run = lax.broadcasted_iota(jnp.int32, ends_made.shape, 1)
    for run in range(runs - 1):
        count = jnp.sum((held_here & (moved <= run)).astype(jnp.int32), axis=1, keepdims=True)
        counted = jnp.where(at_run == run, count, counted)
    ends_made[...] = counted
    ends_copy = pltpu.make_async_copy(ends_made, ends, ends_sem)
    ends_copy.start()
    plane_a[:maps] = jnp.zeros_like(plane_a[:maps])
    plane_b[:maps] = jnp.zeros_like(plane_b[:maps])

    def correlate(e, turn):
        sigma = jnp.full((8, LANES), sigmas[e], jnp.float32)
        power = 1.0 / (sigma * sigma)
        tap = lax.broadcasted_iota(jnp.int32, (8, LANES), 1) - PSFR
        norm = jnp.sum(jnp.exp(exponents(tap) * power), axis=1, keepdims=True)
        scale = (1.0 / norm)[:1]
        power = power[:1, :1]

        def both(q):
            profile = jnp.exp(q * power) * scale
            return profile.astype(jnp.bfloat16), (profile * profile).astype(jnp.bfloat16)

        row_bands = both(row_q[...])
        for part, q in enumerate((own_q[...], side_q[0])):
            for m, made in enumerate(both(q)):
                bands[turn, m, part * LANES : (part + 1) * LANES] = made
        for m in range(maps):
            side = halo[e, m]
            held = jnp.concatenate([own[e, m], side], axis=1)
            rows = jnp.dot(row_bands[m], held, preferred_element_type=jnp.float32)
            done = jnp.dot(
                rows.astype(jnp.bfloat16), bands[turn, m], preferred_element_type=jnp.float32
            )
            at = maps * e + m
            plane_a[at + maps] = plane_a[at] + done[:, :LANES]
            plane_b[at + maps] = plane_b[at] + done[:, LANES:]

    step = 2 if epochs % 2 == 0 else 1

    def several(i, carry):
        for turn in range(step):
            correlate(step * i + turn, turn)
        return carry

    lax.fori_loop(0, epochs // step, several, 0)

    def vel_copy(at):
        return pltpu.make_async_remote_copy(
            src_ref=send_v.at[at], dst_ref=recv_v.at[at], send_sem=sv.at[at], recv_sem=rv.at[at],
            device_id={"vel": partner}, device_id_type=mesh_id,
        )

    def epoch_copy(at):
        peer = lax.rem(group + 1 + at // block, blocks)
        return pltpu.make_async_remote_copy(
            src_ref=send_x.at[at], dst_ref=recv_x.at[at], send_sem=sx.at[at], recv_sem=rx.at[at],
            device_id={"epoch": peer}, device_id_type=mesh_id,
        )

    def stack(slot, carry):
        a = blocks - 1 - slot // (2 * block)
        turn = lax.rem(slot, 2 * block)
        mine = ((turn > 0) & (lax.rem(turn, 2) == 0)) | (turn == 2 * block - 1)
        b = jnp.where(mine, 0, 1)
        j = jnp.where(turn == 2 * block - 1, block - 1, jnp.where(mine, turn // 2 - 1, (turn + 1) // 2))
        place = a * block + j
        k = (lax.rem(group + a, blocks) * 2 + lax.rem(member + b, 2)) * block + j
        lane = lax.broadcasted_iota(jnp.int32, (tile, LANES), 1)
        summed = [jnp.zeros((tile, LANES), jnp.float32) for _ in range(maps)]
        low = jnp.zeros((), jnp.int32)
        for run in range(runs):
            high = ends[k, run] if run < runs - 1 else epochs
            at = first + jnp.minimum(low, epochs - 1)
            down = offsets[0, k, at] + REACH
            right = offsets[1, k, at] + REACH
            rows = pl.ds(down, tile)
            for m in range(maps):
                left_part = plane_a[maps * high + m, rows, :] - plane_a[maps * low + m, rows, :]
                right_part = plane_b[maps * high + m, rows, :] - plane_b[maps * low + m, rows, :]
                merged = jnp.where(lane >= right, left_part, right_part)
                summed[m] += pltpu.roll(merged, LANES - right, axis=1)
            low = high
        for m in range(maps):
            keep[b, j, m] = summed[m]

        @pl.when(b == 1)
        def _():
            send_v[place] = keep[1, j].astype(jnp.bfloat16)
            vel_copy(place).start()

        @pl.when(b == 0)
        def _():
            vel_copy(place).wait_recv()
            keep[0, j] = keep[0, j] + recv_v[place].astype(jnp.float32)

            @pl.when(a > 0)
            def _():
                send_x[place - block] = keep[0, j].astype(jnp.bfloat16)
                epoch_copy(place - block).start()

        return carry

    ends_copy.wait()
    lax.fori_loop(0, 2 * blocks * block, stack, 0)

    def finish(j, carry):
        total = keep[0, j]
        for a in range(1, blocks):
            at = (a - 1) * block + j
            epoch_copy(at).wait_recv()
            total = total + recv_x[at].astype(jnp.float32)
        psi_out[j] = total[0]
        phi_out[j] = total[1]
        return carry

    lax.fori_loop(0, block, finish, 0)

    def drain_v(at, carry):
        vel_copy(at).wait_send()
        return carry

    lax.fori_loop(0, blocks * block, drain_v, 0)

    def drain_x(at, carry):
        epoch_copy(at).wait_send()
        return carry

    lax.fori_loop(0, (blocks - 1) * block, drain_x, 0)


def strips(own, tile_count, tile):
    position = (lax.axis_index("sky") + GRID_X // 2) % tile_count
    column = position % GRID_X
    left = shifted(own[..., tile - MARGIN :], "sky", 1)
    right = shifted(own[..., :MARGIN], "sky", -1)
    left = jnp.where(column > 0, left, jnp.zeros_like(left))
    right = jnp.where(column < GRID_X - 1, right, jnp.zeros_like(right))
    blank = jnp.zeros(own.shape[:3] + (LANES - 2 * MARGIN,), jnp.bfloat16)
    both = jnp.concatenate([own, left, right, blank], axis=3)
    upper = shifted(both[:, :, tile - MARGIN :], "sky", GRID_X)
    lower = shifted(both[:, :, :MARGIN], "sky", -GRID_X)
    upper = jnp.where(position >= GRID_X, upper, jnp.zeros_like(upper))
    lower = jnp.where(position < tile_count - GRID_X, lower, jnp.zeros_like(lower))
    blank = jnp.zeros(both.shape[:2] + (LANES - 2 * MARGIN, both.shape[3]), jnp.bfloat16)
    both = jnp.concatenate([both, upper, lower, blank], axis=2)
    return both[..., :tile], both[..., tile:]


def near_kernel(plan, *refs):
    tile, sky, blocks, block, epochs, runs, chunk = plan
    (offsets, motion, sigmas, valid, images, variances, psi_out, phi_out, plane, edge, ends, ends_made, ends_sem,
     image, variance, load_sem, shift, edge_shift, unplace, row_q, edge_q,
     send_v, recv_v, send_x, recv_x, keep, strip, send_z, recv_z, passed,
     sv, rv, sx, rx, sz, rz, sp, rp) = refs
    maps = 2
    mesh_id = pl.DeviceIdType.MESH
    me = lax.axis_index("sky")
    group = lax.axis_index("epoch")
    member = lax.axis_index("vel")
    column = lax.rem(lax.rem(me + GRID_X // 2, sky), GRID_X)
    before = lax.rem(me + sky - 1, sky)
    after = lax.rem(me + 1, sky)
    partner = 1 - member
    peer = 1 - group
    has_before = column > 0
    has_after = column < GRID_X - 1

    barrier = pltpu.get_barrier_semaphore()
    pl.semaphore_signal(barrier, inc=1, device_id={"vel": partner}, device_id_type=mesh_id)
    pl.semaphore_signal(barrier, inc=1, device_id={"epoch": peer}, device_id_type=mesh_id)

    @pl.when(has_before)
    def _():
        pl.semaphore_signal(barrier, inc=1, device_id={"sky": before}, device_id_type=mesh_id)

    @pl.when(has_after)
    def _():
        pl.semaphore_signal(barrier, inc=1, device_id={"sky": after}, device_id_type=mesh_id)

    greeted = 2 + jnp.where(has_before, 1, 0) + jnp.where(has_after, 1, 0)

    def load(which, c):
        source, held = ((images, image), (variances, variance))[which]
        span = pl.ds(c * chunk, chunk)
        return pltpu.make_async_copy(source.at[span, 0], held.at[span], load_sem.at[which, c])

    for c in range(epochs // chunk):
        for which in range(2):
            load(which, c).start()

    def iota(shape, axis):
        return lax.broadcasted_iota(jnp.int32, shape, axis)

    def one_hot(hit):
        return jnp.where(hit, 1.0, 0.0).astype(jnp.bfloat16)

    lane = iota((tile, LANES), 1)
    row = iota((tile, LANES), 0)

    def beyond(lanes):
        at_left = (lanes >= 0) & (lanes < MARGIN)
        at_right = (lanes >= WINDOW) & (lanes < WINDOW + MARGIN)
        return jnp.where(at_left, lanes - MARGIN, jnp.where(at_right, lanes - WINDOW + tile, 8 * tile))

    def edge_column(lanes):
        index = (lanes & (EDGE - 1)) - EDGE // 2
        held = (index >= -PSFR) & (index < PSFR)
        return jnp.where(held, jnp.where(index < 0, index, index + tile), 4 * tile)

    short = iota((EDGE, LANES), 1)
    from_edge = edge_column(iota((EDGE, LANES), 0))

    def make_shift(at, carry):
        right = at - REACH
        shift[at, :, :LANES] = one_hot(row == lane + right)
        shift[at, :, LANES:] = one_hot(row == beyond(lane) + right)
        edge_shift[at, :, :LANES] = one_hot(from_edge == short + right)
        edge_shift[at, :, LANES:] = one_hot(from_edge == beyond(short) + right)
        return carry

    lax.fori_loop(0, 2 * REACH + 1, make_shift, 0)
    for odd in range(2):
        for m in range(maps):
            begin = WINDOW * odd + 2 * WINDOW * m
            inside = (row >= begin) & (row < begin + MARGIN)
            unplace[odd, m, :tile] = one_hot(inside & (lane == row - begin))
            unplace[odd, m, tile:] = one_hot(inside & (lane == row - begin + tile - MARGIN))

    row_q[...] = exponents(iota(row_q.shape, 1) - iota(row_q.shape, 0) + HEAD)
    at = iota(edge_q.shape, 0)
    at = jnp.where(at < PACK, at, at + tile - 2 * PACK)
    edge_q[...] = exponents(at - edge_column(iota(edge_q.shape, 1)))

    first = member * epochs
    at_epoch = iota(motion.shape[1:], 1)
    moved = jnp.zeros(motion.shape[1:], jnp.int32)
    for way in range(2):
        start = jnp.where(at_epoch == first, motion[way], 0)
        moved += jnp.abs(motion[way] - jnp.sum(start, axis=1, keepdims=True))
    held_here = (at_epoch >= first) & (at_epoch < first + epochs)
    counted = jnp.zeros(ends_made.shape, jnp.int32)
    at_run = iota(ends_made.shape, 1)
    for run in range(runs - 1):
        count = jnp.sum((held_here & (moved <= run)).astype(jnp.int32), axis=1, keepdims=True)
        counted = jnp.where(at_run == run, count, counted)
    ends_made[...] = counted
    ends_copy = pltpu.make_async_copy(ends_made, ends, ends_sem)
    ends_copy.start()
    plane[:maps] = jnp.zeros_like(plane[:maps])
    edge[:maps] = jnp.zeros_like(edge[:maps])

    @pl.when(column == 0)
    def _():
        recv_z[1] = jnp.zeros_like(recv_z[1])
        passed[1] = jnp.zeros_like(passed[1])

    @pl.when(column == GRID_X - 1)
    def _():
        recv_z[0] = jnp.zeros_like(recv_z[0])
        passed[0] = jnp.zeros_like(passed[0])

    def correlate(e):
        usable = valid[e].astype(jnp.float32)
        inverse = usable / variance[e].astype(jnp.float32)
        scaled = image[e].astype(jnp.float32) * inverse
        sigma = jnp.full((8, LANES), sigmas[e], jnp.float32)
        power = 1.0 / (sigma * sigma)
        tap = iota((8, LANES), 1) - PSFR
        norm = jnp.sum(jnp.exp(exponents(tap) * power), axis=1, keepdims=True)
        scale = (1.0 / norm)[:1]
        power = power[:1, :1]

        def both(q):
            profile = jnp.exp(q * power) * scale
            return profile.astype(jnp.bfloat16), (profile * profile).astype(jnp.bfloat16)

        row_bands, edge_bands = both(row_q[...]), both(edge_q[...])
        for m, field in enumerate((scaled, inverse)):
            blank = jnp.zeros((tile - 2 * PACK, LANES), jnp.bfloat16)
            bands = jnp.concatenate(
                [
                    row_bands[m][HEAD : HEAD + tile],
                    jnp.concatenate([edge_bands[m][:PACK], blank, edge_bands[m][PACK:]], axis=0),
                ],
                axis=1,
            )
            columns = jnp.dot(field.astype(jnp.bfloat16), bands, preferred_element_type=jnp.float32)
            done = jnp.dot(row_bands[m], columns.astype(jnp.bfloat16), preferred_element_type=jnp.float32)
            slot = maps * e + m
            plane[slot + maps] = plane[slot] + done[:, :LANES]
            edge[slot + maps] = edge[slot] + done[:, LANES:]

    step = 4

    def several(i, carry):
        @pl.when(lax.rem(step * i, chunk) == 0)
        def _():
            for which in range(2):
                load(which, step * i // chunk).wait()

        for turn in range(step):
            correlate(step * i + turn)
        return carry

    lax.fori_loop(0, epochs // step, several, 0)

    def vel_copy(at):
        return pltpu.make_async_remote_copy(
            src_ref=send_v.at[at], dst_ref=recv_v.at[at], send_sem=sv.at[at], recv_sem=rv.at[at],
            device_id={"vel": partner}, device_id_type=mesh_id,
        )

    def epoch_copy(at):
        return pltpu.make_async_remote_copy(
            src_ref=send_x.at[at], dst_ref=recv_x.at[at], send_sem=sx.at[at], recv_sem=rx.at[at],
            device_id={"epoch": peer}, device_id_type=mesh_id,
        )

    def side_copy(to_after, at):
        return pltpu.make_async_remote_copy(
            src_ref=send_z.at[to_after, at], dst_ref=recv_z.at[to_after, at],
            send_sem=sz.at[to_after, at], recv_sem=rz.at[to_after, at],
            device_id={"sky": after if to_after else before}, device_id_type=mesh_id,
        )

    pairs = block // 2

    def pass_copy(to_after, at):
        return pltpu.make_async_remote_copy(
            src_ref=recv_z.at[to_after, pairs + at], dst_ref=passed.at[to_after, at],
            send_sem=sp.at[to_after, at], recv_sem=rp.at[to_after, at],
            device_id={"epoch": peer}, device_id_type=mesh_id,
        )

    part = iota((tile, LANES), 1) // EDGE
    first_window = (lane & WINDOW) == 0

    def stacked(k):
        low = jnp.zeros((), jnp.int32)
        summed = jnp.zeros((maps * tile, 2 * LANES), jnp.float32)
        rims = [jnp.zeros((tile, LANES), jnp.float32) for _ in range(maps)]
        lefts, rights, rim_rights = [], [], []
        for run in range(runs):
            high = ends[k, run] if run < runs - 1 else epochs
            at = first + jnp.minimum(low, epochs - 1)
            down = offsets[0, k, at]
            right = offsets[1, k, at]
            rows = pl.ds(down + HEAD, tile)
            pieces = []
            for m in range(maps):
                piece = plane[maps * high + m, rows, :]
                rim = edge[maps * high + m, rows, :]
                if run > 0:
                    piece = piece - plane[maps * low + m, rows, :]
                    rim = rim - edge[maps * low + m, rows, :]
                pieces.append(piece.astype(jnp.bfloat16))
                rims[m] = jnp.where(part == run, rim, rims[m])
            lefts.append(jnp.concatenate(pieces, axis=0))
            rights.append(shift[right + REACH])
            rim_rights.append(edge_shift[right + REACH])
            low = high
            if run == runs - 1:
                lefts.append(jnp.concatenate([rim.astype(jnp.bfloat16) for rim in rims], axis=0))
                spare = jnp.zeros((LANES - EDGE * runs, 2 * LANES), jnp.bfloat16)
                rights.append(jnp.concatenate(rim_rights + [spare], axis=0))
            while len(lefts) > 1:
                summed += jnp.dot(
                    jnp.concatenate(lefts[:2], axis=1), jnp.concatenate(rights[:2], axis=0),
                    preferred_element_type=jnp.float32,
                )
                lefts, rights = lefts[2:], rights[2:]
        outer = summed[:tile, LANES:] + pltpu.roll(summed[tile:, LANES:], 2 * WINDOW, axis=1)
        return summed[:tile, :LANES], summed[tile:, :LANES], outer

    def spot_of(turn):
        return (blocks - 1 - turn // block) * block + lax.rem(turn, block)

    def finish(turn):
        spot = spot_of(turn)
        j = lax.rem(turn, block)
        vel_copy(spot).wait_recv()
        for m in range(maps):
            keep[spot, m] = keep[spot, m] + recv_v[spot, m].astype(jnp.float32)
        strip[spot] = strip[spot] + recv_v[spot, maps].astype(jnp.float32)

        @pl.when(spot >= block)
        def _():
            send_x[j] = keep[spot].astype(jnp.bfloat16)
            epoch_copy(j).start()

        @pl.when(lax.rem(j, 2) == 1)
        def _():
            even, odd = strip[spot - 1], strip[spot]
            at = spot // 2
            send_z[0, at] = jnp.where(first_window, even, pltpu.roll(odd, WINDOW, axis=1)).astype(jnp.bfloat16)
            send_z[1, at] = jnp.where(first_window, pltpu.roll(even, LANES - WINDOW, axis=1), odd).astype(jnp.bfloat16)

            @pl.when(has_before)
            def _():
                side_copy(0, at).start()

            @pl.when(has_after)
            def _():
                side_copy(1, at).start()

    def stack(turn, carry):
        spot = spot_of(turn)
        owner = lax.rem(group + spot // block, blocks) * 2
        theirs = stacked((owner + partner) * block + lax.rem(turn, block))
        mine = stacked((owner + member) * block + lax.rem(turn, block))
        for m in range(maps + 1):
            send_v[spot, m] = theirs[m].astype(jnp.bfloat16)
        vel_copy(spot).start()
        for m in range(maps):
            keep[spot, m] = mine[m]
        strip[spot] = mine[maps]

        @pl.when(turn > 0)
        def _():
            finish(turn - 1)

        return carry

    ends_copy.wait()
    pl.semaphore_wait(barrier, greeted)
    lax.fori_loop(0, blocks * block, stack, 0)
    finish(blocks * block - 1)

    for at in range(pairs):
        @pl.when(has_before)
        def _():
            side_copy(1, pairs + at).wait_recv()
            pass_copy(1, at).start()

        @pl.when(has_after)
        def _():
            side_copy(0, pairs + at).wait_recv()
            pass_copy(0, at).start()

    for at in range(pairs):
        @pl.when(has_before)
        def _():
            side_copy(1, at).wait_recv()
            pass_copy(1, at).wait_recv()

        @pl.when(has_after)
        def _():
            side_copy(0, at).wait_recv()
            pass_copy(0, at).wait_recv()

        for odd in range(2):
            j = 2 * at + odd
            epoch_copy(j).wait_recv()
            strips_in = jnp.concatenate([recv_z[1, at], recv_z[0, at], passed[1, at], passed[0, at]], axis=1)
            for m, out in enumerate((psi_out, phi_out)):
                added = jnp.dot(
                    strips_in, jnp.concatenate([unplace[odd, m]] * 2, axis=0), preferred_element_type=jnp.float32
                )
                out[j] = keep[j, m] + recv_x[j, m].astype(jnp.float32) + added

    def drain_v(at, carry):
        vel_copy(at).wait_send()
        return carry

    lax.fori_loop(0, blocks * block, drain_v, 0)

    def drain_x(at, carry):
        epoch_copy(at).wait_send()
        return carry

    lax.fori_loop(0, block, drain_x, 0)

    for to_after, there, back in ((0, has_before, has_after), (1, has_after, has_before)):
        @pl.when(there)
        def _():
            for at in range(blocks * pairs):
                side_copy(to_after, at).wait_send()

        @pl.when(back)
        def _():
            for at in range(pairs):
                pass_copy(to_after, at).wait_send()


def near_stacks(images, variances, valid, psf_sigma, offsets, plan):
    tile, sky, blocks, block, epochs, runs, chunk = plan
    rows_out = tile + 2 * HEAD
    smem = pl.BlockSpec(memory_space=pltpu.SMEM)
    vmem = pl.BlockSpec(memory_space=pltpu.VMEM)
    anywhere = pl.BlockSpec(memory_space=pl.ANY)
    dma = pltpu.SemaphoreType.DMA
    half = blocks * block
    pairs = block // 2
    narrow, wide = jnp.bfloat16, jnp.float32
    scratch = [
        pltpu.VMEM((2 * (epochs + 1), rows_out, LANES), wide),
        pltpu.VMEM((2 * (epochs + 1), rows_out, LANES), wide),
        pltpu.SMEM((VELS, LANES), jnp.int32),
        pltpu.VMEM((VELS, LANES), jnp.int32),
        dma(()),
        pltpu.VMEM((epochs, tile, tile), narrow),
        pltpu.VMEM((epochs, tile, tile), narrow),
        dma((2, epochs // chunk)),
        pltpu.VMEM((2 * REACH + 1, tile, 2 * LANES), narrow),
        pltpu.VMEM((2 * REACH + 1, EDGE, 2 * LANES), narrow),
        pltpu.VMEM((2, 2, 2 * tile, LANES), narrow),
        pltpu.VMEM((rows_out, tile), wide),
        pltpu.VMEM((2 * PACK, LANES), wide),
        pltpu.VMEM((half, 3, tile, tile), narrow),
        pltpu.VMEM((half, 3, tile, tile), narrow),
        pltpu.VMEM((block, 2, tile, tile), narrow),
        pltpu.VMEM((block, 2, tile, tile), narrow),
        pltpu.VMEM((half, 2, tile, tile), wide),
        pltpu.VMEM((half, tile, LANES), wide),
        pltpu.VMEM((2, half // 2, tile, LANES), narrow),
        pltpu.VMEM((2, half // 2, tile, LANES), narrow),
        pltpu.VMEM((2, pairs, tile, LANES), narrow),
        dma((half,)), dma((half,)), dma((block,)), dma((block,)),
        dma((2, half // 2)), dma((2, half // 2)), dma((2, pairs)), dma((2, pairs)),
    ]
    out = jax.ShapeDtypeStruct((block, tile, tile), jnp.float32)
    return pl.pallas_call(
        functools.partial(near_kernel, plan),
        out_shape=(out, out),
        in_specs=[smem, vmem, smem, smem, anywhere, anywhere],
        out_specs=(vmem, vmem),
        scratch_shapes=scratch,
        compiler_params=pltpu.CompilerParams(
            collective_id=0, has_side_effects=True, vmem_limit_bytes=KEPT
        ),
    )(offsets, offsets, psf_sigma, valid.reshape(epochs), images, variances)


def far_stacks(images, variances, valid, psf_sigma, offsets, plan):
    tile, sky, blocks, block, epochs, runs = plan
    rows_out = -(-(tile + 2 * REACH) // 16) * 16
    smem = pl.BlockSpec(memory_space=pltpu.SMEM)
    vmem = pl.BlockSpec(memory_space=pltpu.VMEM)
    dma = pltpu.SemaphoreType.DMA
    half = blocks * block
    far = max(1, (blocks - 1) * block)
    scratch = [
        pltpu.VMEM((2 * (epochs + 1), rows_out, LANES), jnp.float32),
        pltpu.VMEM((2 * (epochs + 1), rows_out, LANES), jnp.float32),
        pltpu.SMEM((VELS, LANES), jnp.int32),
        pltpu.VMEM((VELS, LANES), jnp.int32),
        dma(()),
        pltpu.VMEM((rows_out, tile + LANES), jnp.float32),
        pltpu.VMEM((LANES, 2 * LANES), jnp.float32),
        pltpu.VMEM((1, LANES, 2 * LANES), jnp.float32),
        pltpu.VMEM((2, 2, 2 * LANES, 2 * LANES), jnp.bfloat16),
        pltpu.VMEM((half, 2, tile, tile), jnp.bfloat16),
        pltpu.VMEM((half, 2, tile, tile), jnp.bfloat16),
        pltpu.VMEM((far, 2, tile, tile), jnp.bfloat16),
        pltpu.VMEM((far, 2, tile, tile), jnp.bfloat16),
        pltpu.VMEM((2, block, 2, tile, tile), jnp.float32),
        dma((half,)), dma((half,)), dma((far,)), dma((far,)),
    ]
    usable = valid[:, 0].astype(jnp.float32)[:, None, None]
    inverse = usable / variances[:, 0].astype(jnp.float32)
    scaled = images[:, 0].astype(jnp.float32) * inverse
    own = jnp.stack([scaled.astype(jnp.bfloat16), inverse.astype(jnp.bfloat16)], axis=1)
    out = jax.ShapeDtypeStruct((block, tile, tile), jnp.float32)
    return pl.pallas_call(
        functools.partial(fused_kernel, plan),
        out_shape=(out, out),
        in_specs=[smem, vmem, smem, vmem, vmem],
        out_specs=(vmem, vmem),
        scratch_shapes=scratch,
        compiler_params=pltpu.CompilerParams(
            collective_id=0, has_side_effects=True, vmem_limit_bytes=56 * 2**20
        ),
    )(offsets, offsets, psf_sigma, *strips(own, sky, tile))


def on_device(images, variances, valid, psf_sigma, offsets):
    epochs = images.shape[0]
    tile = images.shape[-1]
    sky = lax.axis_size("sky")
    blocks = lax.axis_size("epoch")
    block = VELS // (blocks * lax.axis_size("vel"))
    last_epoch = epochs * blocks * lax.axis_size("vel") - 1
    runs = 1 + 2 * -(-REACH * (epochs - 1) // last_epoch)
    plan = (tile, sky, blocks, block, epochs, runs)
    few = EDGE * runs <= LANES and epochs % CHUNK == 0
    if sky == GRID_X and blocks == 2 and lax.axis_size("vel") == 2 and block % 2 == 0 and few:
        plan += (CHUNK,)
        psi_sum, phi_sum = near_stacks(images, variances, valid, psf_sigma, offsets, plan)
    else:
        psi_sum, phi_sum = far_stacks(images, variances, valid, psf_sigma, offsets, plan)
    phi_sum = jnp.maximum(phi_sum, phi_floor)
    likelihood = psi_sum / jnp.sqrt(phi_sum)
    flux = psi_sum / phi_sum
    return (likelihood[:, None], flux[:, None])


def solution(mesh):
    placed = (
        P(("epoch", "vel"), ("field", "sky"), None, None),
        P(("epoch", "vel"), ("field", "sky"), None, None),
        P(("epoch", "vel"), ("field", "sky")),
        P(("field", "epoch", "vel")),
        P(None, None, "epoch"),
    )
    return jax.shard_map(
        on_device,
        mesh=mesh,
        in_specs=placed,
        out_specs=(
            P(("epoch", "vel"), ("field", "sky"), None, None),
            P(("epoch", "vel"), ("field", "sky"), None, None),
        ),
        check_vma=False,
    )
```

```python
import functools

import jax
import jax.numpy as jnp
from jax import lax
from jax.experimental import pallas as pl
from jax.experimental.pallas import tpu as pltpu
from jax.sharding import PartitionSpec as P

VELS = 16
REACH = 12
PSFR = 7
GRID_X = 4
MARGIN = REACH + PSFR
LANES = 128
HEAD = 16
PACK = 16
EDGE = 16
WINDOW = 32
CHUNK = 4
STEP = 2
KEPT = 55705600

phi_floor = 0.25


def shifted(block, axis, distance):
    devices = range(lax.axis_size(axis))
    route = [((i - distance) % len(devices), i) for i in devices]
    return lax.ppermute(block, axis, route)


def positions(index, tile):
    return jnp.where(
        index < tile,
        index,
        jnp.where(
            index < tile + MARGIN,
            index - tile - MARGIN,
            jnp.where(index < tile + 2 * MARGIN, index - MARGIN, 4 * tile),
        ),
    )


FAR = -1.0e9


def exponents(distance):
    away = distance.astype(jnp.float32)
    return jnp.where(jnp.abs(distance) <= PSFR, -0.5 * away * away, FAR)


def fused_kernel(plan, *refs):
    tile, sky, blocks, block, epochs, runs = plan
    (offsets, motion, sigmas, own, halo, psi_out, phi_out, plane_a, plane_b, ends, ends_made, ends_sem, row_q,
     own_q, side_q, bands, send_v, recv_v, send_x, recv_x, keep, sv, rv, sx, rx) = refs
    maps = 2
    rows_in = row_q.shape[1]
    rows_out = plane_a.shape[1]
    width = 2 * LANES
    mesh_id = pl.DeviceIdType.MESH
    group = lax.axis_index("epoch")
    member = lax.axis_index("vel")
    partner = 1 - member

    barrier = pltpu.get_barrier_semaphore()
    greeted = 1
    pl.semaphore_signal(barrier, inc=1, device_id={"vel": partner}, device_id_type=mesh_id)
    for a in range(1, blocks):
        peer = lax.rem(group + a, blocks)
        pl.semaphore_signal(barrier, inc=1, device_id={"epoch": peer}, device_id_type=mesh_id)
        greeted += 1
    pl.semaphore_wait(barrier, greeted)

    shape = (rows_out, rows_in)
    row_q[...] = exponents(
        positions(lax.broadcasted_iota(jnp.int32, shape, 1), tile)
        - lax.broadcasted_iota(jnp.int32, shape, 0) + REACH
    )
    shape = (LANES, width)
    held = lax.broadcasted_iota(jnp.int32, shape, 0)
    shifted_out = lax.broadcasted_iota(jnp.int32, shape, 1) - REACH
    own_q[...] = exponents(held - shifted_out)
    side_q[0] = exponents(positions(held + tile, tile) - shifted_out)

    first = member * epochs

    at_epoch = lax.broadcasted_iota(jnp.int32, motion.shape[1:], 1)
    moved = jnp.zeros(motion.shape[1:], jnp.int32)
    for way in range(2):
        start = jnp.where(at_epoch == first, motion[way], 0)
        moved += jnp.abs(motion[way] - jnp.sum(start, axis=1, keepdims=True))
    held_here = (at_epoch >= first) & (at_epoch < first + epochs)
    counted = jnp.zeros(ends_made.shape, jnp.int32)
    at_run = lax.broadcasted_iota(jnp.int32, ends_made.shape, 1)
    for run in range(runs - 1):
        count = jnp.sum((held_here & (moved <= run)).astype(jnp.int32), axis=1, keepdims=True)
        counted = jnp.where(at_run == run, count, counted)
    ends_made[...] = counted
    ends_copy = pltpu.make_async_copy(ends_made, ends, ends_sem)
    ends_copy.start()
    plane_a[:maps] = jnp.zeros_like(plane_a[:maps])
    plane_b[:maps] = jnp.zeros_like(plane_b[:maps])

    def correlate(e, turn):
        sigma = jnp.full((8, LANES), sigmas[e], jnp.float32)
        power = 1.0 / (sigma * sigma)
        tap = lax.broadcasted_iota(jnp.int32, (8, LANES), 1) - PSFR
        norm = jnp.sum(jnp.exp(exponents(tap) * power), axis=1, keepdims=True)
        scale = (1.0 / norm)[:1]
        power = power[:1, :1]

        def both(q):
            profile = jnp.exp(q * power) * scale
            return profile.astype(jnp.bfloat16), (profile * profile).astype(jnp.bfloat16)

        row_bands = both(row_q[...])
        for part, q in enumerate((own_q[...], side_q[0])):
            for m, made in enumerate(both(q)):
                bands[turn, m, part * LANES : (part + 1) * LANES] = made
        for m in range(maps):
            side = halo[e, m]
            held = jnp.concatenate([own[e, m], side], axis=1)
            rows = jnp.dot(row_bands[m], held, preferred_element_type=jnp.float32)
            done = jnp.dot(
                rows.astype(jnp.bfloat16), bands[turn, m], preferred_element_type=jnp.float32
            )
            at = maps * e + m
            plane_a[at + maps] = plane_a[at] + done[:, :LANES]
            plane_b[at + maps] = plane_b[at] + done[:, LANES:]

    step = 2 if epochs % 2 == 0 else 1

    def several(i, carry):
        for turn in range(step):
            correlate(step * i + turn, turn)
        return carry

    lax.fori_loop(0, epochs // step, several, 0)

    def vel_copy(at):
        return pltpu.make_async_remote_copy(
            src_ref=send_v.at[at], dst_ref=recv_v.at[at], send_sem=sv.at[at], recv_sem=rv.at[at],
            device_id={"vel": partner}, device_id_type=mesh_id,
        )

    def epoch_copy(at):
        peer = lax.rem(group + 1 + at // block, blocks)
        return pltpu.make_async_remote_copy(
            src_ref=send_x.at[at], dst_ref=recv_x.at[at], send_sem=sx.at[at], recv_sem=rx.at[at],
            device_id={"epoch": peer}, device_id_type=mesh_id,
        )

    def stack(slot, carry):
        a = blocks - 1 - slot // (2 * block)
        turn = lax.rem(slot, 2 * block)
        mine = ((turn > 0) & (lax.rem(turn, 2) == 0)) | (turn == 2 * block - 1)
        b = jnp.where(mine, 0, 1)
        j = jnp.where(turn == 2 * block - 1, block - 1, jnp.where(mine, turn // 2 - 1, (turn + 1) // 2))
        place = a * block + j
        k = (lax.rem(group + a, blocks) * 2 + lax.rem(member + b, 2)) * block + j
        lane = lax.broadcasted_iota(jnp.int32, (tile, LANES), 1)
        summed = [jnp.zeros((tile, LANES), jnp.float32) for _ in range(maps)]
        low = jnp.zeros((), jnp.int32)
        for run in range(runs):
            high = ends[k, run] if run < runs - 1 else epochs
            at = first + jnp.minimum(low, epochs - 1)
            down = offsets[0, k, at] + REACH
            right = offsets[1, k, at] + REACH
            rows = pl.ds(down, tile)
            for m in range(maps):
                left_part = plane_a[maps * high + m, rows, :] - plane_a[maps * low + m, rows, :]
                right_part = plane_b[maps * high + m, rows, :] - plane_b[maps * low + m, rows, :]
                merged = jnp.where(lane >= right, left_part, right_part)
                summed[m] += pltpu.roll(merged, LANES - right, axis=1)
            low = high
        for m in range(maps):
            keep[b, j, m] = summed[m]

        @pl.when(b == 1)
        def _():
            send_v[place] = keep[1, j].astype(jnp.bfloat16)
            vel_copy(place).start()

        @pl.when(b == 0)
        def _():
            vel_copy(place).wait_recv()
            keep[0, j] = keep[0, j] + recv_v[place].astype(jnp.float32)

            @pl.when(a > 0)
            def _():
                send_x[place - block] = keep[0, j].astype(jnp.bfloat16)
                epoch_copy(place - block).start()

        return carry

    ends_copy.wait()
    lax.fori_loop(0, 2 * blocks * block, stack, 0)

    def finish(j, carry):
        total = keep[0, j]
        for a in range(1, blocks):
            at = (a - 1) * block + j
            epoch_copy(at).wait_recv()
            total = total + recv_x[at].astype(jnp.float32)
        psi_out[j] = total[0]
        phi_out[j] = total[1]
        return carry

    lax.fori_loop(0, block, finish, 0)

    def drain_v(at, carry):
        vel_copy(at).wait_send()
        return carry

    lax.fori_loop(0, blocks * block, drain_v, 0)

    def drain_x(at, carry):
        epoch_copy(at).wait_send()
        return carry

    lax.fori_loop(0, (blocks - 1) * block, drain_x, 0)


def strips(own, tile_count, tile):
    position = (lax.axis_index("sky") + GRID_X // 2) % tile_count
    column = position % GRID_X
    left = shifted(own[..., tile - MARGIN :], "sky", 1)
    right = shifted(own[..., :MARGIN], "sky", -1)
    left = jnp.where(column > 0, left, jnp.zeros_like(left))
    right = jnp.where(column < GRID_X - 1, right, jnp.zeros_like(right))
    blank = jnp.zeros(own.shape[:3] + (LANES - 2 * MARGIN,), jnp.bfloat16)
    both = jnp.concatenate([own, left, right, blank], axis=3)
    upper = shifted(both[:, :, tile - MARGIN :], "sky", GRID_X)
    lower = shifted(both[:, :, :MARGIN], "sky", -GRID_X)
    upper = jnp.where(position >= GRID_X, upper, jnp.zeros_like(upper))
    lower = jnp.where(position < tile_count - GRID_X, lower, jnp.zeros_like(lower))
    blank = jnp.zeros(both.shape[:2] + (LANES - 2 * MARGIN, both.shape[3]), jnp.bfloat16)
    both = jnp.concatenate([both, upper, lower, blank], axis=2)
    return both[..., :tile], both[..., tile:]


def near_kernel(plan, *refs):
    tile, sky, blocks, block, epochs, runs, chunk = plan
    (offsets, motion, sigmas, valid, images, variances, psi_out, phi_out, plane, edge, ends, ends_made, ends_sem,
     image, variance, load_sem, shift, edge_shift, unplace, row_q, edge_q, row_bands, edge_bands, columns,
     send_v, recv_v, send_x, recv_x, keep, strip, send_z, recv_z, passed,
     sv, rv, sx, rx, sz, rz, sp, rp) = refs
    maps = 2
    mesh_id = pl.DeviceIdType.MESH
    me = lax.axis_index("sky")
    group = lax.axis_index("epoch")
    member = lax.axis_index("vel")
    column = lax.rem(lax.rem(me + GRID_X // 2, sky), GRID_X)
    before = lax.rem(me + sky - 1, sky)
    after = lax.rem(me + 1, sky)
    partner = 1 - member
    peer = 1 - group
    has_before = column > 0
    has_after = column < GRID_X - 1

    barrier = pltpu.get_barrier_semaphore()
    pl.semaphore_signal(barrier, inc=1, device_id={"vel": partner}, device_id_type=mesh_id)
    pl.semaphore_signal(barrier, inc=1, device_id={"epoch": peer}, device_id_type=mesh_id)

    @pl.when(has_before)
    def _():
        pl.semaphore_signal(barrier, inc=1, device_id={"sky": before}, device_id_type=mesh_id)

    @pl.when(has_after)
    def _():
        pl.semaphore_signal(barrier, inc=1, device_id={"sky": after}, device_id_type=mesh_id)

    greeted = 2 + jnp.where(has_before, 1, 0) + jnp.where(has_after, 1, 0)

    def load(which, c):
        source, held = ((images, image), (variances, variance))[which]
        span = pl.ds(c * chunk, chunk)
        return pltpu.make_async_copy(source.at[span, 0], held.at[span], load_sem.at[which, c])

    for c in range(epochs // chunk):
        for which in range(2):
            load(which, c).start()

    def iota(shape, axis):
        return lax.broadcasted_iota(jnp.int32, shape, axis)

    def one_hot(hit):
        return jnp.where(hit, 1.0, 0.0).astype(jnp.bfloat16)

    lane = iota((tile, LANES), 1)
    row = iota((tile, LANES), 0)

    def beyond(lanes):
        at_left = (lanes >= 0) & (lanes < MARGIN)
        at_right = (lanes >= WINDOW) & (lanes < WINDOW + MARGIN)
        return jnp.where(at_left, lanes - MARGIN, jnp.where(at_right, lanes - WINDOW + tile, 8 * tile))

    def edge_column(lanes):
        index = (lanes & (EDGE - 1)) - EDGE // 2
        held = (index >= -PSFR) & (index < PSFR)
        return jnp.where(held, jnp.where(index < 0, index, index + tile), 4 * tile)

    short = iota((EDGE, LANES), 1)
    from_edge = edge_column(iota((EDGE, LANES), 0))

    def make_shift(at, carry):
        right = at - REACH
        shift[at, :, :LANES] = one_hot(row == lane + right)
        shift[at, :, LANES:] = one_hot(row == beyond(lane) + right)
        edge_shift[at, :, :LANES] = one_hot(from_edge == short + right)
        edge_shift[at, :, LANES:] = one_hot(from_edge == beyond(short) + right)
        return carry

    lax.fori_loop(0, 2 * REACH + 1, make_shift, 0)
    for odd in range(2):
        for m in range(maps):
            begin = WINDOW * odd + 2 * WINDOW * m
            inside = (row >= begin) & (row < begin + MARGIN)
            unplace[odd, m, :tile] = one_hot(inside & (lane == row - begin))
            unplace[odd, m, tile:] = one_hot(inside & (lane == row - begin + tile - MARGIN))

    row_q[...] = exponents(iota(row_q.shape, 1) - iota(row_q.shape, 0) + HEAD)
    at = iota(edge_q.shape, 0)
    at = jnp.where(at < PACK, at, at + tile - 2 * PACK)
    edge_q[...] = exponents(at - edge_column(iota(edge_q.shape, 1)))

    first = member * epochs
    at_epoch = iota(motion.shape[1:], 1)
    moved = jnp.zeros(motion.shape[1:], jnp.int32)
    for way in range(2):
        start = jnp.where(at_epoch == first, motion[way], 0)
        moved += jnp.abs(motion[way] - jnp.sum(start, axis=1, keepdims=True))
    held_here = (at_epoch >= first) & (at_epoch < first + epochs)
    counted = jnp.zeros(ends_made.shape, jnp.int32)
    at_run = iota(ends_made.shape, 1)
    for run in range(runs - 1):
        count = jnp.sum((held_here & (moved <= run)).astype(jnp.int32), axis=1, keepdims=True)
        counted = jnp.where(at_run == run, count, counted)
    ends_made[...] = counted
    ends_copy = pltpu.make_async_copy(ends_made, ends, ends_sem)
    ends_copy.start()
    plane[:maps] = jnp.zeros_like(plane[:maps])
    edge[:maps] = jnp.zeros_like(edge[:maps])

    @pl.when(column == 0)
    def _():
        recv_z[1] = jnp.zeros_like(recv_z[1])
        passed[1] = jnp.zeros_like(passed[1])

    @pl.when(column == GRID_X - 1)
    def _():
        recv_z[0] = jnp.zeros_like(recv_z[0])
        passed[0] = jnp.zeros_like(passed[0])

    def make_bands(e, carry):
        sigma = jnp.full((8, LANES), sigmas[e], jnp.float32)
        power = 1.0 / (sigma * sigma)
        tap = iota((8, LANES), 1) - PSFR
        norm = jnp.sum(jnp.exp(exponents(tap) * power), axis=1, keepdims=True)
        scale = (1.0 / norm)[:1]
        power = power[:1, :1]
        for q, bands in ((row_q, row_bands), (edge_q, edge_bands)):
            profile = jnp.exp(q[...] * power) * scale
            bands[e, 0] = profile.astype(jnp.bfloat16)
            bands[e, 1] = (profile * profile).astype(jnp.bfloat16)
        return carry

    lax.fori_loop(0, epochs, make_bands, 0)

    def across(e):
        usable = valid[e].astype(jnp.float32)
        inverse = usable / variance[e].astype(jnp.float32)
        scaled = image[e].astype(jnp.float32) * inverse
        blank = jnp.zeros((tile - 2 * PACK, LANES), jnp.bfloat16)
        for m, field in enumerate((scaled, inverse)):
            rims = jnp.concatenate([edge_bands[e, m, :PACK], blank, edge_bands[e, m, PACK:]], axis=0)
            bands = jnp.concatenate([row_bands[e, m, HEAD : HEAD + tile], rims], axis=1)
            done = jnp.dot(field.astype(jnp.bfloat16), bands, preferred_element_type=jnp.float32)
            columns[e, m] = done.astype(jnp.bfloat16)

    def down(e):
        for m in range(maps):
            done = jnp.dot(row_bands[e, m], columns[e, m], preferred_element_type=jnp.float32)
            slot = maps * e + m
            plane[slot + maps] = plane[slot] + done[:, :LANES]
            edge[slot + maps] = edge[slot] + done[:, LANES:]

    def all_across(c, carry):
        for which in range(2):
            load(which, c).wait()
        for turn in range(chunk):
            across(chunk * c + turn)
        return carry

    lax.fori_loop(0, epochs // chunk, all_across, 0)

    def all_down(c, carry):
        for turn in range(STEP):
            down(STEP * c + turn)
        return carry

    lax.fori_loop(0, epochs // STEP, all_down, 0)

    def vel_copy(at):
        return pltpu.make_async_remote_copy(
            src_ref=send_v.at[at], dst_ref=recv_v.at[at], send_sem=sv.at[at], recv_sem=rv.at[at],
            device_id={"vel": partner}, device_id_type=mesh_id,
        )

    def epoch_copy(at):
        return pltpu.make_async_remote_copy(
            src_ref=send_x.at[at], dst_ref=recv_x.at[at], send_sem=sx.at[at], recv_sem=rx.at[at],
            device_id={"epoch": peer}, device_id_type=mesh_id,
        )

    def side_copy(to_after, at):
        return pltpu.make_async_remote_copy(
            src_ref=send_z.at[to_after, at], dst_ref=recv_z.at[to_after, at],
            send_sem=sz.at[to_after, at], recv_sem=rz.at[to_after, at],
            device_id={"sky": after if to_after else before}, device_id_type=mesh_id,
        )

    pairs = block // 2

    def pass_copy(to_after, at):
        return pltpu.make_async_remote_copy(
            src_ref=recv_z.at[to_after, pairs + at], dst_ref=passed.at[to_after, at],
            send_sem=sp.at[to_after, at], recv_sem=rp.at[to_after, at],
            device_id={"epoch": peer}, device_id_type=mesh_id,
        )

    part = iota((tile, LANES), 1) // EDGE
    first_window = (lane & WINDOW) == 0

    def stacked(k):
        low = jnp.zeros((), jnp.int32)
        summed = jnp.zeros((maps * tile, 2 * LANES), jnp.float32)
        rims = [jnp.zeros((tile, LANES), jnp.float32) for _ in range(maps)]
        lefts, rights, rim_rights = [], [], []
        for run in range(runs):
            high = ends[k, run] if run < runs - 1 else epochs
            at = first + jnp.minimum(low, epochs - 1)
            down = offsets[0, k, at]
            right = offsets[1, k, at]
            rows = pl.ds(down + HEAD, tile)
            pieces = []
            for m in range(maps):
                piece = plane[maps * high + m, rows, :]
                rim = edge[maps * high + m, rows, :]
                if run > 0:
                    piece = piece - plane[maps * low + m, rows, :]
                    rim = rim - edge[maps * low + m, rows, :]
                pieces.append(piece.astype(jnp.bfloat16))
                rims[m] = jnp.where(part == run, rim, rims[m])
            lefts.append(jnp.concatenate(pieces, axis=0))
            rights.append(shift[right + REACH])
            rim_rights.append(edge_shift[right + REACH])
            low = high
            if run == runs - 1:
                lefts.append(jnp.concatenate([rim.astype(jnp.bfloat16) for rim in rims], axis=0))
                spare = jnp.zeros((LANES - EDGE * runs, 2 * LANES), jnp.bfloat16)
                rights.append(jnp.concatenate(rim_rights + [spare], axis=0))
            while len(lefts) > 1:
                summed += jnp.dot(
                    jnp.concatenate(lefts[:2], axis=1), jnp.concatenate(rights[:2], axis=0),
                    preferred_element_type=jnp.float32,
                )
                lefts, rights = lefts[2:], rights[2:]
        outer = summed[:tile, LANES:] + pltpu.roll(summed[tile:, LANES:], 2 * WINDOW, axis=1)
        return summed[:tile, :LANES], summed[tile:, :LANES], outer

    def spot_of(turn):
        return (blocks - 1 - turn // block) * block + lax.rem(turn, block)

    def owner_of(turn):
        return lax.rem(group + spot_of(turn) // block, blocks) * 2

    def theirs(turn):
        return stacked((owner_of(turn) + partner) * block + lax.rem(turn, block))

    def ours(turn):
        return stacked((owner_of(turn) + member) * block + lax.rem(turn, block))

    def hand_over(turn, parts):
        spot = spot_of(turn)
        for m in range(maps + 1):
            send_v[spot, m] = parts[m].astype(jnp.bfloat16)
        vel_copy(spot).start()

    def finish(turn, parts):
        spot = spot_of(turn)
        j = lax.rem(turn, block)
        vel_copy(spot).wait_recv()
        totals = [parts[m] + recv_v[spot, m].astype(jnp.float32) for m in range(maps + 1)]
        strip[spot] = totals[maps]

        @pl.when(spot >= block)
        def _():
            for m in range(maps):
                send_x[j, m] = totals[m].astype(jnp.bfloat16)
            epoch_copy(j).start()

        @pl.when(spot < block)
        def _():
            for m in range(maps):
                keep[j, m] = totals[m]

        @pl.when(lax.rem(j, 2) == 1)
        def _():
            even, odd = strip[spot - 1], strip[spot]
            at = spot // 2
            send_z[0, at] = jnp.where(first_window, even, pltpu.roll(odd, WINDOW, axis=1)).astype(jnp.bfloat16)
            send_z[1, at] = jnp.where(first_window, pltpu.roll(even, LANES - WINDOW, axis=1), odd).astype(jnp.bfloat16)

            @pl.when(has_before)
            def _():
                side_copy(0, at).start()

            @pl.when(has_after)
            def _():
                side_copy(1, at).start()

    last = blocks * block - 1

    def stack(turn, carry):
        ahead = theirs(turn + 1)
        kept = ours(turn)
        hand_over(turn + 1, ahead)
        finish(turn, kept)
        return carry

    ends_copy.wait()
    ahead = theirs(0)
    pl.semaphore_wait(barrier, greeted)
    hand_over(0, ahead)
    lax.fori_loop(0, last, stack, 0)
    finish(last, ours(last))

    for at in range(pairs):
        @pl.when(has_before)
        def _():
            side_copy(1, pairs + at).wait_recv()
            pass_copy(1, at).start()

        @pl.when(has_after)
        def _():
            side_copy(0, pairs + at).wait_recv()
            pass_copy(0, at).start()

    for at in range(pairs):
        @pl.when(has_before)
        def _():
            side_copy(1, at).wait_recv()
            pass_copy(1, at).wait_recv()

        @pl.when(has_after)
        def _():
            side_copy(0, at).wait_recv()
            pass_copy(0, at).wait_recv()

        for odd in range(2):
            j = 2 * at + odd
            epoch_copy(j).wait_recv()
            strips_in = jnp.concatenate([recv_z[1, at], recv_z[0, at], passed[1, at], passed[0, at]], axis=1)
            for m, out in enumerate((psi_out, phi_out)):
                added = jnp.dot(
                    strips_in, jnp.concatenate([unplace[odd, m]] * 2, axis=0), preferred_element_type=jnp.float32
                )
                out[j] = keep[j, m] + recv_x[j, m].astype(jnp.float32) + added

    def drain_v(at, carry):
        vel_copy(at).wait_send()
        return carry

    lax.fori_loop(0, blocks * block, drain_v, 0)

    def drain_x(at, carry):
        epoch_copy(at).wait_send()
        return carry

    lax.fori_loop(0, block, drain_x, 0)

    for to_after, there, back in ((0, has_before, has_after), (1, has_after, has_before)):
        @pl.when(there)
        def _():
            for at in range(blocks * pairs):
                side_copy(to_after, at).wait_send()

        @pl.when(back)
        def _():
            for at in range(pairs):
                pass_copy(to_after, at).wait_send()


def near_stacks(images, variances, valid, psf_sigma, offsets, plan):
    tile, sky, blocks, block, epochs, runs, chunk = plan
    rows_out = tile + 2 * HEAD
    smem = pl.BlockSpec(memory_space=pltpu.SMEM)
    vmem = pl.BlockSpec(memory_space=pltpu.VMEM)
    anywhere = pl.BlockSpec(memory_space=pl.ANY)
    dma = pltpu.SemaphoreType.DMA
    half = blocks * block
    pairs = block // 2
    narrow, wide = jnp.bfloat16, jnp.float32
    scratch = [
        pltpu.VMEM((2 * (epochs + 1), rows_out, LANES), wide),
        pltpu.VMEM((2 * (epochs + 1), rows_out, LANES), wide),
        pltpu.SMEM((VELS, LANES), jnp.int32),
        pltpu.VMEM((VELS, LANES), jnp.int32),
        dma(()),
        pltpu.VMEM((epochs, tile, tile), narrow),
        pltpu.VMEM((epochs, tile, tile), narrow),
        dma((2, epochs // chunk)),
        pltpu.VMEM((2 * REACH + 1, tile, 2 * LANES), narrow),
        pltpu.VMEM((2 * REACH + 1, EDGE, 2 * LANES), narrow),
        pltpu.VMEM((2, 2, 2 * tile, LANES), narrow),
        pltpu.VMEM((rows_out, tile), wide),
        pltpu.VMEM((2 * PACK, LANES), wide),
        pltpu.VMEM((epochs, 2, rows_out, tile), narrow),
        pltpu.VMEM((epochs, 2, 2 * PACK, LANES), narrow),
        pltpu.VMEM((epochs, 2, tile, 2 * LANES), narrow),
        pltpu.VMEM((half, 3, tile, tile), narrow),
        pltpu.VMEM((half, 3, tile, tile), narrow),
        pltpu.VMEM((block, 2, tile, tile), narrow),
        pltpu.VMEM((block, 2, tile, tile), narrow),
        pltpu.VMEM((block, 2, tile, tile), wide),
        pltpu.VMEM((half, tile, LANES), wide),
        pltpu.VMEM((2, half // 2, tile, LANES), narrow),
        pltpu.VMEM((2, half // 2, tile, LANES), narrow),
        pltpu.VMEM((2, pairs, tile, LANES), narrow),
        dma((half,)), dma((half,)), dma((block,)), dma((block,)),
        dma((2, half // 2)), dma((2, half // 2)), dma((2, pairs)), dma((2, pairs)),
    ]
    out = jax.ShapeDtypeStruct((block, tile, tile), jnp.float32)
    return pl.pallas_call(
        functools.partial(near_kernel, plan),
        out_shape=(out, out),
        in_specs=[smem, vmem, smem, smem, anywhere, anywhere],
        out_specs=(vmem, vmem),
        scratch_shapes=scratch,
        compiler_params=pltpu.CompilerParams(
            collective_id=0, has_side_effects=True, vmem_limit_bytes=KEPT
        ),
    )(offsets, offsets, psf_sigma, valid.reshape(epochs), images, variances)


def far_stacks(images, variances, valid, psf_sigma, offsets, plan):
    tile, sky, blocks, block, epochs, runs = plan
    rows_out = -(-(tile + 2 * REACH) // 16) * 16
    smem = pl.BlockSpec(memory_space=pltpu.SMEM)
    vmem = pl.BlockSpec(memory_space=pltpu.VMEM)
    dma = pltpu.SemaphoreType.DMA
    half = blocks * block
    far = max(1, (blocks - 1) * block)
    scratch = [
        pltpu.VMEM((2 * (epochs + 1), rows_out, LANES), jnp.float32),
        pltpu.VMEM((2 * (epochs + 1), rows_out, LANES), jnp.float32),
        pltpu.SMEM((VELS, LANES), jnp.int32),
        pltpu.VMEM((VELS, LANES), jnp.int32),
        dma(()),
        pltpu.VMEM((rows_out, tile + LANES), jnp.float32),
        pltpu.VMEM((LANES, 2 * LANES), jnp.float32),
        pltpu.VMEM((1, LANES, 2 * LANES), jnp.float32),
        pltpu.VMEM((2, 2, 2 * LANES, 2 * LANES), jnp.bfloat16),
        pltpu.VMEM((half, 2, tile, tile), jnp.bfloat16),
        pltpu.VMEM((half, 2, tile, tile), jnp.bfloat16),
        pltpu.VMEM((far, 2, tile, tile), jnp.bfloat16),
        pltpu.VMEM((far, 2, tile, tile), jnp.bfloat16),
        pltpu.VMEM((2, block, 2, tile, tile), jnp.float32),
        dma((half,)), dma((half,)), dma((far,)), dma((far,)),
    ]
    usable = valid[:, 0].astype(jnp.float32)[:, None, None]
    inverse = usable / variances[:, 0].astype(jnp.float32)
    scaled = images[:, 0].astype(jnp.float32) * inverse
    own = jnp.stack([scaled.astype(jnp.bfloat16), inverse.astype(jnp.bfloat16)], axis=1)
    out = jax.ShapeDtypeStruct((block, tile, tile), jnp.float32)
    return pl.pallas_call(
        functools.partial(fused_kernel, plan),
        out_shape=(out, out),
        in_specs=[smem, vmem, smem, vmem, vmem],
        out_specs=(vmem, vmem),
        scratch_shapes=scratch,
        compiler_params=pltpu.CompilerParams(
            collective_id=0, has_side_effects=True, vmem_limit_bytes=56 * 2**20
        ),
    )(offsets, offsets, psf_sigma, *strips(own, sky, tile))


def on_device(images, variances, valid, psf_sigma, offsets):
    epochs = images.shape[0]
    tile = images.shape[-1]
    sky = lax.axis_size("sky")
    blocks = lax.axis_size("epoch")
    block = VELS // (blocks * lax.axis_size("vel"))
    last_epoch = epochs * blocks * lax.axis_size("vel") - 1
    runs = 1 + 2 * -(-REACH * (epochs - 1) // last_epoch)
    plan = (tile, sky, blocks, block, epochs, runs)
    few = EDGE * runs <= LANES and epochs % CHUNK == 0
    if sky == GRID_X and blocks == 2 and lax.axis_size("vel") == 2 and block % 2 == 0 and few:
        plan += (CHUNK,)
        psi_sum, phi_sum = near_stacks(images, variances, valid, psf_sigma, offsets, plan)
    else:
        psi_sum, phi_sum = far_stacks(images, variances, valid, psf_sigma, offsets, plan)
    phi_sum = jnp.maximum(phi_sum, phi_floor)
    likelihood = psi_sum / jnp.sqrt(phi_sum)
    flux = psi_sum / phi_sum
    return (likelihood[:, None], flux[:, None])


def solution(mesh):
    placed = (
        P(("epoch", "vel"), ("field", "sky"), None, None),
        P(("epoch", "vel"), ("field", "sky"), None, None),
        P(("epoch", "vel"), ("field", "sky")),
        P(("field", "epoch", "vel")),
        P(None, None, "epoch"),
    )
    return jax.shard_map(
        on_device,
        mesh=mesh,
        in_specs=placed,
        out_specs=(
            P(("epoch", "vel"), ("field", "sky"), None, None),
            P(("epoch", "vel"), ("field", "sky"), None, None),
        ),
        check_vma=False,
    )
```

```python
import functools

import jax
import jax.numpy as jnp
from jax import lax
from jax.experimental import pallas as pl
from jax.experimental.pallas import tpu as pltpu
from jax.sharding import PartitionSpec as P

VELS = 16
REACH = 12
PSFR = 7
GRID_X = 4
MARGIN = REACH + PSFR
LANES = 128
HEAD = 16
PACK = 16
EDGE = 16
WINDOW = 32
CHUNK = 4
STEP = 2
KEPT = 55705600

phi_floor = 0.25


def shifted(block, axis, distance):
    devices = range(lax.axis_size(axis))
    route = [((i - distance) % len(devices), i) for i in devices]
    return lax.ppermute(block, axis, route)


def positions(index, tile):
    return jnp.where(
        index < tile,
        index,
        jnp.where(
            index < tile + MARGIN,
            index - tile - MARGIN,
            jnp.where(index < tile + 2 * MARGIN, index - MARGIN, 4 * tile),
        ),
    )


FAR = -1.0e9


def exponents(distance):
    away = distance.astype(jnp.float32)
    return jnp.where(jnp.abs(distance) <= PSFR, -0.5 * away * away, FAR)


def fused_kernel(plan, *refs):
    tile, sky, blocks, block, epochs, runs = plan
    (offsets, motion, sigmas, own, halo, psi_out, phi_out, plane_a, plane_b, ends, ends_made, ends_sem, row_q,
     own_q, side_q, bands, send_v, recv_v, send_x, recv_x, keep, sv, rv, sx, rx) = refs
    maps = 2
    rows_in = row_q.shape[1]
    rows_out = plane_a.shape[1]
    width = 2 * LANES
    mesh_id = pl.DeviceIdType.MESH
    group = lax.axis_index("epoch")
    member = lax.axis_index("vel")
    partner = 1 - member

    barrier = pltpu.get_barrier_semaphore()
    greeted = 1
    pl.semaphore_signal(barrier, inc=1, device_id={"vel": partner}, device_id_type=mesh_id)
    for a in range(1, blocks):
        peer = lax.rem(group + a, blocks)
        pl.semaphore_signal(barrier, inc=1, device_id={"epoch": peer}, device_id_type=mesh_id)
        greeted += 1
    pl.semaphore_wait(barrier, greeted)

    shape = (rows_out, rows_in)
    row_q[...] = exponents(
        positions(lax.broadcasted_iota(jnp.int32, shape, 1), tile)
        - lax.broadcasted_iota(jnp.int32, shape, 0) + REACH
    )
    shape = (LANES, width)
    held = lax.broadcasted_iota(jnp.int32, shape, 0)
    shifted_out = lax.broadcasted_iota(jnp.int32, shape, 1) - REACH
    own_q[...] = exponents(held - shifted_out)
    side_q[0] = exponents(positions(held + tile, tile) - shifted_out)

    first = member * epochs

    at_epoch = lax.broadcasted_iota(jnp.int32, motion.shape[1:], 1)
    moved = jnp.zeros(motion.shape[1:], jnp.int32)
    for way in range(2):
        start = jnp.where(at_epoch == first, motion[way], 0)
        moved += jnp.abs(motion[way] - jnp.sum(start, axis=1, keepdims=True))
    held_here = (at_epoch >= first) & (at_epoch < first + epochs)
    counted = jnp.zeros(ends_made.shape, jnp.int32)
    at_run = lax.broadcasted_iota(jnp.int32, ends_made.shape, 1)
    for run in range(runs - 1):
        count = jnp.sum((held_here & (moved <= run)).astype(jnp.int32), axis=1, keepdims=True)
        counted = jnp.where(at_run == run, count, counted)
    ends_made[...] = counted
    ends_copy = pltpu.make_async_copy(ends_made, ends, ends_sem)
    ends_copy.start()
    plane_a[:maps] = jnp.zeros_like(plane_a[:maps])
    plane_b[:maps] = jnp.zeros_like(plane_b[:maps])

    def correlate(e, turn):
        sigma = jnp.full((8, LANES), sigmas[e], jnp.float32)
        power = 1.0 / (sigma * sigma)
        tap = lax.broadcasted_iota(jnp.int32, (8, LANES), 1) - PSFR
        norm = jnp.sum(jnp.exp(exponents(tap) * power), axis=1, keepdims=True)
        scale = (1.0 / norm)[:1]
        power = power[:1, :1]

        def both(q):
            profile = jnp.exp(q * power) * scale
            return profile.astype(jnp.bfloat16), (profile * profile).astype(jnp.bfloat16)

        row_bands = both(row_q[...])
        for part, q in enumerate((own_q[...], side_q[0])):
            for m, made in enumerate(both(q)):
                bands[turn, m, part * LANES : (part + 1) * LANES] = made
        for m in range(maps):
            side = halo[e, m]
            held = jnp.concatenate([own[e, m], side], axis=1)
            rows = jnp.dot(row_bands[m], held, preferred_element_type=jnp.float32)
            done = jnp.dot(
                rows.astype(jnp.bfloat16), bands[turn, m], preferred_element_type=jnp.float32
            )
            at = maps * e + m
            plane_a[at + maps] = plane_a[at] + done[:, :LANES]
            plane_b[at + maps] = plane_b[at] + done[:, LANES:]

    step = 2 if epochs % 2 == 0 else 1

    def several(i, carry):
        for turn in range(step):
            correlate(step * i + turn, turn)
        return carry

    lax.fori_loop(0, epochs // step, several, 0)

    def vel_copy(at):
        return pltpu.make_async_remote_copy(
            src_ref=send_v.at[at], dst_ref=recv_v.at[at], send_sem=sv.at[at], recv_sem=rv.at[at],
            device_id={"vel": partner}, device_id_type=mesh_id,
        )

    def epoch_copy(at):
        peer = lax.rem(group + 1 + at // block, blocks)
        return pltpu.make_async_remote_copy(
            src_ref=send_x.at[at], dst_ref=recv_x.at[at], send_sem=sx.at[at], recv_sem=rx.at[at],
            device_id={"epoch": peer}, device_id_type=mesh_id,
        )

    def stack(slot, carry):
        a = blocks - 1 - slot // (2 * block)
        turn = lax.rem(slot, 2 * block)
        mine = ((turn > 0) & (lax.rem(turn, 2) == 0)) | (turn == 2 * block - 1)
        b = jnp.where(mine, 0, 1)
        j = jnp.where(turn == 2 * block - 1, block - 1, jnp.where(mine, turn // 2 - 1, (turn + 1) // 2))
        place = a * block + j
        k = (lax.rem(group + a, blocks) * 2 + lax.rem(member + b, 2)) * block + j
        lane = lax.broadcasted_iota(jnp.int32, (tile, LANES), 1)
        summed = [jnp.zeros((tile, LANES), jnp.float32) for _ in range(maps)]
        low = jnp.zeros((), jnp.int32)
        for run in range(runs):
            high = ends[k, run] if run < runs - 1 else epochs
            at = first + jnp.minimum(low, epochs - 1)
            down = offsets[0, k, at] + REACH
            right = offsets[1, k, at] + REACH
            rows = pl.ds(down, tile)
            for m in range(maps):
                left_part = plane_a[maps * high + m, rows, :] - plane_a[maps * low + m, rows, :]
                right_part = plane_b[maps * high + m, rows, :] - plane_b[maps * low + m, rows, :]
                merged = jnp.where(lane >= right, left_part, right_part)
                summed[m] += pltpu.roll(merged, LANES - right, axis=1)
            low = high
        for m in range(maps):
            keep[b, j, m] = summed[m]

        @pl.when(b == 1)
        def _():
            send_v[place] = keep[1, j].astype(jnp.bfloat16)
            vel_copy(place).start()

        @pl.when(b == 0)
        def _():
            vel_copy(place).wait_recv()
            keep[0, j] = keep[0, j] + recv_v[place].astype(jnp.float32)

            @pl.when(a > 0)
            def _():
                send_x[place - block] = keep[0, j].astype(jnp.bfloat16)
                epoch_copy(place - block).start()

        return carry

    ends_copy.wait()
    lax.fori_loop(0, 2 * blocks * block, stack, 0)

    def finish(j, carry):
        total = keep[0, j]
        for a in range(1, blocks):
            at = (a - 1) * block + j
            epoch_copy(at).wait_recv()
            total = total + recv_x[at].astype(jnp.float32)
        psi_out[j] = total[0]
        phi_out[j] = total[1]
        return carry

    lax.fori_loop(0, block, finish, 0)

    def drain_v(at, carry):
        vel_copy(at).wait_send()
        return carry

    lax.fori_loop(0, blocks * block, drain_v, 0)

    def drain_x(at, carry):
        epoch_copy(at).wait_send()
        return carry

    lax.fori_loop(0, (blocks - 1) * block, drain_x, 0)


def strips(own, tile_count, tile):
    position = (lax.axis_index("sky") + GRID_X // 2) % tile_count
    column = position % GRID_X
    left = shifted(own[..., tile - MARGIN :], "sky", 1)
    right = shifted(own[..., :MARGIN], "sky", -1)
    left = jnp.where(column > 0, left, jnp.zeros_like(left))
    right = jnp.where(column < GRID_X - 1, right, jnp.zeros_like(right))
    blank = jnp.zeros(own.shape[:3] + (LANES - 2 * MARGIN,), jnp.bfloat16)
    both = jnp.concatenate([own, left, right, blank], axis=3)
    upper = shifted(both[:, :, tile - MARGIN :], "sky", GRID_X)
    lower = shifted(both[:, :, :MARGIN], "sky", -GRID_X)
    upper = jnp.where(position >= GRID_X, upper, jnp.zeros_like(upper))
    lower = jnp.where(position < tile_count - GRID_X, lower, jnp.zeros_like(lower))
    blank = jnp.zeros(both.shape[:2] + (LANES - 2 * MARGIN, both.shape[3]), jnp.bfloat16)
    both = jnp.concatenate([both, upper, lower, blank], axis=2)
    return both[..., :tile], both[..., tile:]


def near_kernel(plan, *refs):
    tile, sky, blocks, block, epochs, runs, chunk = plan
    (offsets, motion, sigmas, valid, images, variances, psi_out, phi_out, plane, edge, ends, ends_made, ends_sem,
     image, variance, load_sem, shift, edge_shift, unplace, row_q, edge_q, row_bands, edge_bands, columns,
     send_v, recv_v, send_x, recv_x, keep, strip, send_z, recv_z, passed,
     sv, rv, sx, rx, sz, rz, sp, rp) = refs
    maps = 2
    rows_out = row_q.shape[0]
    mesh_id = pl.DeviceIdType.MESH
    me = lax.axis_index("sky")
    group = lax.axis_index("epoch")
    member = lax.axis_index("vel")
    column = lax.rem(lax.rem(me + GRID_X // 2, sky), GRID_X)
    before = lax.rem(me + sky - 1, sky)
    after = lax.rem(me + 1, sky)
    partner = 1 - member
    peer = 1 - group
    has_before = column > 0
    has_after = column < GRID_X - 1

    barrier = pltpu.get_barrier_semaphore()
    pl.semaphore_signal(barrier, inc=1, device_id={"vel": partner}, device_id_type=mesh_id)
    pl.semaphore_signal(barrier, inc=1, device_id={"epoch": peer}, device_id_type=mesh_id)

    @pl.when(has_before)
    def _():
        pl.semaphore_signal(barrier, inc=1, device_id={"sky": before}, device_id_type=mesh_id)

    @pl.when(has_after)
    def _():
        pl.semaphore_signal(barrier, inc=1, device_id={"sky": after}, device_id_type=mesh_id)

    greeted = 2 + jnp.where(has_before, 1, 0) + jnp.where(has_after, 1, 0)

    def load(which, c):
        source, held = ((images, image), (variances, variance))[which]
        span = pl.ds(c * chunk, chunk)
        return pltpu.make_async_copy(source.at[span, 0], held.at[span], load_sem.at[which, c])

    for c in range(epochs // chunk):
        for which in range(2):
            load(which, c).start()

    def iota(shape, axis):
        return lax.broadcasted_iota(jnp.int32, shape, axis)

    def one_hot(hit):
        return jnp.where(hit, 1.0, 0.0).astype(jnp.bfloat16)

    lane = iota((tile, LANES), 1)
    row = iota((tile, LANES), 0)

    def beyond(lanes):
        at_left = (lanes >= 0) & (lanes < MARGIN)
        at_right = (lanes >= WINDOW) & (lanes < WINDOW + MARGIN)
        return jnp.where(at_left, lanes - MARGIN, jnp.where(at_right, lanes - WINDOW + tile, 8 * tile))

    def edge_column(lanes):
        index = (lanes & (EDGE - 1)) - EDGE // 2
        held = (index >= -PSFR) & (index < PSFR)
        return jnp.where(held, jnp.where(index < 0, index, index + tile), 4 * tile)

    short = iota((EDGE, LANES), 1)
    from_edge = edge_column(iota((EDGE, LANES), 0))

    def make_shift(at, carry):
        right = at - REACH
        shift[at, :, :LANES] = one_hot(row == lane + right)
        shift[at, :, LANES:] = one_hot(row == beyond(lane) + right)
        edge_shift[at, :, :LANES] = one_hot(from_edge == short + right)
        edge_shift[at, :, LANES:] = one_hot(from_edge == beyond(short) + right)
        return carry

    lax.fori_loop(0, 2 * REACH + 1, make_shift, 0)
    for odd in range(2):
        for m in range(maps):
            begin = WINDOW * odd + 2 * WINDOW * m
            inside = (row >= begin) & (row < begin + MARGIN)
            unplace[odd, m, :tile] = one_hot(inside & (lane == row - begin))
            unplace[odd, m, tile:] = one_hot(inside & (lane == row - begin + tile - MARGIN))

    row_q[...] = exponents(iota(row_q.shape, 1) - iota(row_q.shape, 0) + HEAD)
    at = iota(edge_q.shape, 0)
    at = jnp.where(at < PACK, at, at + tile - 2 * PACK)
    edge_q[...] = exponents(at - edge_column(iota(edge_q.shape, 1)))

    first = member * epochs
    at_epoch = iota(motion.shape[1:], 1)
    moved = jnp.zeros(motion.shape[1:], jnp.int32)
    for way in range(2):
        start = jnp.where(at_epoch == first, motion[way], 0)
        moved += jnp.abs(motion[way] - jnp.sum(start, axis=1, keepdims=True))
    held_here = (at_epoch >= first) & (at_epoch < first + epochs)
    counted = jnp.zeros(ends_made.shape, jnp.int32)
    at_run = iota(ends_made.shape, 1)
    low = jnp.zeros((VELS, 1), jnp.int32)
    for run in range(runs):
        high = jnp.full((VELS, 1), epochs, jnp.int32)
        if run < runs - 1:
            high = jnp.sum((held_here & (moved <= run)).astype(jnp.int32), axis=1, keepdims=True)
        begins = at_epoch == first + jnp.minimum(low, epochs - 1)
        down = jnp.sum(jnp.where(begins, motion[0], 0), axis=1, keepdims=True) + HEAD
        right = jnp.sum(jnp.where(begins, motion[1], 0), axis=1, keepdims=True) + REACH
        entries = (
            maps * rows_out * high + down, maps * rows_out * low + down,
            rows_out * high + down, rows_out * low + down, right,
        )
        for which, entry in enumerate(entries):
            counted = jnp.where(at_run == EDGE * which + run, entry, counted)
        low = high
    ends_made[...] = counted
    ends_copy = pltpu.make_async_copy(ends_made, ends, ends_sem)
    ends_copy.start()
    plane[: maps * rows_out] = jnp.zeros((maps * rows_out, LANES), jnp.float32)
    edge[:rows_out] = jnp.zeros((rows_out, LANES), jnp.float32)

    @pl.when(column == 0)
    def _():
        recv_z[1] = jnp.zeros_like(recv_z[1])
        passed[1] = jnp.zeros_like(passed[1])

    @pl.when(column == GRID_X - 1)
    def _():
        recv_z[0] = jnp.zeros_like(recv_z[0])
        passed[0] = jnp.zeros_like(passed[0])

    def make_bands(e):
        sigma = jnp.full((8, LANES), sigmas[e], jnp.float32)
        power = 1.0 / (sigma * sigma)
        tap = iota((8, LANES), 1) - PSFR
        norm = jnp.sum(jnp.exp(exponents(tap) * power), axis=1, keepdims=True)
        scale = (1.0 / norm)[:1]
        power = power[:1, :1]
        for q, bands in ((row_q, row_bands), (edge_q, edge_bands)):
            profile = jnp.exp(q[...] * power) * scale
            bands[e, 0] = profile.astype(jnp.bfloat16)
            bands[e, 1] = (profile * profile).astype(jnp.bfloat16)

    def all_bands(c, carry):
        for turn in range(chunk):
            make_bands(chunk * c + turn)
        return carry

    lax.fori_loop(0, epochs // chunk, all_bands, 0)

    def across(e):
        usable = valid[e].astype(jnp.float32)
        inverse = usable / variance[e].astype(jnp.float32)
        scaled = image[e].astype(jnp.float32) * inverse
        blank = jnp.zeros((tile - 2 * PACK, LANES), jnp.bfloat16)
        for m, field in enumerate((scaled, inverse)):
            rims = jnp.concatenate([edge_bands[e, m, :PACK], blank, edge_bands[e, m, PACK:]], axis=0)
            bands = jnp.concatenate([row_bands[e, m, HEAD : HEAD + tile], rims], axis=1)
            done = jnp.dot(field.astype(jnp.bfloat16), bands, preferred_element_type=jnp.float32)
            columns[e, m] = done.astype(jnp.bfloat16)

    own_half = iota((rows_out, LANES), 1) < LANES // 2

    def down(e):
        rims = []
        for m in range(maps):
            done = jnp.dot(row_bands[e, m], columns[e, m], preferred_element_type=jnp.float32)
            begin = pl.multiple_of((maps * e + m) * rows_out, 8)
            ends_at = pl.multiple_of((maps * e + m + maps) * rows_out, 8)
            plane[pl.ds(ends_at, rows_out)] = plane[pl.ds(begin, rows_out)] + done[:, :LANES]
            rims.append(done[:, LANES:])
        begin = pl.multiple_of(e * rows_out, 8)
        ends_at = pl.multiple_of((e + 1) * rows_out, 8)
        edge[pl.ds(ends_at, rows_out)] = edge[pl.ds(begin, rows_out)] + jnp.where(own_half, rims[0], rims[1])

    def all_across(c, carry):
        for which in range(2):
            load(which, c).wait()
        for turn in range(chunk):
            across(chunk * c + turn)
        return carry

    lax.fori_loop(0, epochs // chunk, all_across, 0)

    def all_down(c, carry):
        for turn in range(STEP):
            down(STEP * c + turn)
        return carry

    lax.fori_loop(0, epochs // STEP, all_down, 0)

    def vel_copy(at):
        return pltpu.make_async_remote_copy(
            src_ref=send_v.at[at], dst_ref=recv_v.at[at], send_sem=sv.at[at], recv_sem=rv.at[at],
            device_id={"vel": partner}, device_id_type=mesh_id,
        )

    def epoch_copy(at):
        return pltpu.make_async_remote_copy(
            src_ref=send_x.at[at], dst_ref=recv_x.at[at], send_sem=sx.at[at], recv_sem=rx.at[at],
            device_id={"epoch": peer}, device_id_type=mesh_id,
        )

    def side_copy(to_after, at):
        return pltpu.make_async_remote_copy(
            src_ref=send_z.at[to_after, at], dst_ref=recv_z.at[to_after, at],
            send_sem=sz.at[to_after, at], recv_sem=rz.at[to_after, at],
            device_id={"sky": after if to_after else before}, device_id_type=mesh_id,
        )

    pairs = block // 2

    def pass_copy(to_after, at):
        return pltpu.make_async_remote_copy(
            src_ref=recv_z.at[to_after, pairs + at], dst_ref=passed.at[to_after, at],
            send_sem=sp.at[to_after, at], recv_sem=rp.at[to_after, at],
            device_id={"epoch": peer}, device_id_type=mesh_id,
        )

    each = LANES // (maps * EDGE)
    part = (lane // EDGE) & (each - 1)
    low_half = lane < LANES // 2
    first_window = (lane & WINDOW) == 0

    def stacked(k):
        summed = jnp.zeros((maps * tile, 2 * LANES), jnp.float32)
        rims = [jnp.zeros((tile, LANES), jnp.float32) for _ in range(2)]
        lefts, rights, rim_rights = [], [], []
        for run in range(runs):
            high, low, rim_high, rim_low, right = (ends[k, EDGE * which + run] for which in range(5))
            rim = edge[pl.ds(rim_high, tile), :]
            if run > 0:
                rim = rim - edge[pl.ds(rim_low, tile), :]
            rims[run // each] = jnp.where(part == run % each, rim, rims[run // each])
            pieces = []
            for m in range(maps):
                piece = plane[pl.ds(high + m * rows_out, tile), :]
                if run > 0:
                    piece = piece - plane[pl.ds(low + m * rows_out, tile), :]
                pieces.append(piece.astype(jnp.bfloat16))
            lefts.append(jnp.concatenate(pieces, axis=0))
            rights.append(shift[right])
            rim_rights.append(edge_shift[right])
        turned = [pltpu.roll(rim, LANES // 2, axis=1) for rim in rims]
        spread = (jnp.where(low_half, rims[0], turned[1]), jnp.where(low_half, turned[0], rims[1]))
        lefts.append(jnp.concatenate([rim.astype(jnp.bfloat16) for rim in spread], axis=0))
        spare = jnp.zeros((LANES - EDGE * runs, 2 * LANES), jnp.bfloat16)
        rights.append(jnp.concatenate(rim_rights + [spare], axis=0))
        for run in range(0, len(lefts), 2):
            summed += jnp.dot(
                jnp.concatenate(lefts[run : run + 2], axis=1), jnp.concatenate(rights[run : run + 2], axis=0),
                preferred_element_type=jnp.float32,
            )
        outer = summed[:tile, LANES:] + pltpu.roll(summed[tile:, LANES:], 2 * WINDOW, axis=1)
        return summed[:tile, :LANES], summed[tile:, :LANES], outer

    def spot_of(turn):
        return (blocks - 1 - turn // block) * block + lax.rem(turn, block)

    def owner_of(turn):
        return lax.rem(group + spot_of(turn) // block, blocks) * 2

    def theirs(turn):
        return stacked((owner_of(turn) + partner) * block + lax.rem(turn, block))

    def ours(turn):
        return stacked((owner_of(turn) + member) * block + lax.rem(turn, block))

    def hand_over(turn, parts):
        spot = spot_of(turn)
        for m in range(maps + 1):
            send_v[spot, m] = parts[m].astype(jnp.bfloat16)
        vel_copy(spot).start()

    def finish(turn, parts):
        spot = spot_of(turn)
        j = lax.rem(turn, block)
        vel_copy(spot).wait_recv()
        totals = [parts[m] + recv_v[spot, m].astype(jnp.float32) for m in range(maps + 1)]
        strip[spot] = totals[maps]

        @pl.when(spot >= block)
        def _():
            for m in range(maps):
                send_x[j, m] = totals[m].astype(jnp.bfloat16)
            epoch_copy(j).start()

        @pl.when(spot < block)
        def _():
            for m in range(maps):
                keep[j, m] = totals[m]

        @pl.when(lax.rem(j, 2) == 1)
        def _():
            even, odd = strip[spot - 1], strip[spot]
            at = spot // 2
            send_z[0, at] = jnp.where(first_window, even, pltpu.roll(odd, WINDOW, axis=1)).astype(jnp.bfloat16)
            send_z[1, at] = jnp.where(first_window, pltpu.roll(even, LANES - WINDOW, axis=1), odd).astype(jnp.bfloat16)

            @pl.when(has_before)
            def _():
                side_copy(0, at).start()

            @pl.when(has_after)
            def _():
                side_copy(1, at).start()

    last = blocks * block - 1

    def stack(turn, carry):
        ahead = theirs(turn + 1)
        kept = ours(turn)
        hand_over(turn + 1, ahead)
        finish(turn, kept)
        return carry

    ends_copy.wait()
    ahead = theirs(0)
    pl.semaphore_wait(barrier, greeted)
    hand_over(0, ahead)
    lax.fori_loop(0, last, stack, 0)
    finish(last, ours(last))

    for at in range(pairs):
        @pl.when(has_before)
        def _():
            side_copy(1, pairs + at).wait_recv()
            pass_copy(1, at).start()

        @pl.when(has_after)
        def _():
            side_copy(0, pairs + at).wait_recv()
            pass_copy(0, at).start()

    for at in range(pairs):
        @pl.when(has_before)
        def _():
            side_copy(1, at).wait_recv()
            pass_copy(1, at).wait_recv()

        @pl.when(has_after)
        def _():
            side_copy(0, at).wait_recv()
            pass_copy(0, at).wait_recv()

        for odd in range(2):
            j = 2 * at + odd
            epoch_copy(j).wait_recv()
            strips_in = jnp.concatenate([recv_z[1, at], recv_z[0, at], passed[1, at], passed[0, at]], axis=1)
            for m, out in enumerate((psi_out, phi_out)):
                added = jnp.dot(
                    strips_in, jnp.concatenate([unplace[odd, m]] * 2, axis=0), preferred_element_type=jnp.float32
                )
                out[j] = keep[j, m] + recv_x[j, m].astype(jnp.float32) + added

    def drain_v(at, carry):
        vel_copy(at).wait_send()
        return carry

    lax.fori_loop(0, blocks * block, drain_v, 0)

    def drain_x(at, carry):
        epoch_copy(at).wait_send()
        return carry

    lax.fori_loop(0, block, drain_x, 0)

    for to_after, there, back in ((0, has_before, has_after), (1, has_after, has_before)):
        @pl.when(there)
        def _():
            for at in range(blocks * pairs):
                side_copy(to_after, at).wait_send()

        @pl.when(back)
        def _():
            for at in range(pairs):
                pass_copy(to_after, at).wait_send()


def near_stacks(images, variances, valid, psf_sigma, offsets, plan):
    tile, sky, blocks, block, epochs, runs, chunk = plan
    rows_out = tile + 2 * HEAD
    smem = pl.BlockSpec(memory_space=pltpu.SMEM)
    vmem = pl.BlockSpec(memory_space=pltpu.VMEM)
    anywhere = pl.BlockSpec(memory_space=pl.ANY)
    dma = pltpu.SemaphoreType.DMA
    half = blocks * block
    pairs = block // 2
    narrow, wide = jnp.bfloat16, jnp.float32
    scratch = [
        pltpu.VMEM((2 * (epochs + 1) * rows_out, LANES), wide),
        pltpu.VMEM(((epochs + 1) * rows_out, LANES), wide),
        pltpu.SMEM((VELS, LANES), jnp.int32),
        pltpu.VMEM((VELS, LANES), jnp.int32),
        dma(()),
        pltpu.VMEM((epochs, tile, tile), narrow),
        pltpu.VMEM((epochs, tile, tile), narrow),
        dma((2, epochs // chunk)),
        pltpu.VMEM((2 * REACH + 1, tile, 2 * LANES), narrow),
        pltpu.VMEM((2 * REACH + 1, EDGE, 2 * LANES), narrow),
        pltpu.VMEM((2, 2, 2 * tile, LANES), narrow),
        pltpu.VMEM((rows_out, tile), wide),
        pltpu.VMEM((2 * PACK, LANES), wide),
        pltpu.VMEM((epochs, 2, rows_out, tile), narrow),
        pltpu.VMEM((epochs, 2, 2 * PACK, LANES), narrow),
        pltpu.VMEM((epochs, 2, tile, 2 * LANES), narrow),
        pltpu.VMEM((half, 3, tile, tile), narrow),
        pltpu.VMEM((half, 3, tile, tile), narrow),
        pltpu.VMEM((block, 2, tile, tile), narrow),
        pltpu.VMEM((block, 2, tile, tile), narrow),
        pltpu.VMEM((block, 2, tile, tile), wide),
        pltpu.VMEM((half, tile, LANES), wide),
        pltpu.VMEM((2, half // 2, tile, LANES), narrow),
        pltpu.VMEM((2, half // 2, tile, LANES), narrow),
        pltpu.VMEM((2, pairs, tile, LANES), narrow),
        dma((half,)), dma((half,)), dma((block,)), dma((block,)),
        dma((2, half // 2)), dma((2, half // 2)), dma((2, pairs)), dma((2, pairs)),
    ]
    out = jax.ShapeDtypeStruct((block, tile, tile), jnp.float32)
    return pl.pallas_call(
        functools.partial(near_kernel, plan),
        out_shape=(out, out),
        in_specs=[smem, vmem, smem, smem, anywhere, anywhere],
        out_specs=(vmem, vmem),
        scratch_shapes=scratch,
        compiler_params=pltpu.CompilerParams(
            collective_id=0, has_side_effects=True, vmem_limit_bytes=KEPT
        ),
    )(offsets, offsets, psf_sigma, valid.reshape(epochs), images, variances)


def far_stacks(images, variances, valid, psf_sigma, offsets, plan):
    tile, sky, blocks, block, epochs, runs = plan
    rows_out = -(-(tile + 2 * REACH) // 16) * 16
    smem = pl.BlockSpec(memory_space=pltpu.SMEM)
    vmem = pl.BlockSpec(memory_space=pltpu.VMEM)
    dma = pltpu.SemaphoreType.DMA
    half = blocks * block
    far = max(1, (blocks - 1) * block)
    scratch = [
        pltpu.VMEM((2 * (epochs + 1), rows_out, LANES), jnp.float32),
        pltpu.VMEM((2 * (epochs + 1), rows_out, LANES), jnp.float32),
        pltpu.SMEM((VELS, LANES), jnp.int32),
        pltpu.VMEM((VELS, LANES), jnp.int32),
        dma(()),
        pltpu.VMEM((rows_out, tile + LANES), jnp.float32),
        pltpu.VMEM((LANES, 2 * LANES), jnp.float32),
        pltpu.VMEM((1, LANES, 2 * LANES), jnp.float32),
        pltpu.VMEM((2, 2, 2 * LANES, 2 * LANES), jnp.bfloat16),
        pltpu.VMEM((half, 2, tile, tile), jnp.bfloat16),
        pltpu.VMEM((half, 2, tile, tile), jnp.bfloat16),
        pltpu.VMEM((far, 2, tile, tile), jnp.bfloat16),
        pltpu.VMEM((far, 2, tile, tile), jnp.bfloat16),
        pltpu.VMEM((2, block, 2, tile, tile), jnp.float32),
        dma((half,)), dma((half,)), dma((far,)), dma((far,)),
    ]
    usable = valid[:, 0].astype(jnp.float32)[:, None, None]
    inverse = usable / variances[:, 0].astype(jnp.float32)
    scaled = images[:, 0].astype(jnp.float32) * inverse
    own = jnp.stack([scaled.astype(jnp.bfloat16), inverse.astype(jnp.bfloat16)], axis=1)
    out = jax.ShapeDtypeStruct((block, tile, tile), jnp.float32)
    return pl.pallas_call(
        functools.partial(fused_kernel, plan),
        out_shape=(out, out),
        in_specs=[smem, vmem, smem, vmem, vmem],
        out_specs=(vmem, vmem),
        scratch_shapes=scratch,
        compiler_params=pltpu.CompilerParams(
            collective_id=0, has_side_effects=True, vmem_limit_bytes=56 * 2**20
        ),
    )(offsets, offsets, psf_sigma, *strips(own, sky, tile))


def on_device(images, variances, valid, psf_sigma, offsets):
    epochs = images.shape[0]
    tile = images.shape[-1]
    sky = lax.axis_size("sky")
    blocks = lax.axis_size("epoch")
    block = VELS // (blocks * lax.axis_size("vel"))
    last_epoch = epochs * blocks * lax.axis_size("vel") - 1
    runs = 1 + 2 * -(-REACH * (epochs - 1) // last_epoch)
    plan = (tile, sky, blocks, block, epochs, runs)
    few = EDGE * runs < LANES and epochs % CHUNK == 0
    if sky == GRID_X and blocks == 2 and lax.axis_size("vel") == 2 and block % 2 == 0 and few:
        plan += (CHUNK,)
        psi_sum, phi_sum = near_stacks(images, variances, valid, psf_sigma, offsets, plan)
    else:
        psi_sum, phi_sum = far_stacks(images, variances, valid, psf_sigma, offsets, plan)
    phi_sum = jnp.maximum(phi_sum, phi_floor)
    likelihood = psi_sum / jnp.sqrt(phi_sum)
    flux = psi_sum / phi_sum
    return (likelihood[:, None], flux[:, None])


def solution(mesh):
    placed = (
        P(("epoch", "vel"), ("field", "sky"), None, None),
        P(("epoch", "vel"), ("field", "sky"), None, None),
        P(("epoch", "vel"), ("field", "sky")),
        P(("field", "epoch", "vel")),
        P(None, None, "epoch"),
    )
    return jax.shard_map(
        on_device,
        mesh=mesh,
        in_specs=placed,
        out_specs=(
            P(("epoch", "vel"), ("field", "sky"), None, None),
            P(("epoch", "vel"), ("field", "sky"), None, None),
        ),
        check_vma=False,
    )
```

```python
import functools

import jax
import jax.numpy as jnp
from jax import lax
from jax.experimental import pallas as pl
from jax.experimental.pallas import tpu as pltpu
from jax.sharding import PartitionSpec as P

VELS = 16
REACH = 12
PSFR = 7
GRID_X = 4
MARGIN = REACH + PSFR
LANES = 128
HEAD = 16
PACK = 16
EDGE = 16
WINDOW = 32
CHUNK = 4
STEP = 4
KEPT = 55705600

phi_floor = 0.25


def shifted(block, axis, distance):
    devices = range(lax.axis_size(axis))
    route = [((i - distance) % len(devices), i) for i in devices]
    return lax.ppermute(block, axis, route)


def positions(index, tile):
    return jnp.where(
        index < tile,
        index,
        jnp.where(
            index < tile + MARGIN,
            index - tile - MARGIN,
            jnp.where(index < tile + 2 * MARGIN, index - MARGIN, 4 * tile),
        ),
    )


FAR = -1.0e9


def exponents(distance):
    away = distance.astype(jnp.float32)
    return jnp.where(jnp.abs(distance) <= PSFR, -0.5 * away * away, FAR)


def fused_kernel(plan, *refs):
    tile, sky, blocks, block, epochs, runs = plan
    (offsets, motion, sigmas, own, halo, psi_out, phi_out, plane_a, plane_b, ends, ends_made, ends_sem, row_q,
     own_q, side_q, bands, send_v, recv_v, send_x, recv_x, keep, sv, rv, sx, rx) = refs
    maps = 2
    rows_in = row_q.shape[1]
    rows_out = plane_a.shape[1]
    width = 2 * LANES
    mesh_id = pl.DeviceIdType.MESH
    group = lax.axis_index("epoch")
    member = lax.axis_index("vel")
    partner = 1 - member

    barrier = pltpu.get_barrier_semaphore()
    greeted = 1
    pl.semaphore_signal(barrier, inc=1, device_id={"vel": partner}, device_id_type=mesh_id)
    for a in range(1, blocks):
        peer = lax.rem(group + a, blocks)
        pl.semaphore_signal(barrier, inc=1, device_id={"epoch": peer}, device_id_type=mesh_id)
        greeted += 1
    pl.semaphore_wait(barrier, greeted)

    shape = (rows_out, rows_in)
    row_q[...] = exponents(
        positions(lax.broadcasted_iota(jnp.int32, shape, 1), tile)
        - lax.broadcasted_iota(jnp.int32, shape, 0) + REACH
    )
    shape = (LANES, width)
    held = lax.broadcasted_iota(jnp.int32, shape, 0)
    shifted_out = lax.broadcasted_iota(jnp.int32, shape, 1) - REACH
    own_q[...] = exponents(held - shifted_out)
    side_q[0] = exponents(positions(held + tile, tile) - shifted_out)

    first = member * epochs

    at_epoch = lax.broadcasted_iota(jnp.int32, motion.shape[1:], 1)
    moved = jnp.zeros(motion.shape[1:], jnp.int32)
    for way in range(2):
        start = jnp.where(at_epoch == first, motion[way], 0)
        moved += jnp.abs(motion[way] - jnp.sum(start, axis=1, keepdims=True))
    held_here = (at_epoch >= first) & (at_epoch < first + epochs)
    counted = jnp.zeros(ends_made.shape, jnp.int32)
    at_run = lax.broadcasted_iota(jnp.int32, ends_made.shape, 1)
    for run in range(runs - 1):
        count = jnp.sum((held_here & (moved <= run)).astype(jnp.int32), axis=1, keepdims=True)
        counted = jnp.where(at_run == run, count, counted)
    ends_made[...] = counted
    ends_copy = pltpu.make_async_copy(ends_made, ends, ends_sem)
    ends_copy.start()
    plane_a[:maps] = jnp.zeros_like(plane_a[:maps])
    plane_b[:maps] = jnp.zeros_like(plane_b[:maps])

    def correlate(e, turn):
        sigma = jnp.full((8, LANES), sigmas[e], jnp.float32)
        power = 1.0 / (sigma * sigma)
        tap = lax.broadcasted_iota(jnp.int32, (8, LANES), 1) - PSFR
        norm = jnp.sum(jnp.exp(exponents(tap) * power), axis=1, keepdims=True)
        scale = (1.0 / norm)[:1]
        power = power[:1, :1]

        def both(q):
            profile = jnp.exp(q * power) * scale
            return profile.astype(jnp.bfloat16), (profile * profile).astype(jnp.bfloat16)

        row_bands = both(row_q[...])
        for part, q in enumerate((own_q[...], side_q[0])):
            for m, made in enumerate(both(q)):
                bands[turn, m, part * LANES : (part + 1) * LANES] = made
        for m in range(maps):
            side = halo[e, m]
            held = jnp.concatenate([own[e, m], side], axis=1)
            rows = jnp.dot(row_bands[m], held, preferred_element_type=jnp.float32)
            done = jnp.dot(
                rows.astype(jnp.bfloat16), bands[turn, m], preferred_element_type=jnp.float32
            )
            at = maps * e + m
            plane_a[at + maps] = plane_a[at] + done[:, :LANES]
            plane_b[at + maps] = plane_b[at] + done[:, LANES:]

    step = 2 if epochs % 2 == 0 else 1

    def several(i, carry):
        for turn in range(step):
            correlate(step * i + turn, turn)
        return carry

    lax.fori_loop(0, epochs // step, several, 0)

    def vel_copy(at):
        return pltpu.make_async_remote_copy(
            src_ref=send_v.at[at], dst_ref=recv_v.at[at], send_sem=sv.at[at], recv_sem=rv.at[at],
            device_id={"vel": partner}, device_id_type=mesh_id,
        )

    def epoch_copy(at):
        peer = lax.rem(group + 1 + at // block, blocks)
        return pltpu.make_async_remote_copy(
            src_ref=send_x.at[at], dst_ref=recv_x.at[at], send_sem=sx.at[at], recv_sem=rx.at[at],
            device_id={"epoch": peer}, device_id_type=mesh_id,
        )

    def stack(slot, carry):
        a = blocks - 1 - slot // (2 * block)
        turn = lax.rem(slot, 2 * block)
        mine = ((turn > 0) & (lax.rem(turn, 2) == 0)) | (turn == 2 * block - 1)
        b = jnp.where(mine, 0, 1)
        j = jnp.where(turn == 2 * block - 1, block - 1, jnp.where(mine, turn // 2 - 1, (turn + 1) // 2))
        place = a * block + j
        k = (lax.rem(group + a, blocks) * 2 + lax.rem(member + b, 2)) * block + j
        lane = lax.broadcasted_iota(jnp.int32, (tile, LANES), 1)
        summed = [jnp.zeros((tile, LANES), jnp.float32) for _ in range(maps)]
        low = jnp.zeros((), jnp.int32)
        for run in range(runs):
            high = ends[k, run] if run < runs - 1 else epochs
            at = first + jnp.minimum(low, epochs - 1)
            down = offsets[0, k, at] + REACH
            right = offsets[1, k, at] + REACH
            rows = pl.ds(down, tile)
            for m in range(maps):
                left_part = plane_a[maps * high + m, rows, :] - plane_a[maps * low + m, rows, :]
                right_part = plane_b[maps * high + m, rows, :] - plane_b[maps * low + m, rows, :]
                merged = jnp.where(lane >= right, left_part, right_part)
                summed[m] += pltpu.roll(merged, LANES - right, axis=1)
            low = high
        for m in range(maps):
            keep[b, j, m] = summed[m]

        @pl.when(b == 1)
        def _():
            send_v[place] = keep[1, j].astype(jnp.bfloat16)
            vel_copy(place).start()

        @pl.when(b == 0)
        def _():
            vel_copy(place).wait_recv()
            keep[0, j] = keep[0, j] + recv_v[place].astype(jnp.float32)

            @pl.when(a > 0)
            def _():
                send_x[place - block] = keep[0, j].astype(jnp.bfloat16)
                epoch_copy(place - block).start()

        return carry

    ends_copy.wait()
    lax.fori_loop(0, 2 * blocks * block, stack, 0)

    def finish(j, carry):
        total = keep[0, j]
        for a in range(1, blocks):
            at = (a - 1) * block + j
            epoch_copy(at).wait_recv()
            total = total + recv_x[at].astype(jnp.float32)
        psi_out[j] = total[0]
        phi_out[j] = total[1]
        return carry

    lax.fori_loop(0, block, finish, 0)

    def drain_v(at, carry):
        vel_copy(at).wait_send()
        return carry

    lax.fori_loop(0, blocks * block, drain_v, 0)

    def drain_x(at, carry):
        epoch_copy(at).wait_send()
        return carry

    lax.fori_loop(0, (blocks - 1) * block, drain_x, 0)


def strips(own, tile_count, tile):
    position = (lax.axis_index("sky") + GRID_X // 2) % tile_count
    column = position % GRID_X
    left = shifted(own[..., tile - MARGIN :], "sky", 1)
    right = shifted(own[..., :MARGIN], "sky", -1)
    left = jnp.where(column > 0, left, jnp.zeros_like(left))
    right = jnp.where(column < GRID_X - 1, right, jnp.zeros_like(right))
    blank = jnp.zeros(own.shape[:3] + (LANES - 2 * MARGIN,), jnp.bfloat16)
    both = jnp.concatenate([own, left, right, blank], axis=3)
    upper = shifted(both[:, :, tile - MARGIN :], "sky", GRID_X)
    lower = shifted(both[:, :, :MARGIN], "sky", -GRID_X)
    upper = jnp.where(position >= GRID_X, upper, jnp.zeros_like(upper))
    lower = jnp.where(position < tile_count - GRID_X, lower, jnp.zeros_like(lower))
    blank = jnp.zeros(both.shape[:2] + (LANES - 2 * MARGIN, both.shape[3]), jnp.bfloat16)
    both = jnp.concatenate([both, upper, lower, blank], axis=2)
    return both[..., :tile], both[..., tile:]


def near_kernel(plan, *refs):
    tile, sky, blocks, block, epochs, runs, chunk = plan
    (motion, sigmas, valid, images, variances, psi_out, phi_out, plane, edge, ends, ends_made, ends_sem,
     image, variance, load_sem, shift, edge_shift, unplace, row_q, edge_q, row_bands, edge_bands, columns,
     send_v, recv_v, send_x, recv_x, keep, send_z, recv_z, passed,
     sv, rv, sx, rx, sz, rz, sp, rp) = refs
    maps = 2
    rows_out = row_q.shape[0]
    mesh_id = pl.DeviceIdType.MESH
    me = lax.axis_index("sky")
    group = lax.axis_index("epoch")
    member = lax.axis_index("vel")
    column = lax.rem(lax.rem(me + GRID_X // 2, sky), GRID_X)
    before = lax.rem(me + sky - 1, sky)
    after = lax.rem(me + 1, sky)
    partner = 1 - member
    peer = 1 - group
    has_before = column > 0
    has_after = column < GRID_X - 1

    barrier = pltpu.get_barrier_semaphore()
    pl.semaphore_signal(barrier, inc=1, device_id={"vel": partner}, device_id_type=mesh_id)
    pl.semaphore_signal(barrier, inc=1, device_id={"epoch": peer}, device_id_type=mesh_id)

    @pl.when(has_before)
    def _():
        pl.semaphore_signal(barrier, inc=1, device_id={"sky": before}, device_id_type=mesh_id)

    @pl.when(has_after)
    def _():
        pl.semaphore_signal(barrier, inc=1, device_id={"sky": after}, device_id_type=mesh_id)

    greeted = 2 + jnp.where(has_before, 1, 0) + jnp.where(has_after, 1, 0)

    def load(which, c):
        source, held = ((images, image), (variances, variance))[which]
        span = pl.ds(c * chunk, chunk)
        return pltpu.make_async_copy(source.at[span, 0], held.at[span], load_sem.at[which, c])

    for c in range(epochs // chunk):
        for which in range(2):
            load(which, c).start()

    def iota(shape, axis):
        return lax.broadcasted_iota(jnp.int32, shape, axis)

    def one_hot(hit):
        return jnp.where(hit, 1.0, 0.0).astype(jnp.bfloat16)

    lane = iota((tile, LANES), 1)
    row = iota((tile, LANES), 0)

    def beyond(lanes):
        outward = lanes & (WINDOW - 1)
        side = jnp.where(lanes < 2 * WINDOW, outward - MARGIN, outward + tile)
        return jnp.where(outward < MARGIN, side, 8 * tile)

    def edge_column(lanes):
        index = (lanes & (EDGE - 1)) - EDGE // 2
        held = (index >= -PSFR) & (index < PSFR)
        return jnp.where(held, jnp.where(index < 0, index, index + tile), 4 * tile)

    short = iota((EDGE, LANES), 1)
    from_edge = edge_column(iota((EDGE, LANES), 0))

    def make_shift(at, carry):
        right = at - REACH
        shift[at, :, :LANES] = one_hot(row == lane + right)
        shift[at, :, LANES:] = one_hot(row == beyond(lane) + right)
        edge_shift[at, :, :LANES] = one_hot(from_edge == short + right)
        edge_shift[at, :, LANES:] = one_hot(from_edge == beyond(short) + right)
        return carry

    lax.fori_loop(0, 2 * REACH + 1, make_shift, 0)
    for m in range(maps):
        for bottom in range(2):
            begin = WINDOW * m + 2 * WINDOW * bottom
            inside = (row >= begin) & (row < begin + MARGIN)
            span = slice(bottom * LANES, (bottom + 1) * LANES)
            unplace[m, :tile, span] = one_hot(inside & (lane == row - begin))
            unplace[m, tile:, span] = one_hot(inside & (lane == row - begin + tile - MARGIN))

    row_q[...] = exponents(iota(row_q.shape, 1) - iota(row_q.shape, 0) + HEAD)
    at = iota(edge_q.shape, 0)
    at = jnp.where(at < PACK, at, at + tile - 2 * PACK)
    edge_q[...] = exponents(at - edge_column(iota(edge_q.shape, 1)))

    first = member * epochs
    at_epoch = iota(motion.shape[1:], 1)
    moved = jnp.zeros(motion.shape[1:], jnp.int32)
    for way in range(2):
        start = jnp.where(at_epoch == first, motion[way], 0)
        moved += jnp.abs(motion[way] - jnp.sum(start, axis=1, keepdims=True))
    held_here = (at_epoch >= first) & (at_epoch < first + epochs)
    counted = jnp.zeros(ends_made.shape, jnp.int32)
    at_run = iota(ends_made.shape, 1)
    low = jnp.zeros((VELS, 1), jnp.int32)
    for run in range(runs):
        high = jnp.full((VELS, 1), epochs, jnp.int32)
        if run < runs - 1:
            high = jnp.sum((held_here & (moved <= run)).astype(jnp.int32), axis=1, keepdims=True)
        begins = at_epoch == first + jnp.minimum(low, epochs - 1)
        down = jnp.sum(jnp.where(begins, motion[0], 0), axis=1, keepdims=True) + HEAD
        right = jnp.sum(jnp.where(begins, motion[1], 0), axis=1, keepdims=True) + REACH
        entries = (
            maps * rows_out * high + down, maps * rows_out * low + down,
            rows_out * high + down, rows_out * low + down, right,
        )
        for which, entry in enumerate(entries):
            counted = jnp.where(at_run == EDGE * which + run, entry, counted)
        low = high
    ends_made[...] = counted
    ends_copy = pltpu.make_async_copy(ends_made, ends, ends_sem)
    ends_copy.start()
    plane[: maps * rows_out] = jnp.zeros((maps * rows_out, LANES), jnp.float32)
    edge[:rows_out] = jnp.zeros((rows_out, LANES), jnp.float32)

    @pl.when(column == 0)
    def _():
        recv_z[1] = jnp.zeros_like(recv_z[1])
        passed[1] = jnp.zeros_like(passed[1])

    @pl.when(column == GRID_X - 1)
    def _():
        recv_z[0] = jnp.zeros_like(recv_z[0])
        passed[0] = jnp.zeros_like(passed[0])

    def make_bands(e):
        sigma = jnp.full((8, LANES), sigmas[e], jnp.float32)
        power = 1.0 / (sigma * sigma)
        tap = iota((8, LANES), 1) - PSFR
        norm = jnp.sum(jnp.exp(exponents(tap) * power), axis=1, keepdims=True)
        scale = (1.0 / norm)[:1]
        power = power[:1, :1]
        for q, bands in ((row_q, row_bands), (edge_q, edge_bands)):
            profile = jnp.exp(q[...] * power) * scale
            bands[e, 0] = profile.astype(jnp.bfloat16)
            bands[e, 1] = (profile * profile).astype(jnp.bfloat16)

    def all_bands(c, carry):
        for turn in range(chunk):
            make_bands(chunk * c + turn)
        return carry

    lax.fori_loop(0, epochs // chunk, all_bands, 0)

    def across(e):
        usable = valid[e].astype(jnp.float32)
        inverse = usable / variance[e].astype(jnp.float32)
        scaled = image[e].astype(jnp.float32) * inverse
        blank = jnp.zeros((tile - 2 * PACK, LANES), jnp.bfloat16)
        for m, field in enumerate((scaled, inverse)):
            rims = jnp.concatenate([edge_bands[e, m, :PACK], blank, edge_bands[e, m, PACK:]], axis=0)
            bands = jnp.concatenate([row_bands[e, m, HEAD : HEAD + tile], rims], axis=1)
            done = jnp.dot(field.astype(jnp.bfloat16), bands, preferred_element_type=jnp.float32)
            columns[e, m] = done.astype(jnp.bfloat16)

    own_half = iota((rows_out, LANES), 1) < LANES // 2

    def down(e):
        rims = []
        for m in range(maps):
            done = jnp.dot(row_bands[e, m], columns[e, m], preferred_element_type=jnp.float32)
            begin = pl.multiple_of((maps * e + m) * rows_out, 8)
            ends_at = pl.multiple_of((maps * e + m + maps) * rows_out, 8)
            plane[pl.ds(ends_at, rows_out)] = plane[pl.ds(begin, rows_out)] + done[:, :LANES]
            rims.append(done[:, LANES:])
        begin = pl.multiple_of(e * rows_out, 8)
        ends_at = pl.multiple_of((e + 1) * rows_out, 8)
        edge[pl.ds(ends_at, rows_out)] = edge[pl.ds(begin, rows_out)] + jnp.where(own_half, rims[0], rims[1])

    def all_across(c, carry):
        for which in range(2):
            load(which, c).wait()
        for turn in range(chunk):
            across(chunk * c + turn)
        return carry

    lax.fori_loop(0, epochs // chunk, all_across, 0)

    def all_down(c, carry):
        for turn in range(STEP):
            down(STEP * c + turn)
        return carry

    lax.fori_loop(0, epochs // STEP, all_down, 0)

    def vel_copy(at):
        return pltpu.make_async_remote_copy(
            src_ref=send_v.at[at], dst_ref=recv_v.at[at], send_sem=sv.at[at], recv_sem=rv.at[at],
            device_id={"vel": partner}, device_id_type=mesh_id,
        )

    def epoch_copy(at):
        return pltpu.make_async_remote_copy(
            src_ref=send_x.at[at], dst_ref=recv_x.at[at], send_sem=sx.at[at], recv_sem=rx.at[at],
            device_id={"epoch": peer}, device_id_type=mesh_id,
        )

    def side_copy(to_after, at):
        return pltpu.make_async_remote_copy(
            src_ref=send_z.at[to_after, at], dst_ref=recv_z.at[to_after, at],
            send_sem=sz.at[to_after, at], recv_sem=rz.at[to_after, at],
            device_id={"sky": after if to_after else before}, device_id_type=mesh_id,
        )

    def pass_copy(to_after, at):
        return pltpu.make_async_remote_copy(
            src_ref=recv_z.at[to_after, block + at], dst_ref=passed.at[to_after, at],
            send_sem=sp.at[to_after, at], recv_sem=rp.at[to_after, at],
            device_id={"epoch": peer}, device_id_type=mesh_id,
        )

    each = LANES // (maps * EDGE)
    part = (lane // EDGE) & (each - 1)
    low_half = lane < LANES // 2
    first_window = (lane & WINDOW) == 0

    def stacked(k):
        summed = jnp.zeros((maps * tile, 2 * LANES), jnp.float32)
        rims = [jnp.zeros((tile, LANES), jnp.float32) for _ in range(2)]
        lefts, rights, rim_rights = [], [], []
        for run in range(runs):
            high, low, rim_high, rim_low, right = (ends[k, EDGE * which + run] for which in range(5))
            rim = edge[pl.ds(rim_high, tile), :]
            if run > 0:
                rim = rim - edge[pl.ds(rim_low, tile), :]
            rims[run // each] = jnp.where(part == run % each, rim, rims[run // each])
            pieces = []
            for m in range(maps):
                piece = plane[pl.ds(high + m * rows_out, tile), :]
                if run > 0:
                    piece = piece - plane[pl.ds(low + m * rows_out, tile), :]
                pieces.append(piece.astype(jnp.bfloat16))
            lefts.append(jnp.concatenate(pieces, axis=0))
            rights.append(shift[right])
            rim_rights.append(edge_shift[right])
        turned = [pltpu.roll(rim, LANES // 2, axis=1) for rim in rims]
        spread = (jnp.where(low_half, rims[0], turned[1]), jnp.where(low_half, turned[0], rims[1]))
        lefts.append(jnp.concatenate([rim.astype(jnp.bfloat16) for rim in spread], axis=0))
        spare = jnp.zeros((LANES - EDGE * runs, 2 * LANES), jnp.bfloat16)
        rights.append(jnp.concatenate(rim_rights + [spare], axis=0))
        for run in range(0, len(lefts), 2):
            summed += jnp.dot(
                jnp.concatenate(lefts[run : run + 2], axis=1), jnp.concatenate(rights[run : run + 2], axis=0),
                preferred_element_type=jnp.float32,
            )
        outer = jnp.where(first_window, summed[:tile, LANES:], summed[tile:, LANES:])
        return summed[:tile, :LANES], summed[tile:, :LANES], outer

    def spot_of(turn):
        return (blocks - 1 - turn // block) * block + lax.rem(turn, block)

    def owner_of(turn):
        return lax.rem(group + spot_of(turn) // block, blocks) * 2

    def theirs(turn):
        return stacked((owner_of(turn) + partner) * block + lax.rem(turn, block))

    def ours(turn):
        return stacked((owner_of(turn) + member) * block + lax.rem(turn, block))

    def hand_over(turn, parts):
        spot = spot_of(turn)
        for m in range(maps + 1):
            send_v[spot, m] = parts[m].astype(jnp.bfloat16)
        vel_copy(spot).start()

    def finish(turn, parts):
        spot = spot_of(turn)
        j = lax.rem(turn, block)
        vel_copy(spot).wait_recv()
        totals = [parts[m] + recv_v[spot, m].astype(jnp.float32) for m in range(maps + 1)]
        upper, lower = totals[maps][: tile // 2], totals[maps][tile // 2 :]
        to_left = low_half[: tile // 2]
        send_z[0, spot] = jnp.where(to_left, upper, pltpu.roll(lower, LANES // 2, axis=1)).astype(jnp.bfloat16)
        send_z[1, spot] = jnp.where(to_left, pltpu.roll(upper, LANES // 2, axis=1), lower).astype(jnp.bfloat16)

        @pl.when(has_before)
        def _():
            side_copy(0, spot).start()

        @pl.when(has_after)
        def _():
            side_copy(1, spot).start()

        @pl.when(spot >= block)
        def _():
            for m in range(maps):
                send_x[j, m] = totals[m].astype(jnp.bfloat16)
            epoch_copy(j).start()

        @pl.when(spot < block)
        def _():
            for m in range(maps):
                keep[j, m] = totals[m]

    last = blocks * block - 1

    def stack(turn, carry):
        ahead = theirs(turn + 1)
        kept = ours(turn)
        hand_over(turn + 1, ahead)
        finish(turn, kept)
        return carry

    ends_copy.wait()
    ahead = theirs(0)
    pl.semaphore_wait(barrier, greeted)
    hand_over(0, ahead)
    lax.fori_loop(0, last, stack, 0)
    finish(last, ours(last))

    def hand_on(at, carry):
        @pl.when(has_before)
        def _():
            side_copy(1, block + at).wait_recv()
            pass_copy(1, at).start()

        @pl.when(has_after)
        def _():
            side_copy(0, block + at).wait_recv()
            pass_copy(0, at).start()

        return carry

    lax.fori_loop(0, block, hand_on, 0)

    def assemble(j, carry):
        epoch_copy(j).wait_recv()

        @pl.when(has_before)
        def _():
            pass_copy(1, j).wait_recv()
            side_copy(1, j).wait_recv()

        @pl.when(has_after)
        def _():
            pass_copy(0, j).wait_recv()
            side_copy(0, j).wait_recv()

        strips_in = jnp.concatenate([recv_z[1, j], recv_z[0, j], passed[1, j], passed[0, j]], axis=1)
        for m, out in enumerate((psi_out, phi_out)):
            added = jnp.dot(
                strips_in, jnp.concatenate([unplace[m]] * 2, axis=0), preferred_element_type=jnp.float32
            )
            for bottom in range(2):
                span = slice(bottom * tile // 2, (bottom + 1) * tile // 2)
                out[j, span] = (
                    keep[j, m, span] + recv_x[j, m, span].astype(jnp.float32)
                    + added[:, bottom * LANES : (bottom + 1) * LANES]
                )
        return carry

    lax.fori_loop(0, block, assemble, 0)

    def drain_v(at, carry):
        vel_copy(at).wait_send()
        return carry

    lax.fori_loop(0, blocks * block, drain_v, 0)

    def drain_x(at, carry):
        epoch_copy(at).wait_send()
        return carry

    lax.fori_loop(0, block, drain_x, 0)

    def drain_z(at, carry):
        @pl.when(has_before)
        def _():
            side_copy(0, at).wait_send()

        @pl.when(has_after)
        def _():
            side_copy(1, at).wait_send()

        return carry

    lax.fori_loop(0, blocks * block, drain_z, 0)

    def drain_passed(at, carry):
        @pl.when(has_before)
        def _():
            pass_copy(1, at).wait_send()

        @pl.when(has_after)
        def _():
            pass_copy(0, at).wait_send()

        return carry

    lax.fori_loop(0, block, drain_passed, 0)


def near_stacks(images, variances, valid, psf_sigma, offsets, plan):
    tile, sky, blocks, block, epochs, runs, chunk = plan
    rows_out = tile + 2 * HEAD
    smem = pl.BlockSpec(memory_space=pltpu.SMEM)
    vmem = pl.BlockSpec(memory_space=pltpu.VMEM)
    anywhere = pl.BlockSpec(memory_space=pl.ANY)
    dma = pltpu.SemaphoreType.DMA
    half = blocks * block
    narrow, wide = jnp.bfloat16, jnp.float32
    scratch = [
        pltpu.VMEM((2 * (epochs + 1) * rows_out, LANES), wide),
        pltpu.VMEM(((epochs + 1) * rows_out, LANES), wide),
        pltpu.SMEM((VELS, LANES), jnp.int32),
        pltpu.VMEM((VELS, LANES), jnp.int32),
        dma(()),
        pltpu.VMEM((epochs, tile, tile), narrow),
        pltpu.VMEM((epochs, tile, tile), narrow),
        dma((2, epochs // chunk)),
        pltpu.VMEM((2 * REACH + 1, tile, 2 * LANES), narrow),
        pltpu.VMEM((2 * REACH + 1, EDGE, 2 * LANES), narrow),
        pltpu.VMEM((2, 2 * tile, 2 * LANES), narrow),
        pltpu.VMEM((rows_out, tile), wide),
        pltpu.VMEM((2 * PACK, LANES), wide),
        pltpu.VMEM((epochs, 2, rows_out, tile), narrow),
        pltpu.VMEM((epochs, 2, 2 * PACK, LANES), narrow),
        pltpu.VMEM((epochs, 2, tile, 2 * LANES), narrow),
        pltpu.VMEM((half, 3, tile, tile), narrow),
        pltpu.VMEM((half, 3, tile, tile), narrow),
        pltpu.VMEM((block, 2, tile, tile), narrow),
        pltpu.VMEM((block, 2, tile, tile), narrow),
        pltpu.VMEM((block, 2, tile, tile), wide),
        pltpu.VMEM((2, half, tile // 2, LANES), narrow),
        pltpu.VMEM((2, half, tile // 2, LANES), narrow),
        pltpu.VMEM((2, block, tile // 2, LANES), narrow),
        dma((half,)), dma((half,)), dma((block,)), dma((block,)),
        dma((2, half)), dma((2, half)), dma((2, block)), dma((2, block)),
    ]
    out = jax.ShapeDtypeStruct((block, tile, tile), jnp.float32)
    return pl.pallas_call(
        functools.partial(near_kernel, plan),
        out_shape=(out, out),
        in_specs=[vmem, smem, smem, anywhere, anywhere],
        out_specs=(vmem, vmem),
        scratch_shapes=scratch,
        compiler_params=pltpu.CompilerParams(
            collective_id=0, has_side_effects=True, vmem_limit_bytes=KEPT
        ),
    )(offsets, psf_sigma, valid.reshape(epochs), images, variances)


def far_stacks(images, variances, valid, psf_sigma, offsets, plan):
    tile, sky, blocks, block, epochs, runs = plan
    rows_out = -(-(tile + 2 * REACH) // 16) * 16
    smem = pl.BlockSpec(memory_space=pltpu.SMEM)
    vmem = pl.BlockSpec(memory_space=pltpu.VMEM)
    dma = pltpu.SemaphoreType.DMA
    half = blocks * block
    far = max(1, (blocks - 1) * block)
    scratch = [
        pltpu.VMEM((2 * (epochs + 1), rows_out, LANES), jnp.float32),
        pltpu.VMEM((2 * (epochs + 1), rows_out, LANES), jnp.float32),
        pltpu.SMEM((VELS, LANES), jnp.int32),
        pltpu.VMEM((VELS, LANES), jnp.int32),
        dma(()),
        pltpu.VMEM((rows_out, tile + LANES), jnp.float32),
        pltpu.VMEM((LANES, 2 * LANES), jnp.float32),
        pltpu.VMEM((1, LANES, 2 * LANES), jnp.float32),
        pltpu.VMEM((2, 2, 2 * LANES, 2 * LANES), jnp.bfloat16),
        pltpu.VMEM((half, 2, tile, tile), jnp.bfloat16),
        pltpu.VMEM((half, 2, tile, tile), jnp.bfloat16),
        pltpu.VMEM((far, 2, tile, tile), jnp.bfloat16),
        pltpu.VMEM((far, 2, tile, tile), jnp.bfloat16),
        pltpu.VMEM((2, block, 2, tile, tile), jnp.float32),
        dma((half,)), dma((half,)), dma((far,)), dma((far,)),
    ]
    usable = valid[:, 0].astype(jnp.float32)[:, None, None]
    inverse = usable / variances[:, 0].astype(jnp.float32)
    scaled = images[:, 0].astype(jnp.float32) * inverse
    own = jnp.stack([scaled.astype(jnp.bfloat16), inverse.astype(jnp.bfloat16)], axis=1)
    out = jax.ShapeDtypeStruct((block, tile, tile), jnp.float32)
    return pl.pallas_call(
        functools.partial(fused_kernel, plan),
        out_shape=(out, out),
        in_specs=[smem, vmem, smem, vmem, vmem],
        out_specs=(vmem, vmem),
        scratch_shapes=scratch,
        compiler_params=pltpu.CompilerParams(
            collective_id=0, has_side_effects=True, vmem_limit_bytes=56 * 2**20
        ),
    )(offsets, offsets, psf_sigma, *strips(own, sky, tile))


def on_device(images, variances, valid, psf_sigma, offsets):
    epochs = images.shape[0]
    tile = images.shape[-1]
    sky = lax.axis_size("sky")
    blocks = lax.axis_size("epoch")
    block = VELS // (blocks * lax.axis_size("vel"))
    last_epoch = epochs * blocks * lax.axis_size("vel") - 1
    runs = 1 + 2 * -(-REACH * (epochs - 1) // last_epoch)
    plan = (tile, sky, blocks, block, epochs, runs)
    few = EDGE * runs < LANES and epochs % CHUNK == 0
    if sky == GRID_X and blocks == 2 and lax.axis_size("vel") == 2 and few:
        plan += (CHUNK,)
        psi_sum, phi_sum = near_stacks(images, variances, valid, psf_sigma, offsets, plan)
    else:
        psi_sum, phi_sum = far_stacks(images, variances, valid, psf_sigma, offsets, plan)
    phi_sum = jnp.maximum(phi_sum, phi_floor)
    likelihood = psi_sum / jnp.sqrt(phi_sum)
    flux = psi_sum / phi_sum
    return (likelihood[:, None], flux[:, None])


def solution(mesh):
    placed = (
        P(("epoch", "vel"), ("field", "sky"), None, None),
        P(("epoch", "vel"), ("field", "sky"), None, None),
        P(("epoch", "vel"), ("field", "sky")),
        P(("field", "epoch", "vel")),
        P(None, None, "epoch"),
    )
    return jax.shard_map(
        on_device,
        mesh=mesh,
        in_specs=placed,
        out_specs=(
            P(("epoch", "vel"), ("field", "sky"), None, None),
            P(("epoch", "vel"), ("field", "sky"), None, None),
        ),
        check_vma=False,
    )
```

```python
import functools

import jax
import jax.numpy as jnp
from jax import lax
from jax.experimental import pallas as pl
from jax.experimental.pallas import tpu as pltpu
from jax.sharding import PartitionSpec as P

VELS = 16
REACH = 12
PSFR = 7
GRID_X = 4
MARGIN = REACH + PSFR
LANES = 128
HEAD = 16
PACK = 16
EDGE = 16
WINDOW = 32
CHUNK = 4
KEPT = 55705600

phi_floor = 0.25


def shifted(block, axis, distance):
    devices = range(lax.axis_size(axis))
    route = [((i - distance) % len(devices), i) for i in devices]
    return lax.ppermute(block, axis, route)


def positions(index, tile):
    return jnp.where(
        index < tile,
        index,
        jnp.where(
            index < tile + MARGIN,
            index - tile - MARGIN,
            jnp.where(index < tile + 2 * MARGIN, index - MARGIN, 4 * tile),
        ),
    )


FAR = -1.0e9


def exponents(distance):
    away = distance.astype(jnp.float32)
    return jnp.where(jnp.abs(distance) <= PSFR, -0.5 * away * away, FAR)


def fused_kernel(plan, *refs):
    tile, sky, blocks, block, epochs, runs = plan
    (offsets, motion, sigmas, own, halo, psi_out, phi_out, plane_a, plane_b, ends, ends_made, ends_sem, row_q,
     own_q, side_q, bands, send_v, recv_v, send_x, recv_x, keep, sv, rv, sx, rx) = refs
    maps = 2
    rows_in = row_q.shape[1]
    rows_out = plane_a.shape[1]
    width = 2 * LANES
    mesh_id = pl.DeviceIdType.MESH
    group = lax.axis_index("epoch")
    member = lax.axis_index("vel")
    partner = 1 - member

    barrier = pltpu.get_barrier_semaphore()
    greeted = 1
    pl.semaphore_signal(barrier, inc=1, device_id={"vel": partner}, device_id_type=mesh_id)
    for a in range(1, blocks):
        peer = lax.rem(group + a, blocks)
        pl.semaphore_signal(barrier, inc=1, device_id={"epoch": peer}, device_id_type=mesh_id)
        greeted += 1
    pl.semaphore_wait(barrier, greeted)

    shape = (rows_out, rows_in)
    row_q[...] = exponents(
        positions(lax.broadcasted_iota(jnp.int32, shape, 1), tile)
        - lax.broadcasted_iota(jnp.int32, shape, 0) + REACH
    )
    shape = (LANES, width)
    held = lax.broadcasted_iota(jnp.int32, shape, 0)
    shifted_out = lax.broadcasted_iota(jnp.int32, shape, 1) - REACH
    own_q[...] = exponents(held - shifted_out)
    side_q[0] = exponents(positions(held + tile, tile) - shifted_out)

    first = member * epochs

    at_epoch = lax.broadcasted_iota(jnp.int32, motion.shape[1:], 1)
    moved = jnp.zeros(motion.shape[1:], jnp.int32)
    for way in range(2):
        start = jnp.where(at_epoch == first, motion[way], 0)
        moved += jnp.abs(motion[way] - jnp.sum(start, axis=1, keepdims=True))
    held_here = (at_epoch >= first) & (at_epoch < first + epochs)
    counted = jnp.zeros(ends_made.shape, jnp.int32)
    at_run = lax.broadcasted_iota(jnp.int32, ends_made.shape, 1)
    for run in range(runs - 1):
        count = jnp.sum((held_here & (moved <= run)).astype(jnp.int32), axis=1, keepdims=True)
        counted = jnp.where(at_run == run, count, counted)
    ends_made[...] = counted
    ends_copy = pltpu.make_async_copy(ends_made, ends, ends_sem)
    ends_copy.start()
    plane_a[:maps] = jnp.zeros_like(plane_a[:maps])
    plane_b[:maps] = jnp.zeros_like(plane_b[:maps])

    def correlate(e, turn):
        sigma = jnp.full((8, LANES), sigmas[e], jnp.float32)
        power = 1.0 / (sigma * sigma)
        tap = lax.broadcasted_iota(jnp.int32, (8, LANES), 1) - PSFR
        norm = jnp.sum(jnp.exp(exponents(tap) * power), axis=1, keepdims=True)
        scale = (1.0 / norm)[:1]
        power = power[:1, :1]

        def both(q):
            profile = jnp.exp(q * power) * scale
            return profile.astype(jnp.bfloat16), (profile * profile).astype(jnp.bfloat16)

        row_bands = both(row_q[...])
        for part, q in enumerate((own_q[...], side_q[0])):
            for m, made in enumerate(both(q)):
                bands[turn, m, part * LANES : (part + 1) * LANES] = made
        for m in range(maps):
            side = halo[e, m]
            held = jnp.concatenate([own[e, m], side], axis=1)
            rows = jnp.dot(row_bands[m], held, preferred_element_type=jnp.float32)
            done = jnp.dot(
                rows.astype(jnp.bfloat16), bands[turn, m], preferred_element_type=jnp.float32
            )
            at = maps * e + m
            plane_a[at + maps] = plane_a[at] + done[:, :LANES]
            plane_b[at + maps] = plane_b[at] + done[:, LANES:]

    step = 2 if epochs % 2 == 0 else 1

    def several(i, carry):
        for turn in range(step):
            correlate(step * i + turn, turn)
        return carry

    lax.fori_loop(0, epochs // step, several, 0)

    def vel_copy(at):
        return pltpu.make_async_remote_copy(
            src_ref=send_v.at[at], dst_ref=recv_v.at[at], send_sem=sv.at[at], recv_sem=rv.at[at],
            device_id={"vel": partner}, device_id_type=mesh_id,
        )

    def epoch_copy(at):
        peer = lax.rem(group + 1 + at // block, blocks)
        return pltpu.make_async_remote_copy(
            src_ref=send_x.at[at], dst_ref=recv_x.at[at], send_sem=sx.at[at], recv_sem=rx.at[at],
            device_id={"epoch": peer}, device_id_type=mesh_id,
        )

    def stack(slot, carry):
        a = blocks - 1 - slot // (2 * block)
        turn = lax.rem(slot, 2 * block)
        mine = ((turn > 0) & (lax.rem(turn, 2) == 0)) | (turn == 2 * block - 1)
        b = jnp.where(mine, 0, 1)
        j = jnp.where(turn == 2 * block - 1, block - 1, jnp.where(mine, turn // 2 - 1, (turn + 1) // 2))
        place = a * block + j
        k = (lax.rem(group + a, blocks) * 2 + lax.rem(member + b, 2)) * block + j
        lane = lax.broadcasted_iota(jnp.int32, (tile, LANES), 1)
        summed = [jnp.zeros((tile, LANES), jnp.float32) for _ in range(maps)]
        low = jnp.zeros((), jnp.int32)
        for run in range(runs):
            high = ends[k, run] if run < runs - 1 else epochs
            at = first + jnp.minimum(low, epochs - 1)
            down = offsets[0, k, at] + REACH
            right = offsets[1, k, at] + REACH
            rows = pl.ds(down, tile)
            for m in range(maps):
                left_part = plane_a[maps * high + m, rows, :] - plane_a[maps * low + m, rows, :]
                right_part = plane_b[maps * high + m, rows, :] - plane_b[maps * low + m, rows, :]
                merged = jnp.where(lane >= right, left_part, right_part)
                summed[m] += pltpu.roll(merged, LANES - right, axis=1)
            low = high
        for m in range(maps):
            keep[b, j, m] = summed[m]

        @pl.when(b == 1)
        def _():
            send_v[place] = keep[1, j].astype(jnp.bfloat16)
            vel_copy(place).start()

        @pl.when(b == 0)
        def _():
            vel_copy(place).wait_recv()
            keep[0, j] = keep[0, j] + recv_v[place].astype(jnp.float32)

            @pl.when(a > 0)
            def _():
                send_x[place - block] = keep[0, j].astype(jnp.bfloat16)
                epoch_copy(place - block).start()

        return carry

    ends_copy.wait()
    lax.fori_loop(0, 2 * blocks * block, stack, 0)

    def finish(j, carry):
        total = keep[0, j]
        for a in range(1, blocks):
            at = (a - 1) * block + j
            epoch_copy(at).wait_recv()
            total = total + recv_x[at].astype(jnp.float32)
        psi_out[j] = total[0]
        phi_out[j] = total[1]
        return carry

    lax.fori_loop(0, block, finish, 0)

    def drain_v(at, carry):
        vel_copy(at).wait_send()
        return carry

    lax.fori_loop(0, blocks * block, drain_v, 0)

    def drain_x(at, carry):
        epoch_copy(at).wait_send()
        return carry

    lax.fori_loop(0, (blocks - 1) * block, drain_x, 0)


def strips(own, tile_count, tile):
    position = (lax.axis_index("sky") + GRID_X // 2) % tile_count
    column = position % GRID_X
    left = shifted(own[..., tile - MARGIN :], "sky", 1)
    right = shifted(own[..., :MARGIN], "sky", -1)
    left = jnp.where(column > 0, left, jnp.zeros_like(left))
    right = jnp.where(column < GRID_X - 1, right, jnp.zeros_like(right))
    blank = jnp.zeros(own.shape[:3] + (LANES - 2 * MARGIN,), jnp.bfloat16)
    both = jnp.concatenate([own, left, right, blank], axis=3)
    upper = shifted(both[:, :, tile - MARGIN :], "sky", GRID_X)
    lower = shifted(both[:, :, :MARGIN], "sky", -GRID_X)
    upper = jnp.where(position >= GRID_X, upper, jnp.zeros_like(upper))
    lower = jnp.where(position < tile_count - GRID_X, lower, jnp.zeros_like(lower))
    blank = jnp.zeros(both.shape[:2] + (LANES - 2 * MARGIN, both.shape[3]), jnp.bfloat16)
    both = jnp.concatenate([both, upper, lower, blank], axis=2)
    return both[..., :tile], both[..., tile:]


def near_kernel(plan, *refs):
    tile, sky, blocks, block, epochs, runs, chunk = plan
    (motion, sigmas, valid, images, variances, psi_out, phi_out, plane, edge, ends, ends_made, ends_sem,
     image, variance, load_sem, shift, edge_shift, unplace, row_q, edge_q, row_bands, edge_bands, columns,
     send_v, recv_v, send_x, recv_x, keep, send_z, recv_z, passed,
     sv, rv, sx, rx, sz, rz, sp, rp) = refs
    maps = 2
    rows_out = row_q.shape[0]
    mesh_id = pl.DeviceIdType.MESH
    me = lax.axis_index("sky")
    group = lax.axis_index("epoch")
    member = lax.axis_index("vel")
    column = lax.rem(lax.rem(me + GRID_X // 2, sky), GRID_X)
    before = lax.rem(me + sky - 1, sky)
    after = lax.rem(me + 1, sky)
    partner = 1 - member
    peer = 1 - group
    has_before = column > 0
    has_after = column < GRID_X - 1

    barrier = pltpu.get_barrier_semaphore()
    pl.semaphore_signal(barrier, inc=1, device_id={"vel": partner}, device_id_type=mesh_id)
    pl.semaphore_signal(barrier, inc=1, device_id={"epoch": peer}, device_id_type=mesh_id)

    @pl.when(has_before)
    def _():
        pl.semaphore_signal(barrier, inc=1, device_id={"sky": before}, device_id_type=mesh_id)

    @pl.when(has_after)
    def _():
        pl.semaphore_signal(barrier, inc=1, device_id={"sky": after}, device_id_type=mesh_id)

    greeted = 2 + jnp.where(has_before, 1, 0) + jnp.where(has_after, 1, 0)

    def load(which, c):
        source, held = ((images, image), (variances, variance))[which]
        span = pl.ds(c * chunk, chunk)
        return pltpu.make_async_copy(source.at[span, 0], held.at[span], load_sem.at[which, c])

    for c in range(epochs // chunk):
        for which in range(2):
            load(which, c).start()

    def iota(shape, axis):
        return lax.broadcasted_iota(jnp.int32, shape, axis)

    def one_hot(hit):
        return jnp.where(hit, 1.0, 0.0).astype(jnp.bfloat16)

    lane = iota((tile, LANES), 1)
    row = iota((tile, LANES), 0)

    def beyond(lanes):
        outward = lanes & (WINDOW - 1)
        side = jnp.where(lanes < 2 * WINDOW, outward - MARGIN, outward + tile)
        return jnp.where(outward < MARGIN, side, 8 * tile)

    def edge_column(lanes):
        index = (lanes & (EDGE - 1)) - EDGE // 2
        held = (index >= -PSFR) & (index < PSFR)
        return jnp.where(held, jnp.where(index < 0, index, index + tile), 4 * tile)

    short = iota((EDGE, LANES), 1)
    from_edge = edge_column(iota((EDGE, LANES), 0))

    moves = (row - lane, row - beyond(lane), from_edge - short, from_edge - beyond(short))

    def make_shift(at, carry):
        right = at - REACH
        shift[at, :, :LANES] = one_hot(moves[0] == right)
        shift[at, :, LANES:] = one_hot(moves[1] == right)
        edge_shift[at, :, :LANES] = one_hot(moves[2] == right)
        edge_shift[at, :, LANES:] = one_hot(moves[3] == right)
        return carry

    lax.fori_loop(0, 2 * REACH + 1, make_shift, 0)
    for m in range(maps):
        for bottom in range(2):
            begin = WINDOW * m + 2 * WINDOW * bottom
            inside = (row >= begin) & (row < begin + MARGIN)
            span = slice(bottom * LANES, (bottom + 1) * LANES)
            unplace[m, :tile, span] = one_hot(inside & (lane == row - begin))
            unplace[m, tile:, span] = one_hot(inside & (lane == row - begin + tile - MARGIN))

    row_q[...] = exponents(iota(row_q.shape, 1) - iota(row_q.shape, 0) + HEAD)
    at = iota(edge_q.shape, 0)
    at = jnp.where(at < PACK, at, at + tile - 2 * PACK)
    edge_q[...] = exponents(at - edge_column(iota(edge_q.shape, 1)))

    first = member * epochs
    at_epoch = iota(motion.shape[1:], 1)
    moved = jnp.zeros(motion.shape[1:], jnp.int32)
    for way in range(2):
        start = jnp.where(at_epoch == first, motion[way], 0)
        moved += jnp.abs(motion[way] - jnp.sum(start, axis=1, keepdims=True))
    held_here = (at_epoch >= first) & (at_epoch < first + epochs)
    counted = jnp.zeros(ends_made.shape, jnp.int32)
    at_run = iota(ends_made.shape, 1)
    low = jnp.zeros((VELS, 1), jnp.int32)
    for run in range(runs):
        high = jnp.full((VELS, 1), epochs, jnp.int32)
        if run < runs - 1:
            high = jnp.sum((held_here & (moved <= run)).astype(jnp.int32), axis=1, keepdims=True)
        begins = at_epoch == first + jnp.minimum(low, epochs - 1)
        down = jnp.sum(jnp.where(begins, motion[0], 0), axis=1, keepdims=True) + HEAD
        right = jnp.sum(jnp.where(begins, motion[1], 0), axis=1, keepdims=True) + REACH
        entries = (
            maps * rows_out * high + down, maps * rows_out * low + down,
            rows_out * high + down, rows_out * low + down, right,
        )
        for which, entry in enumerate(entries):
            counted = jnp.where(at_run == EDGE * which + run, entry, counted)
        low = high
    ends_made[...] = counted
    ends_copy = pltpu.make_async_copy(ends_made, ends, ends_sem)
    ends_copy.start()
    plane[: maps * rows_out] = jnp.zeros((maps * rows_out, LANES), jnp.float32)
    edge[:rows_out] = jnp.zeros((rows_out, LANES), jnp.float32)

    @pl.when(column == 0)
    def _():
        recv_z[1] = jnp.zeros_like(recv_z[1])
        passed[1] = jnp.zeros_like(passed[1])

    @pl.when(column == GRID_X - 1)
    def _():
        recv_z[0] = jnp.zeros_like(recv_z[0])
        passed[0] = jnp.zeros_like(passed[0])

    def make_bands(e):
        sigma = jnp.full((8, LANES), sigmas[e], jnp.float32)
        power = 1.0 / (sigma * sigma)
        tap = iota((8, LANES), 1) - PSFR
        norm = jnp.sum(jnp.exp(exponents(tap) * power), axis=1, keepdims=True)
        scale = (1.0 / norm)[:1]
        power = power[:1, :1]
        for q, bands in ((row_q, row_bands), (edge_q, edge_bands)):
            profile = jnp.exp(q[...] * power) * scale
            bands[e, 0] = profile.astype(jnp.bfloat16)
            bands[e, 1] = (profile * profile).astype(jnp.bfloat16)

    def all_bands(c, carry):
        for turn in range(chunk):
            make_bands(chunk * c + turn)
        return carry

    lax.fori_loop(0, epochs // chunk, all_bands, 0)

    def across(e):
        usable = valid[e].astype(jnp.float32)
        inverse = usable / variance[e].astype(jnp.float32)
        scaled = image[e].astype(jnp.float32) * inverse
        blank = jnp.zeros((tile - 2 * PACK, LANES), jnp.bfloat16)
        for m, field in enumerate((scaled, inverse)):
            rims = jnp.concatenate([edge_bands[e, m, :PACK], blank, edge_bands[e, m, PACK:]], axis=0)
            bands = jnp.concatenate([row_bands[e, m, HEAD : HEAD + tile], rims], axis=1)
            done = jnp.dot(field.astype(jnp.bfloat16), bands, preferred_element_type=jnp.float32)
            columns[e, m] = done.astype(jnp.bfloat16)

    own_half = iota((rows_out, LANES), 1) < LANES // 2

    def down(e):
        rims = []
        for m in range(maps):
            done = jnp.dot(row_bands[e, m], columns[e, m], preferred_element_type=jnp.float32)
            begin = pl.multiple_of((maps * e + m) * rows_out, 8)
            ends_at = pl.multiple_of((maps * e + m + maps) * rows_out, 8)
            plane[pl.ds(ends_at, rows_out)] = plane[pl.ds(begin, rows_out)] + done[:, :LANES]
            rims.append(done[:, LANES:])
        begin = pl.multiple_of(e * rows_out, 8)
        ends_at = pl.multiple_of((e + 1) * rows_out, 8)
        edge[pl.ds(ends_at, rows_out)] = edge[pl.ds(begin, rows_out)] + jnp.where(own_half, rims[0], rims[1])

    def arrive(c):
        for which in range(2):
            load(which, c).wait()

    def all_across(c):
        for turn in range(chunk):
            across(chunk * c + turn)

    def all_down(c):
        for turn in range(chunk):
            down(chunk * c + turn)

    def both_ways(c, carry):
        arrive(c)
        all_down(c - 1)
        all_across(c)
        return carry

    chunks = epochs // chunk
    arrive(0)
    all_across(0)
    lax.fori_loop(1, chunks, both_ways, 0)
    all_down(chunks - 1)

    def vel_copy(at):
        return pltpu.make_async_remote_copy(
            src_ref=send_v.at[at], dst_ref=recv_v.at[at], send_sem=sv.at[at], recv_sem=rv.at[at],
            device_id={"vel": partner}, device_id_type=mesh_id,
        )

    def epoch_copy(at):
        return pltpu.make_async_remote_copy(
            src_ref=send_x.at[at], dst_ref=recv_x.at[at], send_sem=sx.at[at], recv_sem=rx.at[at],
            device_id={"epoch": peer}, device_id_type=mesh_id,
        )

    def side_copy(to_after, at):
        return pltpu.make_async_remote_copy(
            src_ref=send_z.at[to_after, at], dst_ref=recv_z.at[to_after, at],
            send_sem=sz.at[to_after, at], recv_sem=rz.at[to_after, at],
            device_id={"sky": after if to_after else before}, device_id_type=mesh_id,
        )

    def pass_copy(to_after, at):
        return pltpu.make_async_remote_copy(
            src_ref=recv_z.at[to_after, block + at], dst_ref=passed.at[to_after, at],
            send_sem=sp.at[to_after, at], recv_sem=rp.at[to_after, at],
            device_id={"epoch": peer}, device_id_type=mesh_id,
        )

    each = LANES // (maps * EDGE)
    part = (lane // EDGE) & (each - 1)
    low_half = lane < LANES // 2
    first_window = (lane & WINDOW) == 0

    def stacked(k):
        summed = jnp.zeros((maps * tile, 2 * LANES), jnp.float32)
        rims = [jnp.zeros((tile, LANES), jnp.float32) for _ in range(2)]
        lefts, rights, rim_rights = [], [], []
        for run in range(runs):
            high, low, rim_high, rim_low, right = (ends[k, EDGE * which + run] for which in range(5))
            rim = edge[pl.ds(rim_high, tile), :]
            if run > 0:
                rim = rim - edge[pl.ds(rim_low, tile), :]
            rims[run // each] = jnp.where(part == run % each, rim, rims[run // each])
            pieces = []
            for m in range(maps):
                piece = plane[pl.ds(high + m * rows_out, tile), :]
                if run > 0:
                    piece = piece - plane[pl.ds(low + m * rows_out, tile), :]
                pieces.append(piece.astype(jnp.bfloat16))
            lefts.append(jnp.concatenate(pieces, axis=0))
            rights.append(shift[right])
            rim_rights.append(edge_shift[right])
        turned = [pltpu.roll(rim, LANES // 2, axis=1) for rim in rims]
        spread = (jnp.where(low_half, rims[0], turned[1]), jnp.where(low_half, turned[0], rims[1]))
        lefts.append(jnp.concatenate([rim.astype(jnp.bfloat16) for rim in spread], axis=0))
        spare = jnp.zeros((LANES - EDGE * runs, 2 * LANES), jnp.bfloat16)
        rights.append(jnp.concatenate(rim_rights + [spare], axis=0))
        for run in range(0, len(lefts), 2):
            summed += jnp.dot(
                jnp.concatenate(lefts[run : run + 2], axis=1), jnp.concatenate(rights[run : run + 2], axis=0),
                preferred_element_type=jnp.float32,
            )
        outer = jnp.where(first_window, summed[:tile, LANES:], summed[tile:, LANES:])
        return summed[:tile, :LANES], summed[tile:, :LANES], outer

    def spot_of(turn):
        return (blocks - 1 - turn // block) * block + lax.rem(turn, block)

    def owner_of(turn):
        return lax.rem(group + spot_of(turn) // block, blocks) * 2

    def theirs(turn):
        return stacked((owner_of(turn) + partner) * block + lax.rem(turn, block))

    def ours(turn):
        return stacked((owner_of(turn) + member) * block + lax.rem(turn, block))

    def hand_over(turn, parts):
        spot = spot_of(turn)
        for m in range(maps + 1):
            send_v[spot, m] = parts[m].astype(jnp.bfloat16)
        vel_copy(spot).start()

    def finish(turn, parts):
        spot = spot_of(turn)
        j = lax.rem(turn, block)
        vel_copy(spot).wait_recv()
        totals = [parts[m] + recv_v[spot, m].astype(jnp.float32) for m in range(maps + 1)]
        upper, lower = totals[maps][: tile // 2], totals[maps][tile // 2 :]
        to_left = low_half[: tile // 2]
        send_z[0, spot] = jnp.where(to_left, upper, pltpu.roll(lower, LANES // 2, axis=1)).astype(jnp.bfloat16)
        send_z[1, spot] = jnp.where(to_left, pltpu.roll(upper, LANES // 2, axis=1), lower).astype(jnp.bfloat16)

        @pl.when(has_before)
        def _():
            side_copy(0, spot).start()

        @pl.when(has_after)
        def _():
            side_copy(1, spot).start()

        @pl.when(spot >= block)
        def _():
            for m in range(maps):
                send_x[j, m] = totals[m].astype(jnp.bfloat16)
            epoch_copy(j).start()

        @pl.when(spot < block)
        def _():
            for m in range(maps):
                keep[j, m] = totals[m]

    last = blocks * block - 1

    def stack(turn, carry):
        ahead = theirs(turn + 1)
        kept = ours(turn)
        hand_over(turn + 1, ahead)
        finish(turn, kept)
        return carry

    ends_copy.wait()
    ahead = theirs(0)
    pl.semaphore_wait(barrier, greeted)
    hand_over(0, ahead)
    lax.fori_loop(0, last, stack, 0)
    finish(last, ours(last))

    def hand_on(at, carry):
        @pl.when(has_before)
        def _():
            side_copy(1, block + at).wait_recv()
            pass_copy(1, at).start()

        @pl.when(has_after)
        def _():
            side_copy(0, block + at).wait_recv()
            pass_copy(0, at).start()

        return carry

    lax.fori_loop(0, block, hand_on, 0)

    def drain_v(at, carry):
        vel_copy(at).wait_send()
        return carry

    lax.fori_loop(0, blocks * block, drain_v, 0)

    def drain_x(at, carry):
        epoch_copy(at).wait_send()
        return carry

    lax.fori_loop(0, block, drain_x, 0)

    def drain_z(at, carry):
        @pl.when(has_before)
        def _():
            side_copy(0, at).wait_send()

        @pl.when(has_after)
        def _():
            side_copy(1, at).wait_send()

        return carry

    lax.fori_loop(0, blocks * block, drain_z, 0)

    def assemble(j, carry):
        epoch_copy(j).wait_recv()

        @pl.when(has_before)
        def _():
            pass_copy(1, j).wait_recv()
            side_copy(1, j).wait_recv()

        @pl.when(has_after)
        def _():
            pass_copy(0, j).wait_recv()
            side_copy(0, j).wait_recv()

        strips_in = jnp.concatenate([recv_z[1, j], recv_z[0, j], passed[1, j], passed[0, j]], axis=1)
        for m, out in enumerate((psi_out, phi_out)):
            added = jnp.dot(
                strips_in, jnp.concatenate([unplace[m]] * 2, axis=0), preferred_element_type=jnp.float32
            )
            for bottom in range(2):
                span = slice(bottom * tile // 2, (bottom + 1) * tile // 2)
                out[j, span] = (
                    keep[j, m, span] + recv_x[j, m, span].astype(jnp.float32)
                    + added[:, bottom * LANES : (bottom + 1) * LANES]
                )
        return carry

    lax.fori_loop(0, block, assemble, 0)

    def drain_passed(at, carry):
        @pl.when(has_before)
        def _():
            pass_copy(1, at).wait_send()

        @pl.when(has_after)
        def _():
            pass_copy(0, at).wait_send()

        return carry

    lax.fori_loop(0, block, drain_passed, 0)


def near_stacks(images, variances, valid, psf_sigma, offsets, plan):
    tile, sky, blocks, block, epochs, runs, chunk = plan
    rows_out = tile + 2 * HEAD
    smem = pl.BlockSpec(memory_space=pltpu.SMEM)
    vmem = pl.BlockSpec(memory_space=pltpu.VMEM)
    anywhere = pl.BlockSpec(memory_space=pl.ANY)
    dma = pltpu.SemaphoreType.DMA
    half = blocks * block
    narrow, wide = jnp.bfloat16, jnp.float32
    scratch = [
        pltpu.VMEM((2 * (epochs + 1) * rows_out, LANES), wide),
        pltpu.VMEM(((epochs + 1) * rows_out, LANES), wide),
        pltpu.SMEM((VELS, LANES), jnp.int32),
        pltpu.VMEM((VELS, LANES), jnp.int32),
        dma(()),
        pltpu.VMEM((epochs, tile, tile), narrow),
        pltpu.VMEM((epochs, tile, tile), narrow),
        dma((2, epochs // chunk)),
        pltpu.VMEM((2 * REACH + 1, tile, 2 * LANES), narrow),
        pltpu.VMEM((2 * REACH + 1, EDGE, 2 * LANES), narrow),
        pltpu.VMEM((2, 2 * tile, 2 * LANES), narrow),
        pltpu.VMEM((rows_out, tile), wide),
        pltpu.VMEM((2 * PACK, LANES), wide),
        pltpu.VMEM((epochs, 2, rows_out, tile), narrow),
        pltpu.VMEM((epochs, 2, 2 * PACK, LANES), narrow),
        pltpu.VMEM((epochs, 2, tile, 2 * LANES), narrow),
        pltpu.VMEM((half, 3, tile, tile), narrow),
        pltpu.VMEM((half, 3, tile, tile), narrow),
        pltpu.VMEM((block, 2, tile, tile), narrow),
        pltpu.VMEM((block, 2, tile, tile), narrow),
        pltpu.VMEM((block, 2, tile, tile), wide),
        pltpu.VMEM((2, half, tile // 2, LANES), narrow),
        pltpu.VMEM((2, half, tile // 2, LANES), narrow),
        pltpu.VMEM((2, block, tile // 2, LANES), narrow),
        dma((half,)), dma((half,)), dma((block,)), dma((block,)),
        dma((2, half)), dma((2, half)), dma((2, block)), dma((2, block)),
    ]
    out = jax.ShapeDtypeStruct((block, tile, tile), jnp.float32)
    return pl.pallas_call(
        functools.partial(near_kernel, plan),
        out_shape=(out, out),
        in_specs=[vmem, smem, smem, anywhere, anywhere],
        out_specs=(vmem, vmem),
        scratch_shapes=scratch,
        compiler_params=pltpu.CompilerParams(
            collective_id=0, has_side_effects=True, vmem_limit_bytes=KEPT
        ),
    )(offsets, psf_sigma, valid.reshape(epochs), images, variances)


def far_stacks(images, variances, valid, psf_sigma, offsets, plan):
    tile, sky, blocks, block, epochs, runs = plan
    rows_out = -(-(tile + 2 * REACH) // 16) * 16
    smem = pl.BlockSpec(memory_space=pltpu.SMEM)
    vmem = pl.BlockSpec(memory_space=pltpu.VMEM)
    dma = pltpu.SemaphoreType.DMA
    half = blocks * block
    far = max(1, (blocks - 1) * block)
    scratch = [
        pltpu.VMEM((2 * (epochs + 1), rows_out, LANES), jnp.float32),
        pltpu.VMEM((2 * (epochs + 1), rows_out, LANES), jnp.float32),
        pltpu.SMEM((VELS, LANES), jnp.int32),
        pltpu.VMEM((VELS, LANES), jnp.int32),
        dma(()),
        pltpu.VMEM((rows_out, tile + LANES), jnp.float32),
        pltpu.VMEM((LANES, 2 * LANES), jnp.float32),
        pltpu.VMEM((1, LANES, 2 * LANES), jnp.float32),
        pltpu.VMEM((2, 2, 2 * LANES, 2 * LANES), jnp.bfloat16),
        pltpu.VMEM((half, 2, tile, tile), jnp.bfloat16),
        pltpu.VMEM((half, 2, tile, tile), jnp.bfloat16),
        pltpu.VMEM((far, 2, tile, tile), jnp.bfloat16),
        pltpu.VMEM((far, 2, tile, tile), jnp.bfloat16),
        pltpu.VMEM((2, block, 2, tile, tile), jnp.float32),
        dma((half,)), dma((half,)), dma((far,)), dma((far,)),
    ]
    usable = valid[:, 0].astype(jnp.float32)[:, None, None]
    inverse = usable / variances[:, 0].astype(jnp.float32)
    scaled = images[:, 0].astype(jnp.float32) * inverse
    own = jnp.stack([scaled.astype(jnp.bfloat16), inverse.astype(jnp.bfloat16)], axis=1)
    out = jax.ShapeDtypeStruct((block, tile, tile), jnp.float32)
    return pl.pallas_call(
        functools.partial(fused_kernel, plan),
        out_shape=(out, out),
        in_specs=[smem, vmem, smem, vmem, vmem],
        out_specs=(vmem, vmem),
        scratch_shapes=scratch,
        compiler_params=pltpu.CompilerParams(
            collective_id=0, has_side_effects=True, vmem_limit_bytes=56 * 2**20
        ),
    )(offsets, offsets, psf_sigma, *strips(own, sky, tile))


def on_device(images, variances, valid, psf_sigma, offsets):
    epochs = images.shape[0]
    tile = images.shape[-1]
    sky = lax.axis_size("sky")
    blocks = lax.axis_size("epoch")
    block = VELS // (blocks * lax.axis_size("vel"))
    last_epoch = epochs * blocks * lax.axis_size("vel") - 1
    runs = 1 + 2 * -(-REACH * (epochs - 1) // last_epoch)
    plan = (tile, sky, blocks, block, epochs, runs)
    few = EDGE * runs < LANES and epochs % CHUNK == 0
    if sky == GRID_X and blocks == 2 and lax.axis_size("vel") == 2 and few:
        plan += (CHUNK,)
        psi_sum, phi_sum = near_stacks(images, variances, valid, psf_sigma, offsets, plan)
    else:
        psi_sum, phi_sum = far_stacks(images, variances, valid, psf_sigma, offsets, plan)
    phi_sum = jnp.maximum(phi_sum, phi_floor)
    likelihood = psi_sum / jnp.sqrt(phi_sum)
    flux = psi_sum / phi_sum
    return (likelihood[:, None], flux[:, None])


def solution(mesh):
    placed = (
        P(("epoch", "vel"), ("field", "sky"), None, None),
        P(("epoch", "vel"), ("field", "sky"), None, None),
        P(("epoch", "vel"), ("field", "sky")),
        P(("field", "epoch", "vel")),
        P(None, None, "epoch"),
    )
    return jax.shard_map(
        on_device,
        mesh=mesh,
        in_specs=placed,
        out_specs=(
            P(("epoch", "vel"), ("field", "sky"), None, None),
            P(("epoch", "vel"), ("field", "sky"), None, None),
        ),
        check_vma=False,
    )
```

```python
import functools

import jax
import jax.numpy as jnp
from jax import lax
from jax.experimental import pallas as pl
from jax.experimental.pallas import tpu as pltpu
from jax.sharding import PartitionSpec as P

VELS = 16
REACH = 12
PSFR = 7
GRID_X = 4
MARGIN = REACH + PSFR
LANES = 128
HEAD = 16
PACK = 16
EDGE = 16
WINDOW = 32
CHUNK = 4
KEPT = 55705600

phi_floor = 0.25


def shifted(block, axis, distance):
    devices = range(lax.axis_size(axis))
    route = [((i - distance) % len(devices), i) for i in devices]
    return lax.ppermute(block, axis, route)


def positions(index, tile):
    return jnp.where(
        index < tile,
        index,
        jnp.where(
            index < tile + MARGIN,
            index - tile - MARGIN,
            jnp.where(index < tile + 2 * MARGIN, index - MARGIN, 4 * tile),
        ),
    )


FAR = -1.0e9


def exponents(distance):
    away = distance.astype(jnp.float32)
    return jnp.where(jnp.abs(distance) <= PSFR, -0.5 * away * away, FAR)


def fused_kernel(plan, *refs):
    tile, sky, blocks, block, epochs, runs = plan
    (offsets, motion, sigmas, own, halo, psi_out, phi_out, plane_a, plane_b, ends, ends_made, ends_sem, row_q,
     own_q, side_q, bands, send_v, recv_v, send_x, recv_x, keep, sv, rv, sx, rx) = refs
    maps = 2
    rows_in = row_q.shape[1]
    rows_out = plane_a.shape[1]
    width = 2 * LANES
    mesh_id = pl.DeviceIdType.MESH
    group = lax.axis_index("epoch")
    member = lax.axis_index("vel")
    partner = 1 - member

    barrier = pltpu.get_barrier_semaphore()
    greeted = 1
    pl.semaphore_signal(barrier, inc=1, device_id={"vel": partner}, device_id_type=mesh_id)
    for a in range(1, blocks):
        peer = lax.rem(group + a, blocks)
        pl.semaphore_signal(barrier, inc=1, device_id={"epoch": peer}, device_id_type=mesh_id)
        greeted += 1
    pl.semaphore_wait(barrier, greeted)

    shape = (rows_out, rows_in)
    row_q[...] = exponents(
        positions(lax.broadcasted_iota(jnp.int32, shape, 1), tile)
        - lax.broadcasted_iota(jnp.int32, shape, 0) + REACH
    )
    shape = (LANES, width)
    held = lax.broadcasted_iota(jnp.int32, shape, 0)
    shifted_out = lax.broadcasted_iota(jnp.int32, shape, 1) - REACH
    own_q[...] = exponents(held - shifted_out)
    side_q[0] = exponents(positions(held + tile, tile) - shifted_out)

    first = member * epochs

    at_epoch = lax.broadcasted_iota(jnp.int32, motion.shape[1:], 1)
    moved = jnp.zeros(motion.shape[1:], jnp.int32)
    for way in range(2):
        start = jnp.where(at_epoch == first, motion[way], 0)
        moved += jnp.abs(motion[way] - jnp.sum(start, axis=1, keepdims=True))
    held_here = (at_epoch >= first) & (at_epoch < first + epochs)
    counted = jnp.zeros(ends_made.shape, jnp.int32)
    at_run = lax.broadcasted_iota(jnp.int32, ends_made.shape, 1)
    for run in range(runs - 1):
        count = jnp.sum((held_here & (moved <= run)).astype(jnp.int32), axis=1, keepdims=True)
        counted = jnp.where(at_run == run, count, counted)
    ends_made[...] = counted
    ends_copy = pltpu.make_async_copy(ends_made, ends, ends_sem)
    ends_copy.start()
    plane_a[:maps] = jnp.zeros_like(plane_a[:maps])
    plane_b[:maps] = jnp.zeros_like(plane_b[:maps])

    def correlate(e, turn):
        sigma = jnp.full((8, LANES), sigmas[e], jnp.float32)
        power = 1.0 / (sigma * sigma)
        tap = lax.broadcasted_iota(jnp.int32, (8, LANES), 1) - PSFR
        norm = jnp.sum(jnp.exp(exponents(tap) * power), axis=1, keepdims=True)
        scale = (1.0 / norm)[:1]
        power = power[:1, :1]

        def both(q):
            profile = jnp.exp(q * power) * scale
            return profile.astype(jnp.bfloat16), (profile * profile).astype(jnp.bfloat16)

        row_bands = both(row_q[...])
        for part, q in enumerate((own_q[...], side_q[0])):
            for m, made in enumerate(both(q)):
                bands[turn, m, part * LANES : (part + 1) * LANES] = made
        for m in range(maps):
            side = halo[e, m]
            held = jnp.concatenate([own[e, m], side], axis=1)
            rows = jnp.dot(row_bands[m], held, preferred_element_type=jnp.float32)
            done = jnp.dot(
                rows.astype(jnp.bfloat16), bands[turn, m], preferred_element_type=jnp.float32
            )
            at = maps * e + m
            plane_a[at + maps] = plane_a[at] + done[:, :LANES]
            plane_b[at + maps] = plane_b[at] + done[:, LANES:]

    step = 2 if epochs % 2 == 0 else 1

    def several(i, carry):
        for turn in range(step):
            correlate(step * i + turn, turn)
        return carry

    lax.fori_loop(0, epochs // step, several, 0)

    def vel_copy(at):
        return pltpu.make_async_remote_copy(
            src_ref=send_v.at[at], dst_ref=recv_v.at[at], send_sem=sv.at[at], recv_sem=rv.at[at],
            device_id={"vel": partner}, device_id_type=mesh_id,
        )

    def epoch_copy(at):
        peer = lax.rem(group + 1 + at // block, blocks)
        return pltpu.make_async_remote_copy(
            src_ref=send_x.at[at], dst_ref=recv_x.at[at], send_sem=sx.at[at], recv_sem=rx.at[at],
            device_id={"epoch": peer}, device_id_type=mesh_id,
        )

    def stack(slot, carry):
        a = blocks - 1 - slot // (2 * block)
        turn = lax.rem(slot, 2 * block)
        mine = ((turn > 0) & (lax.rem(turn, 2) == 0)) | (turn == 2 * block - 1)
        b = jnp.where(mine, 0, 1)
        j = jnp.where(turn == 2 * block - 1, block - 1, jnp.where(mine, turn // 2 - 1, (turn + 1) // 2))
        place = a * block + j
        k = (lax.rem(group + a, blocks) * 2 + lax.rem(member + b, 2)) * block + j
        lane = lax.broadcasted_iota(jnp.int32, (tile, LANES), 1)
        summed = [jnp.zeros((tile, LANES), jnp.float32) for _ in range(maps)]
        low = jnp.zeros((), jnp.int32)
        for run in range(runs):
            high = ends[k, run] if run < runs - 1 else epochs
            at = first + jnp.minimum(low, epochs - 1)
            down = offsets[0, k, at] + REACH
            right = offsets[1, k, at] + REACH
            rows = pl.ds(down, tile)
            for m in range(maps):
                left_part = plane_a[maps * high + m, rows, :] - plane_a[maps * low + m, rows, :]
                right_part = plane_b[maps * high + m, rows, :] - plane_b[maps * low + m, rows, :]
                merged = jnp.where(lane >= right, left_part, right_part)
                summed[m] += pltpu.roll(merged, LANES - right, axis=1)
            low = high
        for m in range(maps):
            keep[b, j, m] = summed[m]

        @pl.when(b == 1)
        def _():
            send_v[place] = keep[1, j].astype(jnp.bfloat16)
            vel_copy(place).start()

        @pl.when(b == 0)
        def _():
            vel_copy(place).wait_recv()
            keep[0, j] = keep[0, j] + recv_v[place].astype(jnp.float32)

            @pl.when(a > 0)
            def _():
                send_x[place - block] = keep[0, j].astype(jnp.bfloat16)
                epoch_copy(place - block).start()

        return carry

    ends_copy.wait()
    lax.fori_loop(0, 2 * blocks * block, stack, 0)

    def finish(j, carry):
        total = keep[0, j]
        for a in range(1, blocks):
            at = (a - 1) * block + j
            epoch_copy(at).wait_recv()
            total = total + recv_x[at].astype(jnp.float32)
        psi_out[j] = total[0]
        phi_out[j] = total[1]
        return carry

    lax.fori_loop(0, block, finish, 0)

    def drain_v(at, carry):
        vel_copy(at).wait_send()
        return carry

    lax.fori_loop(0, blocks * block, drain_v, 0)

    def drain_x(at, carry):
        epoch_copy(at).wait_send()
        return carry

    lax.fori_loop(0, (blocks - 1) * block, drain_x, 0)


def strips(own, tile_count, tile):
    position = (lax.axis_index("sky") + GRID_X // 2) % tile_count
    column = position % GRID_X
    left = shifted(own[..., tile - MARGIN :], "sky", 1)
    right = shifted(own[..., :MARGIN], "sky", -1)
    left = jnp.where(column > 0, left, jnp.zeros_like(left))
    right = jnp.where(column < GRID_X - 1, right, jnp.zeros_like(right))
    blank = jnp.zeros(own.shape[:3] + (LANES - 2 * MARGIN,), jnp.bfloat16)
    both = jnp.concatenate([own, left, right, blank], axis=3)
    upper = shifted(both[:, :, tile - MARGIN :], "sky", GRID_X)
    lower = shifted(both[:, :, :MARGIN], "sky", -GRID_X)
    upper = jnp.where(position >= GRID_X, upper, jnp.zeros_like(upper))
    lower = jnp.where(position < tile_count - GRID_X, lower, jnp.zeros_like(lower))
    blank = jnp.zeros(both.shape[:2] + (LANES - 2 * MARGIN, both.shape[3]), jnp.bfloat16)
    both = jnp.concatenate([both, upper, lower, blank], axis=2)
    return both[..., :tile], both[..., tile:]


def near_kernel(plan, *refs):
    tile, sky, blocks, block, epochs, runs, chunk = plan
    (motion, sigmas, valid, images, variances, psi_out, phi_out, plane, edge, ends, ends_made, ends_sem,
     image, variance, load_sem, shift, edge_shift, unplace, row_q, edge_q, row_bands, edge_bands, columns,
     send_v, recv_v, send_x, recv_x, keep, send_z, recv_z, passed,
     sv, rv, sx, rx, sz, rz, sp, rp) = refs
    maps = 2
    rows_out = row_q.shape[0]
    mesh_id = pl.DeviceIdType.MESH
    me = lax.axis_index("sky")
    group = lax.axis_index("epoch")
    member = lax.axis_index("vel")
    column = lax.rem(lax.rem(me + GRID_X // 2, sky), GRID_X)
    before = lax.rem(me + sky - 1, sky)
    after = lax.rem(me + 1, sky)
    partner = 1 - member
    peer = 1 - group
    has_before = column > 0
    has_after = column < GRID_X - 1

    barrier = pltpu.get_barrier_semaphore()
    pl.semaphore_signal(barrier, inc=1, device_id={"vel": partner}, device_id_type=mesh_id)
    pl.semaphore_signal(barrier, inc=1, device_id={"epoch": peer}, device_id_type=mesh_id)

    @pl.when(has_before)
    def _():
        pl.semaphore_signal(barrier, inc=1, device_id={"sky": before}, device_id_type=mesh_id)

    @pl.when(has_after)
    def _():
        pl.semaphore_signal(barrier, inc=1, device_id={"sky": after}, device_id_type=mesh_id)

    greeted = 2 + jnp.where(has_before, 1, 0) + jnp.where(has_after, 1, 0)

    def load(which, c):
        source, held = ((images, image), (variances, variance))[which]
        span = pl.ds(c * chunk, chunk)
        return pltpu.make_async_copy(source.at[span, 0], held.at[span], load_sem.at[which, c])

    for c in range(epochs // chunk):
        for which in range(2):
            load(which, c).start()

    @pl.when(column == 0)
    def _():
        recv_z[1] = jnp.zeros_like(recv_z[1])
        passed[1] = jnp.zeros_like(passed[1])

    @pl.when(column == GRID_X - 1)
    def _():
        recv_z[0] = jnp.zeros_like(recv_z[0])
        passed[0] = jnp.zeros_like(passed[0])

    def iota(shape, axis):
        return lax.broadcasted_iota(jnp.int32, shape, axis)

    def one_hot(hit):
        return jnp.where(hit, 1.0, 0.0).astype(jnp.bfloat16)

    lane = iota((tile, LANES), 1)
    row = iota((tile, LANES), 0)

    def beyond(lanes):
        outward = lanes & (WINDOW - 1)
        side = jnp.where(lanes < 2 * WINDOW, outward - MARGIN, outward + tile)
        return jnp.where(outward < MARGIN, side, 8 * tile)

    def edge_column(lanes):
        index = (lanes & (EDGE - 1)) - EDGE // 2
        held = (index >= -PSFR) & (index < PSFR)
        return jnp.where(held, jnp.where(index < 0, index, index + tile), 4 * tile)

    short = iota((EDGE, LANES), 1)
    from_edge = edge_column(iota((EDGE, LANES), 0))

    outward = row - beyond(lane)
    moves = (row - lane, outward[:WINDOW], outward[tile - PACK :], from_edge - short, from_edge - beyond(short))

    def make_shift(at, carry):
        right = at - REACH
        shift[at, :, :LANES] = one_hot(moves[0] == right)
        shift[at, :WINDOW, LANES:] = one_hot(moves[1] == right)
        shift[at, WINDOW : tile - PACK, LANES:] = jnp.zeros((tile - PACK - WINDOW, LANES), jnp.bfloat16)
        shift[at, tile - PACK :, LANES:] = one_hot(moves[2] == right)
        edge_shift[at, :, :LANES] = one_hot(moves[3] == right)
        edge_shift[at, :, LANES:] = one_hot(moves[4] == right)
        return carry

    lax.fori_loop(0, 2 * REACH + 1, make_shift, 0)
    for m in range(maps):
        for bottom in range(2):
            begin = WINDOW * m + 2 * WINDOW * bottom
            inside = (row >= begin) & (row < begin + MARGIN)
            span = slice(bottom * LANES, (bottom + 1) * LANES)
            unplace[m, :tile, span] = one_hot(inside & (lane == row - begin))
            unplace[m, tile:, span] = one_hot(inside & (lane == row - begin + tile - MARGIN))

    row_q[...] = exponents(iota(row_q.shape, 1) - iota(row_q.shape, 0) + HEAD)
    at = iota(edge_q.shape, 0)
    at = jnp.where(at < PACK, at, at + tile - 2 * PACK)
    edge_q[...] = exponents(at - edge_column(iota(edge_q.shape, 1)))

    def make_bands(e):
        sigma = jnp.full((8, LANES), sigmas[e], jnp.float32)
        power = 1.0 / (sigma * sigma)
        tap = iota((8, LANES), 1) - PSFR
        norm = jnp.sum(jnp.exp(exponents(tap) * power), axis=1, keepdims=True)
        scale = (1.0 / norm)[:1]
        power = power[:1, :1]
        for q, bands in ((row_q, row_bands), (edge_q, edge_bands)):
            profile = jnp.exp(q[...] * power) * scale
            bands[e, 0] = profile.astype(jnp.bfloat16)
            bands[e, 1] = (profile * profile).astype(jnp.bfloat16)

    def all_bands(c, carry):
        for turn in range(chunk):
            make_bands(chunk * c + turn)
        return carry

    all_bands(0, 0)

    first = member * epochs
    at_epoch = iota(motion.shape[1:], 1)
    moved = jnp.zeros(motion.shape[1:], jnp.int32)
    for way in range(2):
        start = jnp.where(at_epoch == first, motion[way], 0)
        moved += jnp.abs(motion[way] - jnp.sum(start, axis=1, keepdims=True))
    held_here = (at_epoch >= first) & (at_epoch < first + epochs)
    counted = jnp.zeros(ends_made.shape, jnp.int32)
    at_run = iota(ends_made.shape, 1)
    low = jnp.zeros((VELS, 1), jnp.int32)
    for run in range(runs):
        high = jnp.full((VELS, 1), epochs, jnp.int32)
        if run < runs - 1:
            high = jnp.sum((held_here & (moved <= run)).astype(jnp.int32), axis=1, keepdims=True)
        begins = at_epoch == first + jnp.minimum(low, epochs - 1)
        down = jnp.sum(jnp.where(begins, motion[0], 0), axis=1, keepdims=True) + HEAD
        right = jnp.sum(jnp.where(begins, motion[1], 0), axis=1, keepdims=True) + REACH
        entries = (
            maps * rows_out * high + down, maps * rows_out * low + down,
            rows_out * high + down, rows_out * low + down, right,
        )
        for which, entry in enumerate(entries):
            counted = jnp.where(at_run == EDGE * which + run, entry, counted)
        low = high
    ends_made[...] = counted
    ends_copy = pltpu.make_async_copy(ends_made, ends, ends_sem)
    ends_copy.start()
    plane[: maps * rows_out] = jnp.zeros((maps * rows_out, LANES), jnp.float32)
    edge[:rows_out] = jnp.zeros((rows_out, LANES), jnp.float32)

    lax.fori_loop(1, epochs // chunk, all_bands, 0)

    def across(e):
        usable = valid[e].astype(jnp.float32)
        inverse = usable / variance[e].astype(jnp.float32)
        scaled = image[e].astype(jnp.float32) * inverse
        blank = jnp.zeros((tile - 2 * PACK, LANES), jnp.bfloat16)
        for m, field in enumerate((scaled, inverse)):
            rims = jnp.concatenate([edge_bands[e, m, :PACK], blank, edge_bands[e, m, PACK:]], axis=0)
            bands = jnp.concatenate([row_bands[e, m, HEAD : HEAD + tile], rims], axis=1)
            done = jnp.dot(field.astype(jnp.bfloat16), bands, preferred_element_type=jnp.float32)
            columns[e, m] = done.astype(jnp.bfloat16)

    own_half = iota((rows_out, LANES), 1) < LANES // 2

    def down(e):
        rims = []
        for m in range(maps):
            done = jnp.dot(row_bands[e, m], columns[e, m], preferred_element_type=jnp.float32)
            begin = pl.multiple_of((maps * e + m) * rows_out, 8)
            ends_at = pl.multiple_of((maps * e + m + maps) * rows_out, 8)
            plane[pl.ds(ends_at, rows_out)] = plane[pl.ds(begin, rows_out)] + done[:, :LANES]
            rims.append(done[:, LANES:])
        begin = pl.multiple_of(e * rows_out, 8)
        ends_at = pl.multiple_of((e + 1) * rows_out, 8)
        edge[pl.ds(ends_at, rows_out)] = edge[pl.ds(begin, rows_out)] + jnp.where(own_half, rims[0], rims[1])

    def arrive(c):
        for which in range(2):
            load(which, c).wait()

    def all_across(c):
        for turn in range(chunk):
            across(chunk * c + turn)

    def all_down(c):
        for turn in range(chunk):
            down(chunk * c + turn)

    def both_ways(c, carry):
        arrive(c)
        all_down(c - 1)
        all_across(c)
        return carry

    chunks = epochs // chunk
    arrive(0)
    all_across(0)
    lax.fori_loop(1, chunks, both_ways, 0)
    all_down(chunks - 1)

    def vel_copy(at):
        return pltpu.make_async_remote_copy(
            src_ref=send_v.at[at], dst_ref=recv_v.at[at], send_sem=sv, recv_sem=rv.at[at],
            device_id={"vel": partner}, device_id_type=mesh_id,
        )

    def epoch_copy(at):
        return pltpu.make_async_remote_copy(
            src_ref=send_x.at[at], dst_ref=recv_x.at[at], send_sem=sx, recv_sem=rx.at[at],
            device_id={"epoch": peer}, device_id_type=mesh_id,
        )

    def side_copy(to_after, at):
        return pltpu.make_async_remote_copy(
            src_ref=send_z.at[to_after, at], dst_ref=recv_z.at[to_after, at],
            send_sem=sz.at[to_after], recv_sem=rz.at[to_after, at],
            device_id={"sky": after if to_after else before}, device_id_type=mesh_id,
        )

    def pass_copy(to_after, at):
        return pltpu.make_async_remote_copy(
            src_ref=recv_z.at[to_after, block + at], dst_ref=passed.at[to_after, at],
            send_sem=sp.at[to_after], recv_sem=rp.at[to_after, at],
            device_id={"epoch": peer}, device_id_type=mesh_id,
        )

    each = LANES // (maps * EDGE)
    part = (lane // EDGE) & (each - 1)
    low_half = lane < LANES // 2
    first_window = (lane & WINDOW) == 0

    def stacked(k):
        summed = jnp.zeros((maps * tile, 2 * LANES), jnp.float32)
        rims = [jnp.zeros((tile, LANES), jnp.float32) for _ in range(2)]
        lefts, rights, rim_rights = [], [], []
        for run in range(runs):
            high, low, rim_high, rim_low, right = (ends[k, EDGE * which + run] for which in range(5))
            rim = edge[pl.ds(rim_high, tile), :]
            if run > 0:
                rim = rim - edge[pl.ds(rim_low, tile), :]
            rims[run // each] = jnp.where(part == run % each, rim, rims[run // each])
            pieces = []
            for m in range(maps):
                piece = plane[pl.ds(high + m * rows_out, tile), :]
                if run > 0:
                    piece = piece - plane[pl.ds(low + m * rows_out, tile), :]
                pieces.append(piece.astype(jnp.bfloat16))
            lefts.append(jnp.concatenate(pieces, axis=0))
            rights.append(shift[right])
            rim_rights.append(edge_shift[right])
        turned = [pltpu.roll(rim, LANES // 2, axis=1) for rim in rims]
        spread = (jnp.where(low_half, rims[0], turned[1]), jnp.where(low_half, turned[0], rims[1]))
        lefts.append(jnp.concatenate([rim.astype(jnp.bfloat16) for rim in spread], axis=0))
        spare = jnp.zeros((LANES - EDGE * runs, 2 * LANES), jnp.bfloat16)
        rights.append(jnp.concatenate(rim_rights + [spare], axis=0))
        for run in range(0, len(lefts), 2):
            summed += jnp.dot(
                jnp.concatenate(lefts[run : run + 2], axis=1), jnp.concatenate(rights[run : run + 2], axis=0),
                preferred_element_type=jnp.float32,
            )
        outer = jnp.where(first_window, summed[:tile, LANES:], summed[tile:, LANES:])
        return summed[:tile, :LANES], summed[tile:, :LANES], outer

    def spot_of(turn):
        return (blocks - 1 - turn // block) * block + lax.rem(turn, block)

    def owner_of(turn):
        return lax.rem(group + spot_of(turn) // block, blocks) * 2

    def theirs(turn):
        return stacked((owner_of(turn) + partner) * block + lax.rem(turn, block))

    def ours(turn):
        return stacked((owner_of(turn) + member) * block + lax.rem(turn, block))

    def hand_over(turn, parts):
        spot = spot_of(turn)
        for m in range(maps + 1):
            send_v[spot, m] = parts[m].astype(jnp.bfloat16)
        vel_copy(spot).start()

    def finish(turn, parts):
        spot = spot_of(turn)
        j = lax.rem(turn, block)
        vel_copy(spot).wait_recv()
        totals = [parts[m] + recv_v[spot, m].astype(jnp.float32) for m in range(maps + 1)]
        upper, lower = totals[maps][: tile // 2], totals[maps][tile // 2 :]
        to_left = low_half[: tile // 2]
        send_z[0, spot] = jnp.where(to_left, upper, pltpu.roll(lower, LANES // 2, axis=1)).astype(jnp.bfloat16)
        send_z[1, spot] = jnp.where(to_left, pltpu.roll(upper, LANES // 2, axis=1), lower).astype(jnp.bfloat16)

        @pl.when(has_before)
        def _():
            side_copy(0, spot).start()

        @pl.when(has_after)
        def _():
            side_copy(1, spot).start()

        @pl.when(spot >= block)
        def _():
            for m in range(maps):
                send_x[j, m] = totals[m].astype(jnp.bfloat16)
            epoch_copy(j).start()

        @pl.when(spot < block)
        def _():
            for m in range(maps):
                keep[j, m] = totals[m]

    last = blocks * block - 1

    def stack(turn, carry):
        ahead = theirs(turn + 1)
        kept = ours(turn)
        hand_over(turn + 1, ahead)
        finish(turn, kept)
        return carry

    ends_copy.wait()
    ahead = theirs(0)
    pl.semaphore_wait(barrier, greeted)
    hand_over(0, ahead)
    lax.fori_loop(0, last, stack, 0)
    finish(last, ours(last))

    def hand_on(at, carry):
        @pl.when(has_before)
        def _():
            side_copy(1, block + at).wait_recv()
            pass_copy(1, at).start()

        @pl.when(has_after)
        def _():
            side_copy(0, block + at).wait_recv()
            pass_copy(0, at).start()

        return carry

    lax.fori_loop(0, block, hand_on, 0)

    pltpu.make_async_remote_copy(
        src_ref=send_v, dst_ref=recv_v, send_sem=sv, recv_sem=rv.at[0],
        device_id={"vel": partner}, device_id_type=mesh_id,
    ).wait_send()
    pltpu.make_async_remote_copy(
        src_ref=send_x, dst_ref=recv_x, send_sem=sx, recv_sem=rx.at[0],
        device_id={"epoch": peer}, device_id_type=mesh_id,
    ).wait_send()

    def sent_side(to_after):
        pltpu.make_async_remote_copy(
            src_ref=send_z.at[to_after], dst_ref=recv_z.at[to_after],
            send_sem=sz.at[to_after], recv_sem=rz.at[to_after, 0],
            device_id={"sky": after if to_after else before}, device_id_type=mesh_id,
        ).wait_send()

    def sent_on(to_after):
        pltpu.make_async_remote_copy(
            src_ref=recv_z.at[to_after, pl.ds(block, block)], dst_ref=passed.at[to_after],
            send_sem=sp.at[to_after], recv_sem=rp.at[to_after, 0],
            device_id={"epoch": peer}, device_id_type=mesh_id,
        ).wait_send()

    @pl.when(has_before)
    def _():
        sent_side(0)

    @pl.when(has_after)
    def _():
        sent_side(1)

    def assemble(j, carry):
        epoch_copy(j).wait_recv()

        @pl.when(has_before)
        def _():
            pass_copy(1, j).wait_recv()
            side_copy(1, j).wait_recv()

        @pl.when(has_after)
        def _():
            pass_copy(0, j).wait_recv()
            side_copy(0, j).wait_recv()

        strips_in = jnp.concatenate([recv_z[1, j], recv_z[0, j], passed[1, j], passed[0, j]], axis=1)
        for m, out in enumerate((psi_out, phi_out)):
            added = jnp.dot(
                strips_in, jnp.concatenate([unplace[m]] * 2, axis=0), preferred_element_type=jnp.float32
            )
            for bottom in range(2):
                span = slice(bottom * tile // 2, (bottom + 1) * tile // 2)
                out[j, span] = (
                    keep[j, m, span] + recv_x[j, m, span].astype(jnp.float32)
                    + added[:, bottom * LANES : (bottom + 1) * LANES]
                )
        return carry

    lax.fori_loop(0, block, assemble, 0)

    @pl.when(has_before)
    def _():
        sent_on(1)

    @pl.when(has_after)
    def _():
        sent_on(0)


def near_stacks(images, variances, valid, psf_sigma, offsets, plan):
    tile, sky, blocks, block, epochs, runs, chunk = plan
    rows_out = tile + 2 * HEAD
    smem = pl.BlockSpec(memory_space=pltpu.SMEM)
    vmem = pl.BlockSpec(memory_space=pltpu.VMEM)
    anywhere = pl.BlockSpec(memory_space=pl.ANY)
    dma = pltpu.SemaphoreType.DMA
    half = blocks * block
    narrow, wide = jnp.bfloat16, jnp.float32
    scratch = [
        pltpu.VMEM((2 * (epochs + 1) * rows_out, LANES), wide),
        pltpu.VMEM(((epochs + 1) * rows_out, LANES), wide),
        pltpu.SMEM((VELS, LANES), jnp.int32),
        pltpu.VMEM((VELS, LANES), jnp.int32),
        dma(()),
        pltpu.VMEM((epochs, tile, tile), narrow),
        pltpu.VMEM((epochs, tile, tile), narrow),
        dma((2, epochs // chunk)),
        pltpu.VMEM((2 * REACH + 1, tile, 2 * LANES), narrow),
        pltpu.VMEM((2 * REACH + 1, EDGE, 2 * LANES), narrow),
        pltpu.VMEM((2, 2 * tile, 2 * LANES), narrow),
        pltpu.VMEM((rows_out, tile), wide),
        pltpu.VMEM((2 * PACK, LANES), wide),
        pltpu.VMEM((epochs, 2, rows_out, tile), narrow),
        pltpu.VMEM((epochs, 2, 2 * PACK, LANES), narrow),
        pltpu.VMEM((epochs, 2, tile, 2 * LANES), narrow),
        pltpu.VMEM((half, 3, tile, tile), narrow),
        pltpu.VMEM((half, 3, tile, tile), narrow),
        pltpu.VMEM((block, 2, tile, tile), narrow),
        pltpu.VMEM((block, 2, tile, tile), narrow),
        pltpu.VMEM((block, 2, tile, tile), wide),
        pltpu.VMEM((2, half, tile // 2, LANES), narrow),
        pltpu.VMEM((2, half, tile // 2, LANES), narrow),
        pltpu.VMEM((2, block, tile // 2, LANES), narrow),
        dma(()), dma((half,)), dma(()), dma((block,)),
        dma((2,)), dma((2, half)), dma((2,)), dma((2, block)),
    ]
    out = jax.ShapeDtypeStruct((block, tile, tile), jnp.float32)
    return pl.pallas_call(
        functools.partial(near_kernel, plan),
        out_shape=(out, out),
        in_specs=[vmem, smem, smem, anywhere, anywhere],
        out_specs=(vmem, vmem),
        scratch_shapes=scratch,
        compiler_params=pltpu.CompilerParams(
            collective_id=0, has_side_effects=True, vmem_limit_bytes=KEPT
        ),
    )(offsets, psf_sigma, valid.reshape(epochs), images, variances)


def far_stacks(images, variances, valid, psf_sigma, offsets, plan):
    tile, sky, blocks, block, epochs, runs = plan
    rows_out = -(-(tile + 2 * REACH) // 16) * 16
    smem = pl.BlockSpec(memory_space=pltpu.SMEM)
    vmem = pl.BlockSpec(memory_space=pltpu.VMEM)
    dma = pltpu.SemaphoreType.DMA
    half = blocks * block
    far = max(1, (blocks - 1) * block)
    scratch = [
        pltpu.VMEM((2 * (epochs + 1), rows_out, LANES), jnp.float32),
        pltpu.VMEM((2 * (epochs + 1), rows_out, LANES), jnp.float32),
        pltpu.SMEM((VELS, LANES), jnp.int32),
        pltpu.VMEM((VELS, LANES), jnp.int32),
        dma(()),
        pltpu.VMEM((rows_out, tile + LANES), jnp.float32),
        pltpu.VMEM((LANES, 2 * LANES), jnp.float32),
        pltpu.VMEM((1, LANES, 2 * LANES), jnp.float32),
        pltpu.VMEM((2, 2, 2 * LANES, 2 * LANES), jnp.bfloat16),
        pltpu.VMEM((half, 2, tile, tile), jnp.bfloat16),
        pltpu.VMEM((half, 2, tile, tile), jnp.bfloat16),
        pltpu.VMEM((far, 2, tile, tile), jnp.bfloat16),
        pltpu.VMEM((far, 2, tile, tile), jnp.bfloat16),
        pltpu.VMEM((2, block, 2, tile, tile), jnp.float32),
        dma((half,)), dma((half,)), dma((far,)), dma((far,)),
    ]
    usable = valid[:, 0].astype(jnp.float32)[:, None, None]
    inverse = usable / variances[:, 0].astype(jnp.float32)
    scaled = images[:, 0].astype(jnp.float32) * inverse
    own = jnp.stack([scaled.astype(jnp.bfloat16), inverse.astype(jnp.bfloat16)], axis=1)
    out = jax.ShapeDtypeStruct((block, tile, tile), jnp.float32)
    return pl.pallas_call(
        functools.partial(fused_kernel, plan),
        out_shape=(out, out),
        in_specs=[smem, vmem, smem, vmem, vmem],
        out_specs=(vmem, vmem),
        scratch_shapes=scratch,
        compiler_params=pltpu.CompilerParams(
            collective_id=0, has_side_effects=True, vmem_limit_bytes=56 * 2**20
        ),
    )(offsets, offsets, psf_sigma, *strips(own, sky, tile))


def on_device(images, variances, valid, psf_sigma, offsets):
    epochs = images.shape[0]
    tile = images.shape[-1]
    sky = lax.axis_size("sky")
    blocks = lax.axis_size("epoch")
    block = VELS // (blocks * lax.axis_size("vel"))
    last_epoch = epochs * blocks * lax.axis_size("vel") - 1
    runs = 1 + 2 * -(-REACH * (epochs - 1) // last_epoch)
    plan = (tile, sky, blocks, block, epochs, runs)
    few = EDGE * runs < LANES and epochs % CHUNK == 0
    if sky == GRID_X and blocks == 2 and lax.axis_size("vel") == 2 and few:
        plan += (CHUNK,)
        psi_sum, phi_sum = near_stacks(images, variances, valid, psf_sigma, offsets, plan)
    else:
        psi_sum, phi_sum = far_stacks(images, variances, valid, psf_sigma, offsets, plan)
    phi_sum = jnp.maximum(phi_sum, phi_floor)
    likelihood = psi_sum / jnp.sqrt(phi_sum)
    flux = psi_sum / phi_sum
    return (likelihood[:, None], flux[:, None])


def solution(mesh):
    placed = (
        P(("epoch", "vel"), ("field", "sky"), None, None),
        P(("epoch", "vel"), ("field", "sky"), None, None),
        P(("epoch", "vel"), ("field", "sky")),
        P(("field", "epoch", "vel")),
        P(None, None, "epoch"),
    )
    return jax.shard_map(
        on_device,
        mesh=mesh,
        in_specs=placed,
        out_specs=(
            P(("epoch", "vel"), ("field", "sky"), None, None),
            P(("epoch", "vel"), ("field", "sky"), None, None),
        ),
        check_vma=False,
    )
```

```python
import functools

import jax
import jax.numpy as jnp
from jax import lax
from jax.experimental import pallas as pl
from jax.experimental.pallas import tpu as pltpu
from jax.sharding import PartitionSpec as P

VELS = 16
REACH = 12
PSFR = 7
GRID_X = 4
MARGIN = REACH + PSFR
LANES = 128
HEAD = 16
PACK = 16
EDGE = 16
WINDOW = 32
CHUNK = 4
KEPT = 55705600

phi_floor = 0.25


def shifted(block, axis, distance):
    devices = range(lax.axis_size(axis))
    route = [((i - distance) % len(devices), i) for i in devices]
    return lax.ppermute(block, axis, route)


def positions(index, tile):
    return jnp.where(
        index < tile,
        index,
        jnp.where(
            index < tile + MARGIN,
            index - tile - MARGIN,
            jnp.where(index < tile + 2 * MARGIN, index - MARGIN, 4 * tile),
        ),
    )


FAR = -1.0e9


def exponents(distance):
    away = distance.astype(jnp.float32)
    return jnp.where(jnp.abs(distance) <= PSFR, -0.5 * away * away, FAR)


def fused_kernel(plan, *refs):
    tile, sky, blocks, block, epochs, runs = plan
    (offsets, motion, sigmas, own, halo, psi_out, phi_out, plane_a, plane_b, ends, ends_made, ends_sem, row_q,
     own_q, side_q, bands, send_v, recv_v, send_x, recv_x, keep, sv, rv, sx, rx) = refs
    maps = 2
    rows_in = row_q.shape[1]
    rows_out = plane_a.shape[1]
    width = 2 * LANES
    mesh_id = pl.DeviceIdType.MESH
    group = lax.axis_index("epoch")
    member = lax.axis_index("vel")
    partner = 1 - member

    barrier = pltpu.get_barrier_semaphore()
    greeted = 1
    pl.semaphore_signal(barrier, inc=1, device_id={"vel": partner}, device_id_type=mesh_id)
    for a in range(1, blocks):
        peer = lax.rem(group + a, blocks)
        pl.semaphore_signal(barrier, inc=1, device_id={"epoch": peer}, device_id_type=mesh_id)
        greeted += 1
    pl.semaphore_wait(barrier, greeted)

    shape = (rows_out, rows_in)
    row_q[...] = exponents(
        positions(lax.broadcasted_iota(jnp.int32, shape, 1), tile)
        - lax.broadcasted_iota(jnp.int32, shape, 0) + REACH
    )
    shape = (LANES, width)
    held = lax.broadcasted_iota(jnp.int32, shape, 0)
    shifted_out = lax.broadcasted_iota(jnp.int32, shape, 1) - REACH
    own_q[...] = exponents(held - shifted_out)
    side_q[0] = exponents(positions(held + tile, tile) - shifted_out)

    first = member * epochs

    at_epoch = lax.broadcasted_iota(jnp.int32, motion.shape[1:], 1)
    moved = jnp.zeros(motion.shape[1:], jnp.int32)
    for way in range(2):
        start = jnp.where(at_epoch == first, motion[way], 0)
        moved += jnp.abs(motion[way] - jnp.sum(start, axis=1, keepdims=True))
    held_here = (at_epoch >= first) & (at_epoch < first + epochs)
    counted = jnp.zeros(ends_made.shape, jnp.int32)
    at_run = lax.broadcasted_iota(jnp.int32, ends_made.shape, 1)
    for run in range(runs - 1):
        count = jnp.sum((held_here & (moved <= run)).astype(jnp.int32), axis=1, keepdims=True)
        counted = jnp.where(at_run == run, count, counted)
    ends_made[...] = counted
    ends_copy = pltpu.make_async_copy(ends_made, ends, ends_sem)
    ends_copy.start()
    plane_a[:maps] = jnp.zeros_like(plane_a[:maps])
    plane_b[:maps] = jnp.zeros_like(plane_b[:maps])

    def correlate(e, turn):
        sigma = jnp.full((8, LANES), sigmas[e], jnp.float32)
        power = 1.0 / (sigma * sigma)
        tap = lax.broadcasted_iota(jnp.int32, (8, LANES), 1) - PSFR
        norm = jnp.sum(jnp.exp(exponents(tap) * power), axis=1, keepdims=True)
        scale = (1.0 / norm)[:1]
        power = power[:1, :1]

        def both(q):
            profile = jnp.exp(q * power) * scale
            return profile.astype(jnp.bfloat16), (profile * profile).astype(jnp.bfloat16)

        row_bands = both(row_q[...])
        for part, q in enumerate((own_q[...], side_q[0])):
            for m, made in enumerate(both(q)):
                bands[turn, m, part * LANES : (part + 1) * LANES] = made
        for m in range(maps):
            side = halo[e, m]
            held = jnp.concatenate([own[e, m], side], axis=1)
            rows = jnp.dot(row_bands[m], held, preferred_element_type=jnp.float32)
            done = jnp.dot(
                rows.astype(jnp.bfloat16), bands[turn, m], preferred_element_type=jnp.float32
            )
            at = maps * e + m
            plane_a[at + maps] = plane_a[at] + done[:, :LANES]
            plane_b[at + maps] = plane_b[at] + done[:, LANES:]

    step = 2 if epochs % 2 == 0 else 1

    def several(i, carry):
        for turn in range(step):
            correlate(step * i + turn, turn)
        return carry

    lax.fori_loop(0, epochs // step, several, 0)

    def vel_copy(at):
        return pltpu.make_async_remote_copy(
            src_ref=send_v.at[at], dst_ref=recv_v.at[at], send_sem=sv.at[at], recv_sem=rv.at[at],
            device_id={"vel": partner}, device_id_type=mesh_id,
        )

    def epoch_copy(at):
        peer = lax.rem(group + 1 + at // block, blocks)
        return pltpu.make_async_remote_copy(
            src_ref=send_x.at[at], dst_ref=recv_x.at[at], send_sem=sx.at[at], recv_sem=rx.at[at],
            device_id={"epoch": peer}, device_id_type=mesh_id,
        )

    def stack(slot, carry):
        a = blocks - 1 - slot // (2 * block)
        turn = lax.rem(slot, 2 * block)
        mine = ((turn > 0) & (lax.rem(turn, 2) == 0)) | (turn == 2 * block - 1)
        b = jnp.where(mine, 0, 1)
        j = jnp.where(turn == 2 * block - 1, block - 1, jnp.where(mine, turn // 2 - 1, (turn + 1) // 2))
        place = a * block + j
        k = (lax.rem(group + a, blocks) * 2 + lax.rem(member + b, 2)) * block + j
        lane = lax.broadcasted_iota(jnp.int32, (tile, LANES), 1)
        summed = [jnp.zeros((tile, LANES), jnp.float32) for _ in range(maps)]
        low = jnp.zeros((), jnp.int32)
        for run in range(runs):
            high = ends[k, run] if run < runs - 1 else epochs
            at = first + jnp.minimum(low, epochs - 1)
            down = offsets[0, k, at] + REACH
            right = offsets[1, k, at] + REACH
            rows = pl.ds(down, tile)
            for m in range(maps):
                left_part = plane_a[maps * high + m, rows, :] - plane_a[maps * low + m, rows, :]
                right_part = plane_b[maps * high + m, rows, :] - plane_b[maps * low + m, rows, :]
                merged = jnp.where(lane >= right, left_part, right_part)
                summed[m] += pltpu.roll(merged, LANES - right, axis=1)
            low = high
        for m in range(maps):
            keep[b, j, m] = summed[m]

        @pl.when(b == 1)
        def _():
            send_v[place] = keep[1, j].astype(jnp.bfloat16)
            vel_copy(place).start()

        @pl.when(b == 0)
        def _():
            vel_copy(place).wait_recv()
            keep[0, j] = keep[0, j] + recv_v[place].astype(jnp.float32)

            @pl.when(a > 0)
            def _():
                send_x[place - block] = keep[0, j].astype(jnp.bfloat16)
                epoch_copy(place - block).start()

        return carry

    ends_copy.wait()
    lax.fori_loop(0, 2 * blocks * block, stack, 0)

    def finish(j, carry):
        total = keep[0, j]
        for a in range(1, blocks):
            at = (a - 1) * block + j
            epoch_copy(at).wait_recv()
            total = total + recv_x[at].astype(jnp.float32)
        psi_out[j] = total[0]
        phi_out[j] = total[1]
        return carry

    lax.fori_loop(0, block, finish, 0)

    def drain_v(at, carry):
        vel_copy(at).wait_send()
        return carry

    lax.fori_loop(0, blocks * block, drain_v, 0)

    def drain_x(at, carry):
        epoch_copy(at).wait_send()
        return carry

    lax.fori_loop(0, (blocks - 1) * block, drain_x, 0)


def strips(own, tile_count, tile):
    position = (lax.axis_index("sky") + GRID_X // 2) % tile_count
    column = position % GRID_X
    left = shifted(own[..., tile - MARGIN :], "sky", 1)
    right = shifted(own[..., :MARGIN], "sky", -1)
    left = jnp.where(column > 0, left, jnp.zeros_like(left))
    right = jnp.where(column < GRID_X - 1, right, jnp.zeros_like(right))
    blank = jnp.zeros(own.shape[:3] + (LANES - 2 * MARGIN,), jnp.bfloat16)
    both = jnp.concatenate([own, left, right, blank], axis=3)
    upper = shifted(both[:, :, tile - MARGIN :], "sky", GRID_X)
    lower = shifted(both[:, :, :MARGIN], "sky", -GRID_X)
    upper = jnp.where(position >= GRID_X, upper, jnp.zeros_like(upper))
    lower = jnp.where(position < tile_count - GRID_X, lower, jnp.zeros_like(lower))
    blank = jnp.zeros(both.shape[:2] + (LANES - 2 * MARGIN, both.shape[3]), jnp.bfloat16)
    both = jnp.concatenate([both, upper, lower, blank], axis=2)
    return both[..., :tile], both[..., tile:]


def near_kernel(plan, *refs):
    tile, sky, blocks, block, epochs, runs, chunk = plan
    (motion, sigmas, valid, images, variances, psi_out, phi_out, plane, edge, ends, ends_made, ends_sem,
     image, variance, load_sem, shift, edge_shift, unplace, row_q, edge_q, row_bands, edge_bands, columns,
     send_v, recv_v, send_x, recv_x, keep, send_z, recv_z, passed,
     sv, rv, sx, rx, sz, rz, sp, rp) = refs
    maps = 2
    rows_out = row_q.shape[0]
    mesh_id = pl.DeviceIdType.MESH
    me = lax.axis_index("sky")
    group = lax.axis_index("epoch")
    member = lax.axis_index("vel")
    column = lax.rem(lax.rem(me + GRID_X // 2, sky), GRID_X)
    before = lax.rem(me + sky - 1, sky)
    after = lax.rem(me + 1, sky)
    partner = 1 - member
    peer = 1 - group
    has_before = column > 0
    has_after = column < GRID_X - 1

    barrier = pltpu.get_barrier_semaphore()
    pl.semaphore_signal(barrier, inc=1, device_id={"vel": partner}, device_id_type=mesh_id)
    pl.semaphore_signal(barrier, inc=1, device_id={"epoch": peer}, device_id_type=mesh_id)

    @pl.when(has_before)
    def _():
        pl.semaphore_signal(barrier, inc=1, device_id={"sky": before}, device_id_type=mesh_id)

    @pl.when(has_after)
    def _():
        pl.semaphore_signal(barrier, inc=1, device_id={"sky": after}, device_id_type=mesh_id)

    greeted = 2 + jnp.where(has_before, 1, 0) + jnp.where(has_after, 1, 0)

    def load(which, c):
        source, held = ((images, image), (variances, variance))[which]
        span = pl.ds(c * chunk, chunk)
        return pltpu.make_async_copy(source.at[span, 0], held.at[span], load_sem.at[which, c])

    for c in range(epochs // chunk):
        for which in range(2):
            load(which, c).start()

    @pl.when(column == 0)
    def _():
        recv_z[1] = jnp.zeros_like(recv_z[1])
        passed[1] = jnp.zeros_like(passed[1])

    @pl.when(column == GRID_X - 1)
    def _():
        recv_z[0] = jnp.zeros_like(recv_z[0])
        passed[0] = jnp.zeros_like(passed[0])

    def iota(shape, axis):
        return lax.broadcasted_iota(jnp.int32, shape, axis)

    def one_hot(hit):
        return jnp.where(hit, 1.0, 0.0).astype(jnp.bfloat16)

    lane = iota((tile, LANES), 1)
    row = iota((tile, LANES), 0)

    def beyond(lanes):
        outward = lanes & (WINDOW - 1)
        side = jnp.where(lanes < 2 * WINDOW, outward - MARGIN, outward + tile)
        return jnp.where(outward < MARGIN, side, 8 * tile)

    def edge_column(lanes):
        index = (lanes & (EDGE - 1)) - EDGE // 2
        held = (index >= -PSFR) & (index < PSFR)
        return jnp.where(held, jnp.where(index < 0, index, index + tile), 4 * tile)

    short = iota((EDGE, LANES), 1)
    from_edge = edge_column(iota((EDGE, LANES), 0))

    outward = row - beyond(lane)
    moves = (row - lane, outward[:WINDOW], outward[tile - PACK :], from_edge - short, from_edge - beyond(short))

    def make_shift(at, carry):
        right = at - REACH
        shift[at, :, :LANES] = one_hot(moves[0] == right)
        shift[at, :WINDOW, LANES:] = one_hot(moves[1] == right)
        shift[at, WINDOW : tile - PACK, LANES:] = jnp.zeros((tile - PACK - WINDOW, LANES), jnp.bfloat16)
        shift[at, tile - PACK :, LANES:] = one_hot(moves[2] == right)
        edge_shift[at, :, :LANES] = one_hot(moves[3] == right)
        edge_shift[at, :, LANES:] = one_hot(moves[4] == right)
        return carry

    lax.fori_loop(0, 2 * REACH + 1, make_shift, 0)
    for m in range(maps):
        for bottom in range(2):
            begin = WINDOW * m + 2 * WINDOW * bottom
            inside = (row >= begin) & (row < begin + MARGIN)
            span = slice(bottom * LANES, (bottom + 1) * LANES)
            unplace[m, :tile, span] = one_hot(inside & (lane == row - begin))
            unplace[m, tile:, span] = one_hot(inside & (lane == row - begin + tile - MARGIN))

    row_q[...] = exponents(iota(row_q.shape, 1) - iota(row_q.shape, 0) + HEAD)
    at = iota(edge_q.shape, 0)
    at = jnp.where(at < PACK, at, at + tile - 2 * PACK)
    edge_q[...] = exponents(at - edge_column(iota(edge_q.shape, 1)))

    def make_bands(e):
        sigma = jnp.full((8, LANES), sigmas[e], jnp.float32)
        power = 1.0 / (sigma * sigma)
        tap = iota((8, LANES), 1) - PSFR
        norm = jnp.sum(jnp.exp(exponents(tap) * power), axis=1, keepdims=True)
        scale = (1.0 / norm)[:1]
        power = power[:1, :1]
        for q, bands in ((row_q, row_bands), (edge_q, edge_bands)):
            profile = jnp.exp(q[...] * power) * scale
            bands[e, 0] = profile.astype(jnp.bfloat16)
            bands[e, 1] = (profile * profile).astype(jnp.bfloat16)

    def all_bands(c, carry):
        for turn in range(chunk):
            make_bands(chunk * c + turn)
        return carry

    all_bands(0, 0)

    first = member * epochs
    at_epoch = iota(motion.shape[1:], 1)
    moved = jnp.zeros(motion.shape[1:], jnp.int32)
    for way in range(2):
        start = jnp.where(at_epoch == first, motion[way], 0)
        moved += jnp.abs(motion[way] - jnp.sum(start, axis=1, keepdims=True))
    held_here = (at_epoch >= first) & (at_epoch < first + epochs)
    counted = jnp.zeros(ends_made.shape, jnp.int32)
    at_run = iota(ends_made.shape, 1)
    low = jnp.zeros((VELS, 1), jnp.int32)
    for run in range(runs):
        high = jnp.full((VELS, 1), epochs, jnp.int32)
        if run < runs - 1:
            high = jnp.sum((held_here & (moved <= run)).astype(jnp.int32), axis=1, keepdims=True)
        begins = at_epoch == first + jnp.minimum(low, epochs - 1)
        down = jnp.sum(jnp.where(begins, motion[0], 0), axis=1, keepdims=True) + HEAD
        right = jnp.sum(jnp.where(begins, motion[1], 0), axis=1, keepdims=True) + REACH
        entries = (
            maps * rows_out * high + down, maps * rows_out * low + down,
            rows_out * high + down, rows_out * low + down, right,
        )
        for which, entry in enumerate(entries):
            counted = jnp.where(at_run == EDGE * which + run, entry, counted)
        low = high
    ends_made[...] = counted
    ends_copy = pltpu.make_async_copy(ends_made, ends, ends_sem)
    ends_copy.start()
    plane[: maps * rows_out] = jnp.zeros((maps * rows_out, LANES), jnp.float32)
    edge[:rows_out] = jnp.zeros((rows_out, LANES), jnp.float32)

    def across(e):
        usable = valid[e].astype(jnp.float32)
        inverse = usable / variance[e].astype(jnp.float32)
        scaled = image[e].astype(jnp.float32) * inverse
        blank = jnp.zeros((tile - 2 * PACK, LANES), jnp.bfloat16)
        for m, field in enumerate((scaled, inverse)):
            rims = jnp.concatenate([edge_bands[e, m, :PACK], blank, edge_bands[e, m, PACK:]], axis=0)
            bands = jnp.concatenate([row_bands[e, m, HEAD : HEAD + tile], rims], axis=1)
            done = jnp.dot(field.astype(jnp.bfloat16), bands, preferred_element_type=jnp.float32)
            columns[e, m] = done.astype(jnp.bfloat16)

    own_half = iota((rows_out, LANES), 1) < LANES // 2

    def down(e):
        rims = []
        for m in range(maps):
            done = jnp.dot(row_bands[e, m], columns[e, m], preferred_element_type=jnp.float32)
            begin = pl.multiple_of((maps * e + m) * rows_out, 8)
            ends_at = pl.multiple_of((maps * e + m + maps) * rows_out, 8)
            plane[pl.ds(ends_at, rows_out)] = plane[pl.ds(begin, rows_out)] + done[:, :LANES]
            rims.append(done[:, LANES:])
        begin = pl.multiple_of(e * rows_out, 8)
        ends_at = pl.multiple_of((e + 1) * rows_out, 8)
        edge[pl.ds(ends_at, rows_out)] = edge[pl.ds(begin, rows_out)] + jnp.where(own_half, rims[0], rims[1])

    def arrive(c):
        for which in range(2):
            load(which, c).wait()

    def all_across(c):
        for turn in range(chunk):
            across(chunk * c + turn)

    def all_down(c):
        for turn in range(chunk):
            down(chunk * c + turn)

    def both_ways(c, carry):
        arrive(c)
        all_down(c - 1)
        all_across(c)
        return all_bands(c + 1, carry)

    chunks = epochs // chunk
    arrive(0)
    all_across(0)
    all_bands(1, 0)
    lax.fori_loop(1, chunks - 1, both_ways, 0)
    arrive(chunks - 1)
    all_down(chunks - 2)
    all_across(chunks - 1)
    all_down(chunks - 1)

    def vel_copy(at):
        return pltpu.make_async_remote_copy(
            src_ref=send_v.at[at], dst_ref=recv_v.at[at], send_sem=sv, recv_sem=rv.at[at],
            device_id={"vel": partner}, device_id_type=mesh_id,
        )

    def epoch_copy(at):
        return pltpu.make_async_remote_copy(
            src_ref=send_x.at[at], dst_ref=recv_x.at[at], send_sem=sx, recv_sem=rx.at[at],
            device_id={"epoch": peer}, device_id_type=mesh_id,
        )

    def side_copy(to_after, at):
        return pltpu.make_async_remote_copy(
            src_ref=send_z.at[to_after, at], dst_ref=recv_z.at[to_after, at],
            send_sem=sz.at[to_after], recv_sem=rz.at[to_after, at],
            device_id={"sky": after if to_after else before}, device_id_type=mesh_id,
        )

    def pass_copy(to_after, at):
        return pltpu.make_async_remote_copy(
            src_ref=recv_z.at[to_after, block + at], dst_ref=passed.at[to_after, at],
            send_sem=sp.at[to_after], recv_sem=rp.at[to_after, at],
            device_id={"epoch": peer}, device_id_type=mesh_id,
        )

    each = LANES // (maps * EDGE)
    part = (lane // EDGE) & (each - 1)
    low_half = lane < LANES // 2
    first_window = (lane & WINDOW) == 0

    def stacked(k):
        summed = jnp.zeros((maps * tile, 2 * LANES), jnp.float32)
        rims = [jnp.zeros((tile, LANES), jnp.float32) for _ in range(2)]
        lefts, rights, rim_rights = [], [], []
        for run in range(runs):
            high, low, rim_high, rim_low, right = (ends[k, EDGE * which + run] for which in range(5))
            rim = edge[pl.ds(rim_high, tile), :]
            if run > 0:
                rim = rim - edge[pl.ds(rim_low, tile), :]
            rims[run // each] = jnp.where(part == run % each, rim, rims[run // each])
            pieces = []
            for m in range(maps):
                piece = plane[pl.ds(high + m * rows_out, tile), :]
                if run > 0:
                    piece = piece - plane[pl.ds(low + m * rows_out, tile), :]
                pieces.append(piece.astype(jnp.bfloat16))
            lefts.append(jnp.concatenate(pieces, axis=0))
            rights.append(shift[right])
            rim_rights.append(edge_shift[right])
        turned = [pltpu.roll(rim, LANES // 2, axis=1) for rim in rims]
        spread = (jnp.where(low_half, rims[0], turned[1]), jnp.where(low_half, turned[0], rims[1]))
        lefts.append(jnp.concatenate([rim.astype(jnp.bfloat16) for rim in spread], axis=0))
        spare = jnp.zeros((LANES - EDGE * runs, 2 * LANES), jnp.bfloat16)
        rights.append(jnp.concatenate(rim_rights + [spare], axis=0))
        for run in range(0, len(lefts), 2):
            summed += jnp.dot(
                jnp.concatenate(lefts[run : run + 2], axis=1), jnp.concatenate(rights[run : run + 2], axis=0),
                preferred_element_type=jnp.float32,
            )
        outer = jnp.where(first_window, summed[:tile, LANES:], summed[tile:, LANES:])
        return summed[:tile, :LANES], summed[tile:, :LANES], outer

    def spot_of(turn):
        return (blocks - 1 - turn // block) * block + lax.rem(turn, block)

    def owner_of(turn):
        return lax.rem(group + spot_of(turn) // block, blocks) * 2

    def theirs(turn):
        return stacked((owner_of(turn) + partner) * block + lax.rem(turn, block))

    def ours(turn):
        return stacked((owner_of(turn) + member) * block + lax.rem(turn, block))

    def hand_over(turn, parts):
        spot = spot_of(turn)
        for m in range(maps + 1):
            send_v[spot, m] = parts[m].astype(jnp.bfloat16)
        vel_copy(spot).start()

    def finish(turn, parts):
        spot = spot_of(turn)
        j = lax.rem(turn, block)
        vel_copy(spot).wait_recv()
        totals = [parts[m] + recv_v[spot, m].astype(jnp.float32) for m in range(maps + 1)]
        upper, lower = totals[maps][: tile // 2], totals[maps][tile // 2 :]
        to_left = low_half[: tile // 2]
        send_z[0, spot] = jnp.where(to_left, upper, pltpu.roll(lower, LANES // 2, axis=1)).astype(jnp.bfloat16)
        send_z[1, spot] = jnp.where(to_left, pltpu.roll(upper, LANES // 2, axis=1), lower).astype(jnp.bfloat16)

        @pl.when(has_before)
        def _():
            side_copy(0, spot).start()

        @pl.when(has_after)
        def _():
            side_copy(1, spot).start()

        @pl.when(spot >= block)
        def _():
            for m in range(maps):
                send_x[j, m] = totals[m].astype(jnp.bfloat16)
            epoch_copy(j).start()

        @pl.when(spot < block)
        def _():
            for m in range(maps):
                keep[j, m] = totals[m]

    last = blocks * block - 1

    def stack(turn, carry):
        ahead = theirs(turn + 1)
        kept = ours(turn)
        hand_over(turn + 1, ahead)
        finish(turn, kept)
        return carry

    ends_copy.wait()
    ahead = theirs(0)
    pl.semaphore_wait(barrier, greeted)
    hand_over(0, ahead)
    lax.fori_loop(0, last, stack, 0)
    finish(last, ours(last))

    def hand_on(at, carry):
        @pl.when(has_before)
        def _():
            side_copy(1, block + at).wait_recv()
            pass_copy(1, at).start()

        @pl.when(has_after)
        def _():
            side_copy(0, block + at).wait_recv()
            pass_copy(0, at).start()

        return carry

    lax.fori_loop(0, block, hand_on, 0)

    pltpu.make_async_remote_copy(
        src_ref=send_v, dst_ref=recv_v, send_sem=sv, recv_sem=rv.at[0],
        device_id={"vel": partner}, device_id_type=mesh_id,
    ).wait_send()
    pltpu.make_async_remote_copy(
        src_ref=send_x, dst_ref=recv_x, send_sem=sx, recv_sem=rx.at[0],
        device_id={"epoch": peer}, device_id_type=mesh_id,
    ).wait_send()

    def sent_side(to_after):
        pltpu.make_async_remote_copy(
            src_ref=send_z.at[to_after], dst_ref=recv_z.at[to_after],
            send_sem=sz.at[to_after], recv_sem=rz.at[to_after, 0],
            device_id={"sky": after if to_after else before}, device_id_type=mesh_id,
        ).wait_send()

    def sent_on(to_after):
        pltpu.make_async_remote_copy(
            src_ref=recv_z.at[to_after, pl.ds(block, block)], dst_ref=passed.at[to_after],
            send_sem=sp.at[to_after], recv_sem=rp.at[to_after, 0],
            device_id={"epoch": peer}, device_id_type=mesh_id,
        ).wait_send()

    @pl.when(has_before)
    def _():
        sent_side(0)

    @pl.when(has_after)
    def _():
        sent_side(1)

    def assemble(j, carry):
        epoch_copy(j).wait_recv()

        @pl.when(has_before)
        def _():
            pass_copy(1, j).wait_recv()
            side_copy(1, j).wait_recv()

        @pl.when(has_after)
        def _():
            pass_copy(0, j).wait_recv()
            side_copy(0, j).wait_recv()

        strips_in = jnp.concatenate([recv_z[1, j], recv_z[0, j], passed[1, j], passed[0, j]], axis=1)
        for m, out in enumerate((psi_out, phi_out)):
            added = jnp.dot(
                strips_in, jnp.concatenate([unplace[m]] * 2, axis=0), preferred_element_type=jnp.float32
            )
            for bottom in range(2):
                span = slice(bottom * tile // 2, (bottom + 1) * tile // 2)
                out[j, span] = (
                    keep[j, m, span] + recv_x[j, m, span].astype(jnp.float32)
                    + added[:, bottom * LANES : (bottom + 1) * LANES]
                )
        return carry

    lax.fori_loop(0, block, assemble, 0)

    @pl.when(has_before)
    def _():
        sent_on(1)

    @pl.when(has_after)
    def _():
        sent_on(0)


def near_stacks(images, variances, valid, psf_sigma, offsets, plan):
    tile, sky, blocks, block, epochs, runs, chunk = plan
    rows_out = tile + 2 * HEAD
    smem = pl.BlockSpec(memory_space=pltpu.SMEM)
    vmem = pl.BlockSpec(memory_space=pltpu.VMEM)
    anywhere = pl.BlockSpec(memory_space=pl.ANY)
    dma = pltpu.SemaphoreType.DMA
    half = blocks * block
    narrow, wide = jnp.bfloat16, jnp.float32
    scratch = [
        pltpu.VMEM((2 * (epochs + 1) * rows_out, LANES), wide),
        pltpu.VMEM(((epochs + 1) * rows_out, LANES), wide),
        pltpu.SMEM((VELS, LANES), jnp.int32),
        pltpu.VMEM((VELS, LANES), jnp.int32),
        dma(()),
        pltpu.VMEM((epochs, tile, tile), narrow),
        pltpu.VMEM((epochs, tile, tile), narrow),
        dma((2, epochs // chunk)),
        pltpu.VMEM((2 * REACH + 1, tile, 2 * LANES), narrow),
        pltpu.VMEM((2 * REACH + 1, EDGE, 2 * LANES), narrow),
        pltpu.VMEM((2, 2 * tile, 2 * LANES), narrow),
        pltpu.VMEM((rows_out, tile), wide),
        pltpu.VMEM((2 * PACK, LANES), wide),
        pltpu.VMEM((epochs, 2, rows_out, tile), narrow),
        pltpu.VMEM((epochs, 2, 2 * PACK, LANES), narrow),
        pltpu.VMEM((epochs, 2, tile, 2 * LANES), narrow),
        pltpu.VMEM((half, 3, tile, tile), narrow),
        pltpu.VMEM((half, 3, tile, tile), narrow),
        pltpu.VMEM((block, 2, tile, tile), narrow),
        pltpu.VMEM((block, 2, tile, tile), narrow),
        pltpu.VMEM((block, 2, tile, tile), wide),
        pltpu.VMEM((2, half, tile // 2, LANES), narrow),
        pltpu.VMEM((2, half, tile // 2, LANES), narrow),
        pltpu.VMEM((2, block, tile // 2, LANES), narrow),
        dma(()), dma((half,)), dma(()), dma((block,)),
        dma((2,)), dma((2, half)), dma((2,)), dma((2, block)),
    ]
    out = jax.ShapeDtypeStruct((block, tile, tile), jnp.float32)
    return pl.pallas_call(
        functools.partial(near_kernel, plan),
        out_shape=(out, out),
        in_specs=[vmem, smem, smem, anywhere, anywhere],
        out_specs=(vmem, vmem),
        scratch_shapes=scratch,
        compiler_params=pltpu.CompilerParams(
            collective_id=0, has_side_effects=True, vmem_limit_bytes=KEPT
        ),
    )(offsets, psf_sigma, valid.reshape(epochs), images, variances)


def far_stacks(images, variances, valid, psf_sigma, offsets, plan):
    tile, sky, blocks, block, epochs, runs = plan
    rows_out = -(-(tile + 2 * REACH) // 16) * 16
    smem = pl.BlockSpec(memory_space=pltpu.SMEM)
    vmem = pl.BlockSpec(memory_space=pltpu.VMEM)
    dma = pltpu.SemaphoreType.DMA
    half = blocks * block
    far = max(1, (blocks - 1) * block)
    scratch = [
        pltpu.VMEM((2 * (epochs + 1), rows_out, LANES), jnp.float32),
        pltpu.VMEM((2 * (epochs + 1), rows_out, LANES), jnp.float32),
        pltpu.SMEM((VELS, LANES), jnp.int32),
        pltpu.VMEM((VELS, LANES), jnp.int32),
        dma(()),
        pltpu.VMEM((rows_out, tile + LANES), jnp.float32),
        pltpu.VMEM((LANES, 2 * LANES), jnp.float32),
        pltpu.VMEM((1, LANES, 2 * LANES), jnp.float32),
        pltpu.VMEM((2, 2, 2 * LANES, 2 * LANES), jnp.bfloat16),
        pltpu.VMEM((half, 2, tile, tile), jnp.bfloat16),
        pltpu.VMEM((half, 2, tile, tile), jnp.bfloat16),
        pltpu.VMEM((far, 2, tile, tile), jnp.bfloat16),
        pltpu.VMEM((far, 2, tile, tile), jnp.bfloat16),
        pltpu.VMEM((2, block, 2, tile, tile), jnp.float32),
        dma((half,)), dma((half,)), dma((far,)), dma((far,)),
    ]
    usable = valid[:, 0].astype(jnp.float32)[:, None, None]
    inverse = usable / variances[:, 0].astype(jnp.float32)
    scaled = images[:, 0].astype(jnp.float32) * inverse
    own = jnp.stack([scaled.astype(jnp.bfloat16), inverse.astype(jnp.bfloat16)], axis=1)
    out = jax.ShapeDtypeStruct((block, tile, tile), jnp.float32)
    return pl.pallas_call(
        functools.partial(fused_kernel, plan),
        out_shape=(out, out),
        in_specs=[smem, vmem, smem, vmem, vmem],
        out_specs=(vmem, vmem),
        scratch_shapes=scratch,
        compiler_params=pltpu.CompilerParams(
            collective_id=0, has_side_effects=True, vmem_limit_bytes=56 * 2**20
        ),
    )(offsets, offsets, psf_sigma, *strips(own, sky, tile))


def on_device(images, variances, valid, psf_sigma, offsets):
    epochs = images.shape[0]
    tile = images.shape[-1]
    sky = lax.axis_size("sky")
    blocks = lax.axis_size("epoch")
    block = VELS // (blocks * lax.axis_size("vel"))
    last_epoch = epochs * blocks * lax.axis_size("vel") - 1
    runs = 1 + 2 * -(-REACH * (epochs - 1) // last_epoch)
    plan = (tile, sky, blocks, block, epochs, runs)
    few = EDGE * runs < LANES and epochs % CHUNK == 0 and epochs >= 2 * CHUNK
    if sky == GRID_X and blocks == 2 and lax.axis_size("vel") == 2 and few:
        plan += (CHUNK,)
        psi_sum, phi_sum = near_stacks(images, variances, valid, psf_sigma, offsets, plan)
    else:
        psi_sum, phi_sum = far_stacks(images, variances, valid, psf_sigma, offsets, plan)
    phi_sum = jnp.maximum(phi_sum, phi_floor)
    likelihood = psi_sum / jnp.sqrt(phi_sum)
    flux = psi_sum / phi_sum
    return (likelihood[:, None], flux[:, None])


def solution(mesh):
    placed = (
        P(("epoch", "vel"), ("field", "sky"), None, None),
        P(("epoch", "vel"), ("field", "sky"), None, None),
        P(("epoch", "vel"), ("field", "sky")),
        P(("field", "epoch", "vel")),
        P(None, None, "epoch"),
    )
    return jax.shard_map(
        on_device,
        mesh=mesh,
        in_specs=placed,
        out_specs=(
            P(("epoch", "vel"), ("field", "sky"), None, None),
            P(("epoch", "vel"), ("field", "sky"), None, None),
        ),
        check_vma=False,
    )
```

```python
import functools

import jax
import jax.numpy as jnp
from jax import lax
from jax.experimental import pallas as pl
from jax.experimental.pallas import tpu as pltpu
from jax.sharding import PartitionSpec as P

VELS = 16
REACH = 12
PSFR = 7
GRID_X = 4
MARGIN = REACH + PSFR
LANES = 128
HEAD = 16
PACK = 16
EDGE = 16
WINDOW = 32
CHUNK = 4
KEPT = 55705600

phi_floor = 0.25


def shifted(block, axis, distance):
    devices = range(lax.axis_size(axis))
    route = [((i - distance) % len(devices), i) for i in devices]
    return lax.ppermute(block, axis, route)


def positions(index, tile):
    return jnp.where(
        index < tile,
        index,
        jnp.where(
            index < tile + MARGIN,
            index - tile - MARGIN,
            jnp.where(index < tile + 2 * MARGIN, index - MARGIN, 4 * tile),
        ),
    )


FAR = -1.0e9


def exponents(distance):
    away = distance.astype(jnp.float32)
    return jnp.where(jnp.abs(distance) <= PSFR, -0.5 * away * away, FAR)


def fused_kernel(plan, *refs):
    tile, sky, blocks, block, epochs, runs = plan
    (offsets, motion, sigmas, own, halo, psi_out, phi_out, plane_a, plane_b, ends, ends_made, ends_sem, row_q,
     own_q, side_q, bands, send_v, recv_v, send_x, recv_x, keep, sv, rv, sx, rx) = refs
    maps = 2
    rows_in = row_q.shape[1]
    rows_out = plane_a.shape[1]
    width = 2 * LANES
    mesh_id = pl.DeviceIdType.MESH
    group = lax.axis_index("epoch")
    member = lax.axis_index("vel")
    partner = 1 - member

    barrier = pltpu.get_barrier_semaphore()
    greeted = 1
    pl.semaphore_signal(barrier, inc=1, device_id={"vel": partner}, device_id_type=mesh_id)
    for a in range(1, blocks):
        peer = lax.rem(group + a, blocks)
        pl.semaphore_signal(barrier, inc=1, device_id={"epoch": peer}, device_id_type=mesh_id)
        greeted += 1
    pl.semaphore_wait(barrier, greeted)

    shape = (rows_out, rows_in)
    row_q[...] = exponents(
        positions(lax.broadcasted_iota(jnp.int32, shape, 1), tile)
        - lax.broadcasted_iota(jnp.int32, shape, 0) + REACH
    )
    shape = (LANES, width)
    held = lax.broadcasted_iota(jnp.int32, shape, 0)
    shifted_out = lax.broadcasted_iota(jnp.int32, shape, 1) - REACH
    own_q[...] = exponents(held - shifted_out)
    side_q[0] = exponents(positions(held + tile, tile) - shifted_out)

    first = member * epochs

    at_epoch = lax.broadcasted_iota(jnp.int32, motion.shape[1:], 1)
    moved = jnp.zeros(motion.shape[1:], jnp.int32)
    for way in range(2):
        start = jnp.where(at_epoch == first, motion[way], 0)
        moved += jnp.abs(motion[way] - jnp.sum(start, axis=1, keepdims=True))
    held_here = (at_epoch >= first) & (at_epoch < first + epochs)
    counted = jnp.zeros(ends_made.shape, jnp.int32)
    at_run = lax.broadcasted_iota(jnp.int32, ends_made.shape, 1)
    for run in range(runs - 1):
        count = jnp.sum((held_here & (moved <= run)).astype(jnp.int32), axis=1, keepdims=True)
        counted = jnp.where(at_run == run, count, counted)
    ends_made[...] = counted
    ends_copy = pltpu.make_async_copy(ends_made, ends, ends_sem)
    ends_copy.start()
    plane_a[:maps] = jnp.zeros_like(plane_a[:maps])
    plane_b[:maps] = jnp.zeros_like(plane_b[:maps])

    def correlate(e, turn):
        sigma = jnp.full((8, LANES), sigmas[e], jnp.float32)
        power = 1.0 / (sigma * sigma)
        tap = lax.broadcasted_iota(jnp.int32, (8, LANES), 1) - PSFR
        norm = jnp.sum(jnp.exp(exponents(tap) * power), axis=1, keepdims=True)
        scale = (1.0 / norm)[:1]
        power = power[:1, :1]

        def both(q):
            profile = jnp.exp(q * power) * scale
            return profile.astype(jnp.bfloat16), (profile * profile).astype(jnp.bfloat16)

        row_bands = both(row_q[...])
        for part, q in enumerate((own_q[...], side_q[0])):
            for m, made in enumerate(both(q)):
                bands[turn, m, part * LANES : (part + 1) * LANES] = made
        for m in range(maps):
            side = halo[e, m]
            held = jnp.concatenate([own[e, m], side], axis=1)
            rows = jnp.dot(row_bands[m], held, preferred_element_type=jnp.float32)
            done = jnp.dot(
                rows.astype(jnp.bfloat16), bands[turn, m], preferred_element_type=jnp.float32
            )
            at = maps * e + m
            plane_a[at + maps] = plane_a[at] + done[:, :LANES]
            plane_b[at + maps] = plane_b[at] + done[:, LANES:]

    step = 2 if epochs % 2 == 0 else 1

    def several(i, carry):
        for turn in range(step):
            correlate(step * i + turn, turn)
        return carry

    lax.fori_loop(0, epochs // step, several, 0)

    def vel_copy(at):
        return pltpu.make_async_remote_copy(
            src_ref=send_v.at[at], dst_ref=recv_v.at[at], send_sem=sv.at[at], recv_sem=rv.at[at],
            device_id={"vel": partner}, device_id_type=mesh_id,
        )

    def epoch_copy(at):
        peer = lax.rem(group + 1 + at // block, blocks)
        return pltpu.make_async_remote_copy(
            src_ref=send_x.at[at], dst_ref=recv_x.at[at], send_sem=sx.at[at], recv_sem=rx.at[at],
            device_id={"epoch": peer}, device_id_type=mesh_id,
        )

    def stack(slot, carry):
        a = blocks - 1 - slot // (2 * block)
        turn = lax.rem(slot, 2 * block)
        mine = ((turn > 0) & (lax.rem(turn, 2) == 0)) | (turn == 2 * block - 1)
        b = jnp.where(mine, 0, 1)
        j = jnp.where(turn == 2 * block - 1, block - 1, jnp.where(mine, turn // 2 - 1, (turn + 1) // 2))
        place = a * block + j
        k = (lax.rem(group + a, blocks) * 2 + lax.rem(member + b, 2)) * block + j
        lane = lax.broadcasted_iota(jnp.int32, (tile, LANES), 1)
        summed = [jnp.zeros((tile, LANES), jnp.float32) for _ in range(maps)]
        low = jnp.zeros((), jnp.int32)
        for run in range(runs):
            high = ends[k, run] if run < runs - 1 else epochs
            at = first + jnp.minimum(low, epochs - 1)
            down = offsets[0, k, at] + REACH
            right = offsets[1, k, at] + REACH
            rows = pl.ds(down, tile)
            for m in range(maps):
                left_part = plane_a[maps * high + m, rows, :] - plane_a[maps * low + m, rows, :]
                right_part = plane_b[maps * high + m, rows, :] - plane_b[maps * low + m, rows, :]
                merged = jnp.where(lane >= right, left_part, right_part)
                summed[m] += pltpu.roll(merged, LANES - right, axis=1)
            low = high
        for m in range(maps):
            keep[b, j, m] = summed[m]

        @pl.when(b == 1)
        def _():
            send_v[place] = keep[1, j].astype(jnp.bfloat16)
            vel_copy(place).start()

        @pl.when(b == 0)
        def _():
            vel_copy(place).wait_recv()
            keep[0, j] = keep[0, j] + recv_v[place].astype(jnp.float32)

            @pl.when(a > 0)
            def _():
                send_x[place - block] = keep[0, j].astype(jnp.bfloat16)
                epoch_copy(place - block).start()

        return carry

    ends_copy.wait()
    lax.fori_loop(0, 2 * blocks * block, stack, 0)

    def finish(j, carry):
        total = keep[0, j]
        for a in range(1, blocks):
            at = (a - 1) * block + j
            epoch_copy(at).wait_recv()
            total = total + recv_x[at].astype(jnp.float32)
        psi_out[j] = total[0]
        phi_out[j] = total[1]
        return carry

    lax.fori_loop(0, block, finish, 0)

    def drain_v(at, carry):
        vel_copy(at).wait_send()
        return carry

    lax.fori_loop(0, blocks * block, drain_v, 0)

    def drain_x(at, carry):
        epoch_copy(at).wait_send()
        return carry

    lax.fori_loop(0, (blocks - 1) * block, drain_x, 0)


def strips(own, tile_count, tile):
    position = (lax.axis_index("sky") + GRID_X // 2) % tile_count
    column = position % GRID_X
    left = shifted(own[..., tile - MARGIN :], "sky", 1)
    right = shifted(own[..., :MARGIN], "sky", -1)
    left = jnp.where(column > 0, left, jnp.zeros_like(left))
    right = jnp.where(column < GRID_X - 1, right, jnp.zeros_like(right))
    blank = jnp.zeros(own.shape[:3] + (LANES - 2 * MARGIN,), jnp.bfloat16)
    both = jnp.concatenate([own, left, right, blank], axis=3)
    upper = shifted(both[:, :, tile - MARGIN :], "sky", GRID_X)
    lower = shifted(both[:, :, :MARGIN], "sky", -GRID_X)
    upper = jnp.where(position >= GRID_X, upper, jnp.zeros_like(upper))
    lower = jnp.where(position < tile_count - GRID_X, lower, jnp.zeros_like(lower))
    blank = jnp.zeros(both.shape[:2] + (LANES - 2 * MARGIN, both.shape[3]), jnp.bfloat16)
    both = jnp.concatenate([both, upper, lower, blank], axis=2)
    return both[..., :tile], both[..., tile:]


def near_kernel(plan, *refs):
    tile, sky, blocks, block, epochs, runs, chunk = plan
    (motion, sigmas, valid, images, variances, psi_out, phi_out, plane, edge, ends, ends_made, ends_sem,
     image, variance, load_sem, shift, edge_shift, unplace, row_q, edge_q, row_bands, edge_bands, columns,
     send_v, recv_v, send_x, recv_x, keep, send_z, recv_z, passed,
     sv, rv, sx, rx, sz, rz, sp, rp) = refs
    maps = 2
    rows_out = row_q.shape[0]
    mesh_id = pl.DeviceIdType.MESH
    me = lax.axis_index("sky")
    group = lax.axis_index("epoch")
    member = lax.axis_index("vel")
    column = lax.rem(lax.rem(me + GRID_X // 2, sky), GRID_X)
    before = lax.rem(me + sky - 1, sky)
    after = lax.rem(me + 1, sky)
    partner = 1 - member
    peer = 1 - group
    has_before = column > 0
    has_after = column < GRID_X - 1

    barrier = pltpu.get_barrier_semaphore()
    pl.semaphore_signal(barrier, inc=1, device_id={"vel": partner}, device_id_type=mesh_id)
    pl.semaphore_signal(barrier, inc=1, device_id={"epoch": peer}, device_id_type=mesh_id)

    @pl.when(has_before)
    def _():
        pl.semaphore_signal(barrier, inc=1, device_id={"sky": before}, device_id_type=mesh_id)

    @pl.when(has_after)
    def _():
        pl.semaphore_signal(barrier, inc=1, device_id={"sky": after}, device_id_type=mesh_id)

    greeted = 2 + jnp.where(has_before, 1, 0) + jnp.where(has_after, 1, 0)

    def load(which, c):
        source, held = ((images, image), (variances, variance))[which]
        span = pl.ds(c * chunk, chunk)
        return pltpu.make_async_copy(source.at[span, 0], held.at[span], load_sem.at[which, c])

    for c in range(epochs // chunk):
        for which in range(2):
            load(which, c).start()

    @pl.when(column == 0)
    def _():
        recv_z[1] = jnp.zeros_like(recv_z[1])
        passed[1] = jnp.zeros_like(passed[1])

    @pl.when(column == GRID_X - 1)
    def _():
        recv_z[0] = jnp.zeros_like(recv_z[0])
        passed[0] = jnp.zeros_like(passed[0])

    def iota(shape, axis):
        return lax.broadcasted_iota(jnp.int32, shape, axis)

    def one_hot(hit):
        return jnp.where(hit, 1.0, 0.0).astype(jnp.bfloat16)

    lane = iota((tile, LANES), 1)
    row = iota((tile, LANES), 0)

    def beyond(lanes):
        outward = lanes & (WINDOW - 1)
        side = jnp.where(lanes < 2 * WINDOW, outward - MARGIN, outward + tile)
        return jnp.where(outward < MARGIN, side, 8 * tile)

    def edge_column(lanes):
        index = (lanes & (EDGE - 1)) - EDGE // 2
        held = (index >= -PSFR) & (index < PSFR)
        return jnp.where(held, jnp.where(index < 0, index, index + tile), 4 * tile)

    short = iota((EDGE, LANES), 1)
    from_edge = edge_column(iota((EDGE, LANES), 0))

    outward = row - beyond(lane)
    moves = (row - lane, outward[:WINDOW], outward[tile - PACK :], from_edge - short, from_edge - beyond(short))

    def make_shift(at, carry):
        right = at - REACH
        shift[at, :, :LANES] = one_hot(moves[0] == right)
        shift[at, :WINDOW, LANES:] = one_hot(moves[1] == right)
        shift[at, WINDOW : tile - PACK, LANES:] = jnp.zeros((tile - PACK - WINDOW, LANES), jnp.bfloat16)
        shift[at, tile - PACK :, LANES:] = one_hot(moves[2] == right)
        edge_shift[at, :, :LANES] = one_hot(moves[3] == right)
        edge_shift[at, :, LANES:] = one_hot(moves[4] == right)
        return carry

    lax.fori_loop(0, 2 * REACH + 1, make_shift, 0)
    for m in range(maps):
        for bottom in range(2):
            begin = WINDOW * m + 2 * WINDOW * bottom
            inside = (row >= begin) & (row < begin + MARGIN)
            span = slice(bottom * LANES, (bottom + 1) * LANES)
            unplace[m, :tile, span] = one_hot(inside & (lane == row - begin))
            unplace[m, tile:, span] = one_hot(inside & (lane == row - begin + tile - MARGIN))

    row_q[...] = exponents(iota(row_q.shape, 1) - iota(row_q.shape, 0) + HEAD)
    at = iota(edge_q.shape, 0)
    at = jnp.where(at < PACK, at, at + tile - 2 * PACK)
    edge_q[...] = exponents(at - edge_column(iota(edge_q.shape, 1)))

    def make_bands(e):
        sigma = jnp.full((8, LANES), sigmas[e], jnp.float32)
        power = 1.0 / (sigma * sigma)
        tap = iota((8, LANES), 1) - PSFR
        norm = jnp.sum(jnp.exp(exponents(tap) * power), axis=1, keepdims=True)
        scale = (1.0 / norm)[:1]
        power = power[:1, :1]
        for q, bands in ((row_q, row_bands), (edge_q, edge_bands)):
            profile = jnp.exp(q[...] * power) * scale
            bands[e, 0] = profile.astype(jnp.bfloat16)
            bands[e, 1] = (profile * profile).astype(jnp.bfloat16)

    def all_bands(c, carry):
        for turn in range(chunk):
            make_bands(chunk * c + turn)
        return carry

    all_bands(0, 0)

    first = member * epochs
    at_epoch = iota(motion.shape[1:], 1)
    moved = jnp.zeros(motion.shape[1:], jnp.int32)
    for way in range(2):
        start = jnp.where(at_epoch == first, motion[way], 0)
        moved += jnp.abs(motion[way] - jnp.sum(start, axis=1, keepdims=True))
    held_here = (at_epoch >= first) & (at_epoch < first + epochs)
    counted = jnp.zeros(ends_made.shape, jnp.int32)
    at_run = iota(ends_made.shape, 1)
    low = jnp.zeros((VELS, 1), jnp.int32)
    for run in range(runs):
        high = jnp.full((VELS, 1), epochs, jnp.int32)
        if run < runs - 1:
            high = jnp.sum((held_here & (moved <= run)).astype(jnp.int32), axis=1, keepdims=True)
        begins = at_epoch == first + jnp.minimum(low, epochs - 1)
        down = jnp.sum(jnp.where(begins, motion[0], 0), axis=1, keepdims=True) + HEAD
        right = jnp.sum(jnp.where(begins, motion[1], 0), axis=1, keepdims=True) + REACH
        entries = (
            maps * rows_out * high + down, maps * rows_out * low + down,
            rows_out * high + down, rows_out * low + down, right,
        )
        for which, entry in enumerate(entries):
            counted = jnp.where(at_run == EDGE * which + run, entry, counted)
        low = high
    ends_made[...] = counted
    ends_copy = pltpu.make_async_copy(ends_made, ends, ends_sem)
    ends_copy.start()
    plane[: maps * rows_out] = jnp.zeros((maps * rows_out, LANES), jnp.float32)
    edge[:rows_out] = jnp.zeros((rows_out, LANES), jnp.float32)

    lax.fori_loop(1, epochs // chunk, all_bands, 0)

    def across(e):
        usable = valid[e].astype(jnp.float32)
        inverse = usable / variance[e].astype(jnp.float32)
        scaled = image[e].astype(jnp.float32) * inverse
        blank = jnp.zeros((tile - 2 * PACK, LANES), jnp.bfloat16)
        for m, field in enumerate((scaled, inverse)):
            rims = jnp.concatenate([edge_bands[e, m, :PACK], blank, edge_bands[e, m, PACK:]], axis=0)
            bands = jnp.concatenate([row_bands[e, m, HEAD : HEAD + tile], rims], axis=1)
            done = jnp.dot(field.astype(jnp.bfloat16), bands, preferred_element_type=jnp.float32)
            columns[e, m] = done.astype(jnp.bfloat16)

    own_half = iota((rows_out, LANES), 1) < LANES // 2

    def down(e):
        rims = []
        for m in range(maps):
            done = jnp.dot(row_bands[e, m], columns[e, m], preferred_element_type=jnp.float32)
            begin = pl.multiple_of((maps * e + m) * rows_out, 8)
            ends_at = pl.multiple_of((maps * e + m + maps) * rows_out, 8)
            plane[pl.ds(ends_at, rows_out)] = plane[pl.ds(begin, rows_out)] + done[:, :LANES]
            rims.append(done[:, LANES:])
        begin = pl.multiple_of(e * rows_out, 8)
        ends_at = pl.multiple_of((e + 1) * rows_out, 8)
        edge[pl.ds(ends_at, rows_out)] = edge[pl.ds(begin, rows_out)] + jnp.where(own_half, rims[0], rims[1])

    def arrive(c):
        for which in range(2):
            load(which, c).wait()

    def all_across(c):
        for turn in range(chunk):
            across(chunk * c + turn)

    def all_down(c):
        for turn in range(chunk):
            down(chunk * c + turn)

    def both_ways(c, carry):
        arrive(c)
        all_down(c - 1)
        all_across(c)
        return carry

    chunks = epochs // chunk
    arrive(0)
    all_across(0)
    lax.fori_loop(1, chunks, both_ways, 0)
    all_down(chunks - 1)

    def vel_copy(at):
        return pltpu.make_async_remote_copy(
            src_ref=send_v.at[at], dst_ref=recv_v.at[at], send_sem=sv, recv_sem=rv.at[at],
            device_id={"vel": partner}, device_id_type=mesh_id,
        )

    def epoch_copy(at):
        return pltpu.make_async_remote_copy(
            src_ref=send_x.at[at], dst_ref=recv_x.at[at], send_sem=sx, recv_sem=rx.at[at],
            device_id={"epoch": peer}, device_id_type=mesh_id,
        )

    def side_copy(to_after, at):
        return pltpu.make_async_remote_copy(
            src_ref=send_z.at[to_after, at], dst_ref=recv_z.at[to_after, at],
            send_sem=sz.at[to_after], recv_sem=rz.at[to_after, at],
            device_id={"sky": after if to_after else before}, device_id_type=mesh_id,
        )

    def pass_copy(to_after, at):
        return pltpu.make_async_remote_copy(
            src_ref=recv_z.at[to_after, block + at], dst_ref=passed.at[to_after, at],
            send_sem=sp.at[to_after], recv_sem=rp.at[to_after, at],
            device_id={"epoch": peer}, device_id_type=mesh_id,
        )

    each = LANES // (maps * EDGE)
    part = (lane // EDGE) & (each - 1)
    low_half = lane < LANES // 2
    first_window = (lane & WINDOW) == 0

    def stacked(k):
        summed = jnp.zeros((maps * tile, 2 * LANES), jnp.float32)
        rims = [jnp.zeros((tile, LANES), jnp.float32) for _ in range(2)]
        lefts, rights, rim_rights = [], [], []
        for run in range(runs):
            high, low, rim_high, rim_low, right = (ends[k, EDGE * which + run] for which in range(5))
            rim = edge[pl.ds(rim_high, tile), :]
            if run > 0:
                rim = rim - edge[pl.ds(rim_low, tile), :]
            rims[run // each] = jnp.where(part == run % each, rim, rims[run // each])
            pieces = []
            for m in range(maps):
                piece = plane[pl.ds(high + m * rows_out, tile), :]
                if run > 0:
                    piece = piece - plane[pl.ds(low + m * rows_out, tile), :]
                pieces.append(piece.astype(jnp.bfloat16))
            lefts.append(jnp.concatenate(pieces, axis=0))
            rights.append(shift[right])
            rim_rights.append(edge_shift[right])
        turned = [pltpu.roll(rim, LANES // 2, axis=1) for rim in rims]
        spread = (jnp.where(low_half, rims[0], turned[1]), jnp.where(low_half, turned[0], rims[1]))
        lefts.append(jnp.concatenate([rim.astype(jnp.bfloat16) for rim in spread], axis=0))
        spare = jnp.zeros((LANES - EDGE * runs, 2 * LANES), jnp.bfloat16)
        rights.append(jnp.concatenate(rim_rights + [spare], axis=0))
        for run in range(0, len(lefts), 2):
            summed += jnp.dot(
                jnp.concatenate(lefts[run : run + 2], axis=1), jnp.concatenate(rights[run : run + 2], axis=0),
                preferred_element_type=jnp.float32,
            )
        outer = jnp.where(first_window, summed[:tile, LANES:], summed[tile:, LANES:])
        return summed[:tile, :LANES], summed[tile:, :LANES], outer

    def spot_of(turn):
        late = turn == 2 * block - 1
        near = ((turn > 0) & (lax.rem(turn, 2) == 0)) | late
        return jnp.where(late, block - 1, jnp.where(near, turn // 2 - 1, block + (turn + 1) // 2))

    def owner_of(turn):
        return lax.rem(group + spot_of(turn) // block, blocks) * 2

    def theirs(turn):
        return stacked((owner_of(turn) + partner) * block + lax.rem(spot_of(turn), block))

    def ours(turn):
        return stacked((owner_of(turn) + member) * block + lax.rem(spot_of(turn), block))

    def hand_over(turn, parts):
        spot = spot_of(turn)
        for m in range(maps + 1):
            send_v[spot, m] = parts[m].astype(jnp.bfloat16)
        vel_copy(spot).start()

    def finish(turn, parts):
        spot = spot_of(turn)
        j = lax.rem(spot_of(turn), block)
        vel_copy(spot).wait_recv()
        totals = [parts[m] + recv_v[spot, m].astype(jnp.float32) for m in range(maps + 1)]
        upper, lower = totals[maps][: tile // 2], totals[maps][tile // 2 :]
        to_left = low_half[: tile // 2]
        send_z[0, spot] = jnp.where(to_left, upper, pltpu.roll(lower, LANES // 2, axis=1)).astype(jnp.bfloat16)
        send_z[1, spot] = jnp.where(to_left, pltpu.roll(upper, LANES // 2, axis=1), lower).astype(jnp.bfloat16)

        @pl.when(has_before)
        def _():
            side_copy(0, spot).start()

        @pl.when(has_after)
        def _():
            side_copy(1, spot).start()

        @pl.when(spot >= block)
        def _():
            for m in range(maps):
                send_x[j, m] = totals[m].astype(jnp.bfloat16)
            epoch_copy(j).start()

        @pl.when(spot < block)
        def _():
            for m in range(maps):
                keep[j, m] = totals[m]

    last = blocks * block - 1

    def stack(turn, carry):
        ahead = theirs(turn + 1)
        kept = ours(turn)
        hand_over(turn + 1, ahead)
        finish(turn, kept)
        return carry

    ends_copy.wait()
    ahead = theirs(0)
    pl.semaphore_wait(barrier, greeted)
    hand_over(0, ahead)
    lax.fori_loop(0, last, stack, 0)
    finish(last, ours(last))

    def hand_on(at, carry):
        @pl.when(has_before)
        def _():
            side_copy(1, block + at).wait_recv()
            pass_copy(1, at).start()

        @pl.when(has_after)
        def _():
            side_copy(0, block + at).wait_recv()
            pass_copy(0, at).start()

        return carry

    lax.fori_loop(0, block, hand_on, 0)

    pltpu.make_async_remote_copy(
        src_ref=send_v, dst_ref=recv_v, send_sem=sv, recv_sem=rv.at[0],
        device_id={"vel": partner}, device_id_type=mesh_id,
    ).wait_send()
    pltpu.make_async_remote_copy(
        src_ref=send_x, dst_ref=recv_x, send_sem=sx, recv_sem=rx.at[0],
        device_id={"epoch": peer}, device_id_type=mesh_id,
    ).wait_send()

    def sent_side(to_after):
        pltpu.make_async_remote_copy(
            src_ref=send_z.at[to_after], dst_ref=recv_z.at[to_after],
            send_sem=sz.at[to_after], recv_sem=rz.at[to_after, 0],
            device_id={"sky": after if to_after else before}, device_id_type=mesh_id,
        ).wait_send()

    def sent_on(to_after):
        pltpu.make_async_remote_copy(
            src_ref=recv_z.at[to_after, pl.ds(block, block)], dst_ref=passed.at[to_after],
            send_sem=sp.at[to_after], recv_sem=rp.at[to_after, 0],
            device_id={"epoch": peer}, device_id_type=mesh_id,
        ).wait_send()

    @pl.when(has_before)
    def _():
        sent_side(0)

    @pl.when(has_after)
    def _():
        sent_side(1)

    def assemble(j, carry):
        epoch_copy(j).wait_recv()

        @pl.when(has_before)
        def _():
            pass_copy(1, j).wait_recv()
            side_copy(1, j).wait_recv()

        @pl.when(has_after)
        def _():
            pass_copy(0, j).wait_recv()
            side_copy(0, j).wait_recv()

        strips_in = jnp.concatenate([recv_z[1, j], recv_z[0, j], passed[1, j], passed[0, j]], axis=1)
        for m, out in enumerate((psi_out, phi_out)):
            added = jnp.dot(
                strips_in, jnp.concatenate([unplace[m]] * 2, axis=0), preferred_element_type=jnp.float32
            )
            for bottom in range(2):
                span = slice(bottom * tile // 2, (bottom + 1) * tile // 2)
                out[j, span] = (
                    keep[j, m, span] + recv_x[j, m, span].astype(jnp.float32)
                    + added[:, bottom * LANES : (bottom + 1) * LANES]
                )
        return carry

    lax.fori_loop(0, block, assemble, 0)

    @pl.when(has_before)
    def _():
        sent_on(1)

    @pl.when(has_after)
    def _():
        sent_on(0)


def near_stacks(images, variances, valid, psf_sigma, offsets, plan):
    tile, sky, blocks, block, epochs, runs, chunk = plan
    rows_out = tile + 2 * HEAD
    smem = pl.BlockSpec(memory_space=pltpu.SMEM)
    vmem = pl.BlockSpec(memory_space=pltpu.VMEM)
    anywhere = pl.BlockSpec(memory_space=pl.ANY)
    dma = pltpu.SemaphoreType.DMA
    half = blocks * block
    narrow, wide = jnp.bfloat16, jnp.float32
    scratch = [
        pltpu.VMEM((2 * (epochs + 1) * rows_out, LANES), wide),
        pltpu.VMEM(((epochs + 1) * rows_out, LANES), wide),
        pltpu.SMEM((VELS, LANES), jnp.int32),
        pltpu.VMEM((VELS, LANES), jnp.int32),
        dma(()),
        pltpu.VMEM((epochs, tile, tile), narrow),
        pltpu.VMEM((epochs, tile, tile), narrow),
        dma((2, epochs // chunk)),
        pltpu.VMEM((2 * REACH + 1, tile, 2 * LANES), narrow),
        pltpu.VMEM((2 * REACH + 1, EDGE, 2 * LANES), narrow),
        pltpu.VMEM((2, 2 * tile, 2 * LANES), narrow),
        pltpu.VMEM((rows_out, tile), wide),
        pltpu.VMEM((2 * PACK, LANES), wide),
        pltpu.VMEM((epochs, 2, rows_out, tile), narrow),
        pltpu.VMEM((epochs, 2, 2 * PACK, LANES), narrow),
        pltpu.VMEM((epochs, 2, tile, 2 * LANES), narrow),
        pltpu.VMEM((half, 3, tile, tile), narrow),
        pltpu.VMEM((half, 3, tile, tile), narrow),
        pltpu.VMEM((block, 2, tile, tile), narrow),
        pltpu.VMEM((block, 2, tile, tile), narrow),
        pltpu.VMEM((block, 2, tile, tile), wide),
        pltpu.VMEM((2, half, tile // 2, LANES), narrow),
        pltpu.VMEM((2, half, tile // 2, LANES), narrow),
        pltpu.VMEM((2, block, tile // 2, LANES), narrow),
        dma(()), dma((half,)), dma(()), dma((block,)),
        dma((2,)), dma((2, half)), dma((2,)), dma((2, block)),
    ]
    out = jax.ShapeDtypeStruct((block, tile, tile), jnp.float32)
    return pl.pallas_call(
        functools.partial(near_kernel, plan),
        out_shape=(out, out),
        in_specs=[vmem, smem, smem, anywhere, anywhere],
        out_specs=(vmem, vmem),
        scratch_shapes=scratch,
        compiler_params=pltpu.CompilerParams(
            collective_id=0, has_side_effects=True, vmem_limit_bytes=KEPT
        ),
    )(offsets, psf_sigma, valid.reshape(epochs), images, variances)


def far_stacks(images, variances, valid, psf_sigma, offsets, plan):
    tile, sky, blocks, block, epochs, runs = plan
    rows_out = -(-(tile + 2 * REACH) // 16) * 16
    smem = pl.BlockSpec(memory_space=pltpu.SMEM)
    vmem = pl.BlockSpec(memory_space=pltpu.VMEM)
    dma = pltpu.SemaphoreType.DMA
    half = blocks * block
    far = max(1, (blocks - 1) * block)
    scratch = [
        pltpu.VMEM((2 * (epochs + 1), rows_out, LANES), jnp.float32),
        pltpu.VMEM((2 * (epochs + 1), rows_out, LANES), jnp.float32),
        pltpu.SMEM((VELS, LANES), jnp.int32),
        pltpu.VMEM((VELS, LANES), jnp.int32),
        dma(()),
        pltpu.VMEM((rows_out, tile + LANES), jnp.float32),
        pltpu.VMEM((LANES, 2 * LANES), jnp.float32),
        pltpu.VMEM((1, LANES, 2 * LANES), jnp.float32),
        pltpu.VMEM((2, 2, 2 * LANES, 2 * LANES), jnp.bfloat16),
        pltpu.VMEM((half, 2, tile, tile), jnp.bfloat16),
        pltpu.VMEM((half, 2, tile, tile), jnp.bfloat16),
        pltpu.VMEM((far, 2, tile, tile), jnp.bfloat16),
        pltpu.VMEM((far, 2, tile, tile), jnp.bfloat16),
        pltpu.VMEM((2, block, 2, tile, tile), jnp.float32),
        dma((half,)), dma((half,)), dma((far,)), dma((far,)),
    ]
    usable = valid[:, 0].astype(jnp.float32)[:, None, None]
    inverse = usable / variances[:, 0].astype(jnp.float32)
    scaled = images[:, 0].astype(jnp.float32) * inverse
    own = jnp.stack([scaled.astype(jnp.bfloat16), inverse.astype(jnp.bfloat16)], axis=1)
    out = jax.ShapeDtypeStruct((block, tile, tile), jnp.float32)
    return pl.pallas_call(
        functools.partial(fused_kernel, plan),
        out_shape=(out, out),
        in_specs=[smem, vmem, smem, vmem, vmem],
        out_specs=(vmem, vmem),
        scratch_shapes=scratch,
        compiler_params=pltpu.CompilerParams(
            collective_id=0, has_side_effects=True, vmem_limit_bytes=56 * 2**20
        ),
    )(offsets, offsets, psf_sigma, *strips(own, sky, tile))


def on_device(images, variances, valid, psf_sigma, offsets):
    epochs = images.shape[0]
    tile = images.shape[-1]
    sky = lax.axis_size("sky")
    blocks = lax.axis_size("epoch")
    block = VELS // (blocks * lax.axis_size("vel"))
    last_epoch = epochs * blocks * lax.axis_size("vel") - 1
    runs = 1 + 2 * -(-REACH * (epochs - 1) // last_epoch)
    plan = (tile, sky, blocks, block, epochs, runs)
    few = EDGE * runs < LANES and epochs % CHUNK == 0
    if sky == GRID_X and blocks == 2 and lax.axis_size("vel") == 2 and few:
        plan += (CHUNK,)
        psi_sum, phi_sum = near_stacks(images, variances, valid, psf_sigma, offsets, plan)
    else:
        psi_sum, phi_sum = far_stacks(images, variances, valid, psf_sigma, offsets, plan)
    phi_sum = jnp.maximum(phi_sum, phi_floor)
    likelihood = psi_sum / jnp.sqrt(phi_sum)
    flux = psi_sum / phi_sum
    return (likelihood[:, None], flux[:, None])


def solution(mesh):
    placed = (
        P(("epoch", "vel"), ("field", "sky"), None, None),
        P(("epoch", "vel"), ("field", "sky"), None, None),
        P(("epoch", "vel"), ("field", "sky")),
        P(("field", "epoch", "vel")),
        P(None, None, "epoch"),
    )
    return jax.shard_map(
        on_device,
        mesh=mesh,
        in_specs=placed,
        out_specs=(
            P(("epoch", "vel"), ("field", "sky"), None, None),
            P(("epoch", "vel"), ("field", "sky"), None, None),
        ),
        check_vma=False,
    )
```

```python
import functools

import jax
import jax.numpy as jnp
from jax import lax
from jax.experimental import pallas as pl
from jax.experimental.pallas import tpu as pltpu
from jax.sharding import PartitionSpec as P

VELS = 16
REACH = 12
PSFR = 7
GRID_X = 4
MARGIN = REACH + PSFR
LANES = 128
HEAD = 16
PACK = 16
EDGE = 16
WINDOW = 32
CHUNK = 4
KEPT = 55705600

phi_floor = 0.25


def shifted(block, axis, distance):
    devices = range(lax.axis_size(axis))
    route = [((i - distance) % len(devices), i) for i in devices]
    return lax.ppermute(block, axis, route)


def positions(index, tile):
    return jnp.where(
        index < tile,
        index,
        jnp.where(
            index < tile + MARGIN,
            index - tile - MARGIN,
            jnp.where(index < tile + 2 * MARGIN, index - MARGIN, 4 * tile),
        ),
    )


FAR = -1.0e9


def exponents(distance):
    away = distance.astype(jnp.float32)
    return jnp.where(jnp.abs(distance) <= PSFR, -0.5 * away * away, FAR)


def fused_kernel(plan, *refs):
    tile, sky, blocks, block, epochs, runs = plan
    (offsets, motion, sigmas, own, halo, psi_out, phi_out, plane_a, plane_b, ends, ends_made, ends_sem, row_q,
     own_q, side_q, bands, send_v, recv_v, send_x, recv_x, keep, sv, rv, sx, rx) = refs
    maps = 2
    rows_in = row_q.shape[1]
    rows_out = plane_a.shape[1]
    width = 2 * LANES
    mesh_id = pl.DeviceIdType.MESH
    group = lax.axis_index("epoch")
    member = lax.axis_index("vel")
    partner = 1 - member

    barrier = pltpu.get_barrier_semaphore()
    greeted = 1
    pl.semaphore_signal(barrier, inc=1, device_id={"vel": partner}, device_id_type=mesh_id)
    for a in range(1, blocks):
        peer = lax.rem(group + a, blocks)
        pl.semaphore_signal(barrier, inc=1, device_id={"epoch": peer}, device_id_type=mesh_id)
        greeted += 1
    pl.semaphore_wait(barrier, greeted)

    shape = (rows_out, rows_in)
    row_q[...] = exponents(
        positions(lax.broadcasted_iota(jnp.int32, shape, 1), tile)
        - lax.broadcasted_iota(jnp.int32, shape, 0) + REACH
    )
    shape = (LANES, width)
    held = lax.broadcasted_iota(jnp.int32, shape, 0)
    shifted_out = lax.broadcasted_iota(jnp.int32, shape, 1) - REACH
    own_q[...] = exponents(held - shifted_out)
    side_q[0] = exponents(positions(held + tile, tile) - shifted_out)

    first = member * epochs

    at_epoch = lax.broadcasted_iota(jnp.int32, motion.shape[1:], 1)
    moved = jnp.zeros(motion.shape[1:], jnp.int32)
    for way in range(2):
        start = jnp.where(at_epoch == first, motion[way], 0)
        moved += jnp.abs(motion[way] - jnp.sum(start, axis=1, keepdims=True))
    held_here = (at_epoch >= first) & (at_epoch < first + epochs)
    counted = jnp.zeros(ends_made.shape, jnp.int32)
    at_run = lax.broadcasted_iota(jnp.int32, ends_made.shape, 1)
    for run in range(runs - 1):
        count = jnp.sum((held_here & (moved <= run)).astype(jnp.int32), axis=1, keepdims=True)
        counted = jnp.where(at_run == run, count, counted)
    ends_made[...] = counted
    ends_copy = pltpu.make_async_copy(ends_made, ends, ends_sem)
    ends_copy.start()
    plane_a[:maps] = jnp.zeros_like(plane_a[:maps])
    plane_b[:maps] = jnp.zeros_like(plane_b[:maps])

    def correlate(e, turn):
        sigma = jnp.full((8, LANES), sigmas[e], jnp.float32)
        power = 1.0 / (sigma * sigma)
        tap = lax.broadcasted_iota(jnp.int32, (8, LANES), 1) - PSFR
        norm = jnp.sum(jnp.exp(exponents(tap) * power), axis=1, keepdims=True)
        scale = (1.0 / norm)[:1]
        power = power[:1, :1]

        def both(q):
            profile = jnp.exp(q * power) * scale
            return profile.astype(jnp.bfloat16), (profile * profile).astype(jnp.bfloat16)

        row_bands = both(row_q[...])
        for part, q in enumerate((own_q[...], side_q[0])):
            for m, made in enumerate(both(q)):
                bands[turn, m, part * LANES : (part + 1) * LANES] = made
        for m in range(maps):
            side = halo[e, m]
            held = jnp.concatenate([own[e, m], side], axis=1)
            rows = jnp.dot(row_bands[m], held, preferred_element_type=jnp.float32)
            done = jnp.dot(
                rows.astype(jnp.bfloat16), bands[turn, m], preferred_element_type=jnp.float32
            )
            at = maps * e + m
            plane_a[at + maps] = plane_a[at] + done[:, :LANES]
            plane_b[at + maps] = plane_b[at] + done[:, LANES:]

    step = 2 if epochs % 2 == 0 else 1

    def several(i, carry):
        for turn in range(step):
            correlate(step * i + turn, turn)
        return carry

    lax.fori_loop(0, epochs // step, several, 0)

    def vel_copy(at):
        return pltpu.make_async_remote_copy(
            src_ref=send_v.at[at], dst_ref=recv_v.at[at], send_sem=sv.at[at], recv_sem=rv.at[at],
            device_id={"vel": partner}, device_id_type=mesh_id,
        )

    def epoch_copy(at):
        peer = lax.rem(group + 1 + at // block, blocks)
        return pltpu.make_async_remote_copy(
            src_ref=send_x.at[at], dst_ref=recv_x.at[at], send_sem=sx.at[at], recv_sem=rx.at[at],
            device_id={"epoch": peer}, device_id_type=mesh_id,
        )

    def stack(slot, carry):
        a = blocks - 1 - slot // (2 * block)
        turn = lax.rem(slot, 2 * block)
        mine = ((turn > 0) & (lax.rem(turn, 2) == 0)) | (turn == 2 * block - 1)
        b = jnp.where(mine, 0, 1)
        j = jnp.where(turn == 2 * block - 1, block - 1, jnp.where(mine, turn // 2 - 1, (turn + 1) // 2))
        place = a * block + j
        k = (lax.rem(group + a, blocks) * 2 + lax.rem(member + b, 2)) * block + j
        lane = lax.broadcasted_iota(jnp.int32, (tile, LANES), 1)
        summed = [jnp.zeros((tile, LANES), jnp.float32) for _ in range(maps)]
        low = jnp.zeros((), jnp.int32)
        for run in range(runs):
            high = ends[k, run] if run < runs - 1 else epochs
            at = first + jnp.minimum(low, epochs - 1)
            down = offsets[0, k, at] + REACH
            right = offsets[1, k, at] + REACH
            rows = pl.ds(down, tile)
            for m in range(maps):
                left_part = plane_a[maps * high + m, rows, :] - plane_a[maps * low + m, rows, :]
                right_part = plane_b[maps * high + m, rows, :] - plane_b[maps * low + m, rows, :]
                merged = jnp.where(lane >= right, left_part, right_part)
                summed[m] += pltpu.roll(merged, LANES - right, axis=1)
            low = high
        for m in range(maps):
            keep[b, j, m] = summed[m]

        @pl.when(b == 1)
        def _():
            send_v[place] = keep[1, j].astype(jnp.bfloat16)
            vel_copy(place).start()

        @pl.when(b == 0)
        def _():
            vel_copy(place).wait_recv()
            keep[0, j] = keep[0, j] + recv_v[place].astype(jnp.float32)

            @pl.when(a > 0)
            def _():
                send_x[place - block] = keep[0, j].astype(jnp.bfloat16)
                epoch_copy(place - block).start()

        return carry

    ends_copy.wait()
    lax.fori_loop(0, 2 * blocks * block, stack, 0)

    def finish(j, carry):
        total = keep[0, j]
        for a in range(1, blocks):
            at = (a - 1) * block + j
            epoch_copy(at).wait_recv()
            total = total + recv_x[at].astype(jnp.float32)
        psi_out[j] = total[0]
        phi_out[j] = total[1]
        return carry

    lax.fori_loop(0, block, finish, 0)

    def drain_v(at, carry):
        vel_copy(at).wait_send()
        return carry

    lax.fori_loop(0, blocks * block, drain_v, 0)

    def drain_x(at, carry):
        epoch_copy(at).wait_send()
        return carry

    lax.fori_loop(0, (blocks - 1) * block, drain_x, 0)


def strips(own, tile_count, tile):
    position = (lax.axis_index("sky") + GRID_X // 2) % tile_count
    column = position % GRID_X
    left = shifted(own[..., tile - MARGIN :], "sky", 1)
    right = shifted(own[..., :MARGIN], "sky", -1)
    left = jnp.where(column > 0, left, jnp.zeros_like(left))
    right = jnp.where(column < GRID_X - 1, right, jnp.zeros_like(right))
    blank = jnp.zeros(own.shape[:3] + (LANES - 2 * MARGIN,), jnp.bfloat16)
    both = jnp.concatenate([own, left, right, blank], axis=3)
    upper = shifted(both[:, :, tile - MARGIN :], "sky", GRID_X)
    lower = shifted(both[:, :, :MARGIN], "sky", -GRID_X)
    upper = jnp.where(position >= GRID_X, upper, jnp.zeros_like(upper))
    lower = jnp.where(position < tile_count - GRID_X, lower, jnp.zeros_like(lower))
    blank = jnp.zeros(both.shape[:2] + (LANES - 2 * MARGIN, both.shape[3]), jnp.bfloat16)
    both = jnp.concatenate([both, upper, lower, blank], axis=2)
    return both[..., :tile], both[..., tile:]


def near_kernel(plan, *refs):
    tile, sky, blocks, block, epochs, runs, chunk = plan
    (motion, sigmas, valid, images, variances, psi_out, phi_out, plane, edge, ends, ends_made, ends_sem,
     image, variance, load_sem, shift, edge_shift, unplace, row_q, edge_q, row_bands, edge_bands, columns,
     send_v, recv_v, send_x, recv_x, keep, send_z, recv_z, passed,
     sv, rv, sx, rx, sz, rz, sp, rp) = refs
    maps = 2
    rows_out = row_q.shape[0]
    mesh_id = pl.DeviceIdType.MESH
    me = lax.axis_index("sky")
    group = lax.axis_index("epoch")
    member = lax.axis_index("vel")
    column = lax.rem(lax.rem(me + GRID_X // 2, sky), GRID_X)
    before = lax.rem(me + sky - 1, sky)
    after = lax.rem(me + 1, sky)
    partner = 1 - member
    peer = 1 - group
    has_before = column > 0
    has_after = column < GRID_X - 1

    barrier = pltpu.get_barrier_semaphore()
    pl.semaphore_signal(barrier, inc=1, device_id={"vel": partner}, device_id_type=mesh_id)
    pl.semaphore_signal(barrier, inc=1, device_id={"epoch": peer}, device_id_type=mesh_id)

    @pl.when(has_before)
    def _():
        pl.semaphore_signal(barrier, inc=1, device_id={"sky": before}, device_id_type=mesh_id)

    @pl.when(has_after)
    def _():
        pl.semaphore_signal(barrier, inc=1, device_id={"sky": after}, device_id_type=mesh_id)

    greeted = 2 + jnp.where(has_before, 1, 0) + jnp.where(has_after, 1, 0)

    def load(which, c):
        source, held = ((images, image), (variances, variance))[which]
        span = pl.ds(c * chunk, chunk)
        return pltpu.make_async_copy(source.at[span, 0], held.at[span], load_sem.at[which, c])

    for c in range(epochs // chunk):
        for which in range(2):
            load(which, c).start()

    @pl.when(column == 0)
    def _():
        recv_z[1] = jnp.zeros_like(recv_z[1])
        passed[1] = jnp.zeros_like(passed[1])

    @pl.when(column == GRID_X - 1)
    def _():
        recv_z[0] = jnp.zeros_like(recv_z[0])
        passed[0] = jnp.zeros_like(passed[0])

    def iota(shape, axis):
        return lax.broadcasted_iota(jnp.int32, shape, axis)

    def one_hot(hit):
        return jnp.where(hit, 1.0, 0.0).astype(jnp.bfloat16)

    lane = iota((tile, LANES), 1)
    row = iota((tile, LANES), 0)

    def beyond(lanes):
        outward = lanes & (WINDOW - 1)
        side = jnp.where(lanes < 2 * WINDOW, outward - MARGIN, outward + tile)
        return jnp.where(outward < MARGIN, side, 8 * tile)

    def edge_column(lanes):
        index = (lanes & (EDGE - 1)) - EDGE // 2
        held = (index >= -PSFR) & (index < PSFR)
        return jnp.where(held, jnp.where(index < 0, index, index + tile), 4 * tile)

    short = iota((EDGE, LANES), 1)
    from_edge = edge_column(iota((EDGE, LANES), 0))

    outward = row - beyond(lane)
    moves = (row - lane, outward[:WINDOW], outward[tile - PACK :], from_edge - short, from_edge - beyond(short))

    def make_shift(at, carry):
        right = at - REACH
        shift[at, :, :LANES] = one_hot(moves[0] == right)
        shift[at, :WINDOW, LANES:] = one_hot(moves[1] == right)
        shift[at, WINDOW : tile - PACK, LANES:] = jnp.zeros((tile - PACK - WINDOW, LANES), jnp.bfloat16)
        shift[at, tile - PACK :, LANES:] = one_hot(moves[2] == right)
        edge_shift[at, :, :LANES] = one_hot(moves[3] == right)
        edge_shift[at, :, LANES:] = one_hot(moves[4] == right)
        return carry

    lax.fori_loop(0, 2 * REACH + 1, make_shift, 0)
    for m in range(maps):
        for bottom in range(2):
            begin = WINDOW * m + 2 * WINDOW * bottom
            inside = (row >= begin) & (row < begin + MARGIN)
            span = slice(bottom * LANES, (bottom + 1) * LANES)
            unplace[m, :tile, span] = one_hot(inside & (lane == row - begin))
            unplace[m, tile:, span] = one_hot(inside & (lane == row - begin + tile - MARGIN))

    row_q[...] = exponents(iota(row_q.shape, 1) - iota(row_q.shape, 0) + HEAD)
    at = iota(edge_q.shape, 0)
    at = jnp.where(at < PACK, at, at + tile - 2 * PACK)
    edge_q[...] = exponents(at - edge_column(iota(edge_q.shape, 1)))

    def make_bands(e):
        sigma = jnp.full((8, LANES), sigmas[e], jnp.float32)
        power = 1.0 / (sigma * sigma)
        tap = iota((8, LANES), 1) - PSFR
        norm = jnp.sum(jnp.exp(exponents(tap) * power), axis=1, keepdims=True)
        scale = (1.0 / norm)[:1]
        power = power[:1, :1]
        for q, bands in ((row_q, row_bands), (edge_q, edge_bands)):
            profile = jnp.exp(q[...] * power) * scale
            bands[e, 0] = profile.astype(jnp.bfloat16)
            bands[e, 1] = (profile * profile).astype(jnp.bfloat16)

    def all_bands(c, carry):
        for turn in range(chunk):
            make_bands(chunk * c + turn)
        return carry

    all_bands(0, 0)

    first = member * epochs
    at_epoch = iota(motion.shape[1:], 1)
    moved = jnp.zeros(motion.shape[1:], jnp.int32)
    for way in range(2):
        start = jnp.where(at_epoch == first, motion[way], 0)
        moved += jnp.abs(motion[way] - jnp.sum(start, axis=1, keepdims=True))
    held_here = (at_epoch >= first) & (at_epoch < first + epochs)
    counted = jnp.zeros(ends_made.shape, jnp.int32)
    at_run = iota(ends_made.shape, 1)
    low = jnp.zeros((VELS, 1), jnp.int32)
    for run in range(runs):
        high = jnp.full((VELS, 1), epochs, jnp.int32)
        if run < runs - 1:
            high = jnp.sum((held_here & (moved <= run)).astype(jnp.int32), axis=1, keepdims=True)
        begins = at_epoch == first + jnp.minimum(low, epochs - 1)
        down = jnp.sum(jnp.where(begins, motion[0], 0), axis=1, keepdims=True) + HEAD
        right = jnp.sum(jnp.where(begins, motion[1], 0), axis=1, keepdims=True) + REACH
        entries = (
            maps * rows_out * high + down, maps * rows_out * low + down,
            rows_out * high + down, rows_out * low + down, right,
        )
        for which, entry in enumerate(entries):
            counted = jnp.where(at_run == EDGE * which + run, entry, counted)
        low = high
    ends_made[...] = counted
    ends_copy = pltpu.make_async_copy(ends_made, ends, ends_sem)
    ends_copy.start()
    plane[: maps * rows_out] = jnp.zeros((maps * rows_out, LANES), jnp.float32)
    edge[:rows_out] = jnp.zeros((rows_out, LANES), jnp.float32)

    lax.fori_loop(1, epochs // chunk, all_bands, 0)

    def across(e):
        usable = valid[e].astype(jnp.float32)
        inverse = usable / variance[e].astype(jnp.float32)
        scaled = image[e].astype(jnp.float32) * inverse
        blank = jnp.zeros((tile - 2 * PACK, LANES), jnp.bfloat16)
        for m, field in enumerate((scaled, inverse)):
            rims = jnp.concatenate([edge_bands[e, m, :PACK], blank, edge_bands[e, m, PACK:]], axis=0)
            bands = jnp.concatenate([row_bands[e, m, HEAD : HEAD + tile], rims], axis=1)
            done = jnp.dot(field.astype(jnp.bfloat16), bands, preferred_element_type=jnp.float32)
            columns[e, m] = done.astype(jnp.bfloat16)

    own_half = iota((rows_out, LANES), 1) < LANES // 2

    def down(e):
        rims = []
        for m in range(maps):
            done = jnp.dot(row_bands[e, m], columns[e, m], preferred_element_type=jnp.float32)
            begin = pl.multiple_of((maps * e + m) * rows_out, 8)
            ends_at = pl.multiple_of((maps * e + m + maps) * rows_out, 8)
            plane[pl.ds(ends_at, rows_out)] = plane[pl.ds(begin, rows_out)] + done[:, :LANES]
            rims.append(done[:, LANES:])
        begin = pl.multiple_of(e * rows_out, 8)
        ends_at = pl.multiple_of((e + 1) * rows_out, 8)
        edge[pl.ds(ends_at, rows_out)] = edge[pl.ds(begin, rows_out)] + jnp.where(own_half, rims[0], rims[1])

    def arrive(c):
        for which in range(2):
            load(which, c).wait()

    def all_across(c):
        for turn in range(chunk):
            across(chunk * c + turn)

    def all_down(c):
        for turn in range(chunk):
            down(chunk * c + turn)

    def both_ways(c, carry):
        arrive(c)
        all_down(c - 1)
        all_across(c)
        return carry

    chunks = epochs // chunk
    arrive(0)
    all_across(0)
    lax.fori_loop(1, chunks, both_ways, 0)
    all_down(chunks - 1)

    def vel_copy(at):
        return pltpu.make_async_remote_copy(
            src_ref=send_v.at[at], dst_ref=recv_v.at[at], send_sem=sv, recv_sem=rv.at[at],
            device_id={"vel": partner}, device_id_type=mesh_id,
        )

    def epoch_copy(at):
        return pltpu.make_async_remote_copy(
            src_ref=send_x.at[at], dst_ref=recv_x.at[at], send_sem=sx, recv_sem=rx.at[at],
            device_id={"epoch": peer}, device_id_type=mesh_id,
        )

    def side_copy(to_after, at):
        return pltpu.make_async_remote_copy(
            src_ref=send_z.at[to_after, at], dst_ref=recv_z.at[to_after, at],
            send_sem=sz.at[to_after], recv_sem=rz.at[to_after, at],
            device_id={"sky": after if to_after else before}, device_id_type=mesh_id,
        )

    def pass_copy(to_after, at):
        return pltpu.make_async_remote_copy(
            src_ref=recv_z.at[to_after, block + at], dst_ref=passed.at[to_after, at],
            send_sem=sp.at[to_after], recv_sem=rp.at[to_after, at],
            device_id={"epoch": peer}, device_id_type=mesh_id,
        )

    each = LANES // (maps * EDGE)
    part = (lane // EDGE) & (each - 1)
    low_half = lane < LANES // 2
    first_window = (lane & WINDOW) == 0

    def stacked(k):
        summed = jnp.zeros((maps * tile, 2 * LANES), jnp.float32)
        rims = [jnp.zeros((tile, LANES), jnp.float32) for _ in range(2)]
        lefts, rights, rim_rights = [], [], []
        for run in range(runs):
            high, low, rim_high, rim_low, right = (ends[k, EDGE * which + run] for which in range(5))
            rim = edge[pl.ds(rim_high, tile), :]
            if run > 0:
                rim = rim - edge[pl.ds(rim_low, tile), :]
            rims[run // each] = jnp.where(part == run % each, rim, rims[run // each])
            pieces = []
            for m in range(maps):
                piece = plane[pl.ds(high + m * rows_out, tile), :]
                if run > 0:
                    piece = piece - plane[pl.ds(low + m * rows_out, tile), :]
                pieces.append(piece.astype(jnp.bfloat16))
            lefts.append(jnp.concatenate(pieces, axis=0))
            rights.append(shift[right])
            rim_rights.append(edge_shift[right])
        turned = [pltpu.roll(rim, LANES // 2, axis=1) for rim in rims]
        spread = (jnp.where(low_half, rims[0], turned[1]), jnp.where(low_half, turned[0], rims[1]))
        lefts.append(jnp.concatenate([rim.astype(jnp.bfloat16) for rim in spread], axis=0))
        spare = jnp.zeros((LANES - EDGE * runs, 2 * LANES), jnp.bfloat16)
        rights.append(jnp.concatenate(rim_rights + [spare], axis=0))
        for run in range(0, len(lefts), 2):
            summed += jnp.dot(
                jnp.concatenate(lefts[run : run + 2], axis=1), jnp.concatenate(rights[run : run + 2], axis=0),
                preferred_element_type=jnp.float32,
            )
        outer = jnp.where(first_window, summed[:tile, LANES:], summed[tile:, LANES:])
        return summed[:tile, :LANES], summed[tile:, :LANES], outer

    def spot_of(turn):
        return (blocks - 1 - turn // block) * block + lax.rem(turn, block)

    def owner_of(turn):
        return lax.rem(group + spot_of(turn) // block, blocks) * 2

    def theirs(turn):
        return stacked((owner_of(turn) + partner) * block + lax.rem(turn, block))

    def ours(turn):
        return stacked((owner_of(turn) + member) * block + lax.rem(turn, block))

    def hand_over(turn, parts):
        spot = spot_of(turn)
        for m in range(maps + 1):
            send_v[spot, m] = parts[m].astype(jnp.bfloat16)
        vel_copy(spot).start()

    def finish(turn, parts):
        spot = spot_of(turn)
        j = lax.rem(turn, block)
        vel_copy(spot).wait_recv()
        totals = [parts[m] + recv_v[spot, m].astype(jnp.float32) for m in range(maps + 1)]
        upper, lower = totals[maps][: tile // 2], totals[maps][tile // 2 :]
        to_left = low_half[: tile // 2]
        send_z[0, spot] = jnp.where(to_left, upper, pltpu.roll(lower, LANES // 2, axis=1)).astype(jnp.bfloat16)
        send_z[1, spot] = jnp.where(to_left, pltpu.roll(upper, LANES // 2, axis=1), lower).astype(jnp.bfloat16)

        @pl.when(has_before)
        def _():
            side_copy(0, spot).start()

        @pl.when(has_after)
        def _():
            side_copy(1, spot).start()

        @pl.when(spot >= block)
        def _():
            for m in range(maps):
                send_x[j, m] = totals[m].astype(jnp.bfloat16)
            epoch_copy(j).start()

        @pl.when(spot < block)
        def _():
            for m in range(maps):
                keep[j, m] = totals[m]

    last = blocks * block - 1

    def stack(turn, carry):
        ahead = theirs(turn + 1)
        kept = ours(turn)
        hand_over(turn + 1, ahead)
        finish(turn, kept)
        return carry

    ends_copy.wait()
    ahead = theirs(0)
    pl.semaphore_wait(barrier, greeted)
    hand_over(0, ahead)
    lax.fori_loop(0, last, stack, 0)
    finish(last, ours(last))

    def hand_on(to_after, at):
        side_copy(to_after, block + at).wait_recv()
        pass_copy(to_after, at).start()

    wrapped = column == GRID_X // 2

    def hand_on_near(at, carry):
        @pl.when(has_before & (column != GRID_X // 2))
        def _():
            hand_on(1, at)

        @pl.when(wrapped)
        def _():
            hand_on(0, at)

        return carry

    def hand_on_far(at, carry):
        @pl.when(wrapped)
        def _():
            hand_on(1, at)

        @pl.when(has_after & (column != GRID_X // 2))
        def _():
            hand_on(0, at)

        return carry

    lax.fori_loop(0, block, hand_on_near, 0)
    lax.fori_loop(0, block, hand_on_far, 0)

    pltpu.make_async_remote_copy(
        src_ref=send_v, dst_ref=recv_v, send_sem=sv, recv_sem=rv.at[0],
        device_id={"vel": partner}, device_id_type=mesh_id,
    ).wait_send()
    pltpu.make_async_remote_copy(
        src_ref=send_x, dst_ref=recv_x, send_sem=sx, recv_sem=rx.at[0],
        device_id={"epoch": peer}, device_id_type=mesh_id,
    ).wait_send()

    def sent_side(to_after):
        pltpu.make_async_remote_copy(
            src_ref=send_z.at[to_after], dst_ref=recv_z.at[to_after],
            send_sem=sz.at[to_after], recv_sem=rz.at[to_after, 0],
            device_id={"sky": after if to_after else before}, device_id_type=mesh_id,
        ).wait_send()

    def sent_on(to_after):
        pltpu.make_async_remote_copy(
            src_ref=recv_z.at[to_after, pl.ds(block, block)], dst_ref=passed.at[to_after],
            send_sem=sp.at[to_after], recv_sem=rp.at[to_after, 0],
            device_id={"epoch": peer}, device_id_type=mesh_id,
        ).wait_send()

    @pl.when(has_before)
    def _():
        sent_side(0)

    @pl.when(has_after)
    def _():
        sent_side(1)

    def assemble(j, carry):
        epoch_copy(j).wait_recv()

        @pl.when(has_before)
        def _():
            pass_copy(1, j).wait_recv()
            side_copy(1, j).wait_recv()

        @pl.when(has_after)
        def _():
            pass_copy(0, j).wait_recv()
            side_copy(0, j).wait_recv()

        strips_in = jnp.concatenate([recv_z[1, j], recv_z[0, j], passed[1, j], passed[0, j]], axis=1)
        for m, out in enumerate((psi_out, phi_out)):
            added = jnp.dot(
                strips_in, jnp.concatenate([unplace[m]] * 2, axis=0), preferred_element_type=jnp.float32
            )
            for bottom in range(2):
                span = slice(bottom * tile // 2, (bottom + 1) * tile // 2)
                out[j, span] = (
                    keep[j, m, span] + recv_x[j, m, span].astype(jnp.float32)
                    + added[:, bottom * LANES : (bottom + 1) * LANES]
                )
        return carry

    lax.fori_loop(0, block, assemble, 0)

    @pl.when(has_before)
    def _():
        sent_on(1)

    @pl.when(has_after)
    def _():
        sent_on(0)


def near_stacks(images, variances, valid, psf_sigma, offsets, plan):
    tile, sky, blocks, block, epochs, runs, chunk = plan
    rows_out = tile + 2 * HEAD
    smem = pl.BlockSpec(memory_space=pltpu.SMEM)
    vmem = pl.BlockSpec(memory_space=pltpu.VMEM)
    anywhere = pl.BlockSpec(memory_space=pl.ANY)
    dma = pltpu.SemaphoreType.DMA
    half = blocks * block
    narrow, wide = jnp.bfloat16, jnp.float32
    scratch = [
        pltpu.VMEM((2 * (epochs + 1) * rows_out, LANES), wide),
        pltpu.VMEM(((epochs + 1) * rows_out, LANES), wide),
        pltpu.SMEM((VELS, LANES), jnp.int32),
        pltpu.VMEM((VELS, LANES), jnp.int32),
        dma(()),
        pltpu.VMEM((epochs, tile, tile), narrow),
        pltpu.VMEM((epochs, tile, tile), narrow),
        dma((2, epochs // chunk)),
        pltpu.VMEM((2 * REACH + 1, tile, 2 * LANES), narrow),
        pltpu.VMEM((2 * REACH + 1, EDGE, 2 * LANES), narrow),
        pltpu.VMEM((2, 2 * tile, 2 * LANES), narrow),
        pltpu.VMEM((rows_out, tile), wide),
        pltpu.VMEM((2 * PACK, LANES), wide),
        pltpu.VMEM((epochs, 2, rows_out, tile), narrow),
        pltpu.VMEM((epochs, 2, 2 * PACK, LANES), narrow),
        pltpu.VMEM((epochs, 2, tile, 2 * LANES), narrow),
        pltpu.VMEM((half, 3, tile, tile), narrow),
        pltpu.VMEM((half, 3, tile, tile), narrow),
        pltpu.VMEM((block, 2, tile, tile), narrow),
        pltpu.VMEM((block, 2, tile, tile), narrow),
        pltpu.VMEM((block, 2, tile, tile), wide),
        pltpu.VMEM((2, half, tile // 2, LANES), narrow),
        pltpu.VMEM((2, half, tile // 2, LANES), narrow),
        pltpu.VMEM((2, block, tile // 2, LANES), narrow),
        dma(()), dma((half,)), dma(()), dma((block,)),
        dma((2,)), dma((2, half)), dma((2,)), dma((2, block)),
    ]
    out = jax.ShapeDtypeStruct((block, tile, tile), jnp.float32)
    return pl.pallas_call(
        functools.partial(near_kernel, plan),
        out_shape=(out, out),
        in_specs=[vmem, smem, smem, anywhere, anywhere],
        out_specs=(vmem, vmem),
        scratch_shapes=scratch,
        compiler_params=pltpu.CompilerParams(
            collective_id=0, has_side_effects=True, vmem_limit_bytes=KEPT
        ),
    )(offsets, psf_sigma, valid.reshape(epochs), images, variances)


def far_stacks(images, variances, valid, psf_sigma, offsets, plan):
    tile, sky, blocks, block, epochs, runs = plan
    rows_out = -(-(tile + 2 * REACH) // 16) * 16
    smem = pl.BlockSpec(memory_space=pltpu.SMEM)
    vmem = pl.BlockSpec(memory_space=pltpu.VMEM)
    dma = pltpu.SemaphoreType.DMA
    half = blocks * block
    far = max(1, (blocks - 1) * block)
    scratch = [
        pltpu.VMEM((2 * (epochs + 1), rows_out, LANES), jnp.float32),
        pltpu.VMEM((2 * (epochs + 1), rows_out, LANES), jnp.float32),
        pltpu.SMEM((VELS, LANES), jnp.int32),
        pltpu.VMEM((VELS, LANES), jnp.int32),
        dma(()),
        pltpu.VMEM((rows_out, tile + LANES), jnp.float32),
        pltpu.VMEM((LANES, 2 * LANES), jnp.float32),
        pltpu.VMEM((1, LANES, 2 * LANES), jnp.float32),
        pltpu.VMEM((2, 2, 2 * LANES, 2 * LANES), jnp.bfloat16),
        pltpu.VMEM((half, 2, tile, tile), jnp.bfloat16),
        pltpu.VMEM((half, 2, tile, tile), jnp.bfloat16),
        pltpu.VMEM((far, 2, tile, tile), jnp.bfloat16),
        pltpu.VMEM((far, 2, tile, tile), jnp.bfloat16),
        pltpu.VMEM((2, block, 2, tile, tile), jnp.float32),
        dma((half,)), dma((half,)), dma((far,)), dma((far,)),
    ]
    usable = valid[:, 0].astype(jnp.float32)[:, None, None]
    inverse = usable / variances[:, 0].astype(jnp.float32)
    scaled = images[:, 0].astype(jnp.float32) * inverse
    own = jnp.stack([scaled.astype(jnp.bfloat16), inverse.astype(jnp.bfloat16)], axis=1)
    out = jax.ShapeDtypeStruct((block, tile, tile), jnp.float32)
    return pl.pallas_call(
        functools.partial(fused_kernel, plan),
        out_shape=(out, out),
        in_specs=[smem, vmem, smem, vmem, vmem],
        out_specs=(vmem, vmem),
        scratch_shapes=scratch,
        compiler_params=pltpu.CompilerParams(
            collective_id=0, has_side_effects=True, vmem_limit_bytes=56 * 2**20
        ),
    )(offsets, offsets, psf_sigma, *strips(own, sky, tile))


def on_device(images, variances, valid, psf_sigma, offsets):
    epochs = images.shape[0]
    tile = images.shape[-1]
    sky = lax.axis_size("sky")
    blocks = lax.axis_size("epoch")
    block = VELS // (blocks * lax.axis_size("vel"))
    last_epoch = epochs * blocks * lax.axis_size("vel") - 1
    runs = 1 + 2 * -(-REACH * (epochs - 1) // last_epoch)
    plan = (tile, sky, blocks, block, epochs, runs)
    few = EDGE * runs < LANES and epochs % CHUNK == 0
    if sky == GRID_X and blocks == 2 and lax.axis_size("vel") == 2 and few:
        plan += (CHUNK,)
        psi_sum, phi_sum = near_stacks(images, variances, valid, psf_sigma, offsets, plan)
    else:
        psi_sum, phi_sum = far_stacks(images, variances, valid, psf_sigma, offsets, plan)
    phi_sum = jnp.maximum(phi_sum, phi_floor)
    likelihood = psi_sum / jnp.sqrt(phi_sum)
    flux = psi_sum / phi_sum
    return (likelihood[:, None], flux[:, None])


def solution(mesh):
    placed = (
        P(("epoch", "vel"), ("field", "sky"), None, None),
        P(("epoch", "vel"), ("field", "sky"), None, None),
        P(("epoch", "vel"), ("field", "sky")),
        P(("field", "epoch", "vel")),
        P(None, None, "epoch"),
    )
    return jax.shard_map(
        on_device,
        mesh=mesh,
        in_specs=placed,
        out_specs=(
            P(("epoch", "vel"), ("field", "sky"), None, None),
            P(("epoch", "vel"), ("field", "sky"), None, None),
        ),
        check_vma=False,
    )
```
